32 devices in a mesh: row: 8 (over z, core), col: 4 (over y, x).
Axes of the slice: x: 2, y: 2, z: 4, core: 2. Of those that a mesh axis runs over, the one named last changes fastest.
Arguments:
- source: float32 [16, 256, 512], P(None, 'row', 'col'), may hold values from -6 to 6
- guess: float32 [16, 256, 512], P(None, 'row', 'col'), may hold values from -6 to 6
- conductivity: float32 [256, 512], P('row', 'col'), may hold values from 0.1 to 10
- storage: float32 [256, 512], P('row', 'col'), may hold values from 0.02 to 0.2
- aggregates: int32 [256, 512], P('row', 'col'), may hold values from 0 to 63, as said below
- pair_maps: int32 [4, 8, 4, 128], P(None, 'row', 'col'), may hold values from 0 to 63, as said below
Outputs:
- solution: float32 [16, 256, 512], P(None, 'row', 'col')
- residual: float32 [16, 256, 512], P(None, 'row', 'col')
The draws below stay inside these ranges and needn't reach their ends.
Inputs may be any that keep to these rules, and one draw needn't show every extreme that they name: `aggregates`: within each tile of 32 x 128 cells every id from 0 to 63 names exactly 64 cells of that tile. pair_maps[k, r, c] is the same for all tiles of one group of agglomeration level k + 1, that is all tiles whose row index shifted right by (k + 1) // 2 bits and column index shifted right by (k + 2) // 2 bits agree; each coarse unknown receives exactly two of the 128 entries.
All inputs are finite; a program needn't handle non-finite values.
Results may differ from the reference program's by a relative error of at most 0.0003.
Values sent between devices are 32-bit elements; how exact they have to be, the bound alone decides.
A program may use at most 64 MiB of HBM per device.

```python
import math
import jax
import jax.numpy as jnp
from jax import lax

CY = 32
CX = 128
NA = 64
M = 16
SWEEPS = 3
LEVELS = 4
NY = 256
NX = 512
N_ROW = 8
N_COL = 4


def draw_aggregates(key, part):
    rows_tiles = NY // CY
    cols_tiles = NX // CX
    key_shift, key_perm = jax.random.split(key)
    shifts = jax.random.randint(key_shift, (NY, cols_tiles), 0, 8)
    row_pos = jnp.arange(NY, dtype=jnp.int32)[:, None]
    col_pos = jnp.arange(NX, dtype=jnp.int32)[None, :]
    tile_col = col_pos // CX
    shift_cell = jnp.take(shifts, tile_col[0], axis=1)
    local_row = row_pos % CY
    local_col = col_pos % CX
    block_id = local_row // 8 * (CX // 8) + (local_col + shift_cell) % CX // 8
    perm_keys = jax.random.split(key_perm, rows_tiles * cols_tiles)
    labels = jax.vmap(lambda single: jax.random.permutation(single, NA))(perm_keys)
    tile_id = row_pos // CY * cols_tiles + tile_col
    return labels[tile_id, block_id].astype(jnp.int32)


def draw_pair_maps(key, part):
    rows_tiles = NY // CY
    cols_tiles = NX // CX
    keys = jax.random.split(key, LEVELS * rows_tiles * cols_tiles)
    perms = jax.vmap(lambda single: jax.random.permutation(single, 2 * NA))(keys)
    perms = perms.reshape(LEVELS, rows_tiles, cols_tiles, 2 * NA)
    result = []
    for level in range(LEVELS):
        row_bits = (level + 1) // 2
        col_bits = (level + 2) // 2
        rep_rows = jnp.arange(rows_tiles, dtype=jnp.int32) >> row_bits << row_bits
        rep_cols = jnp.arange(cols_tiles, dtype=jnp.int32) >> col_bits << col_bits
        chosen = perms[level][rep_rows[:, None], rep_cols[None, :]]
        result.append(chosen // 2)
    return jnp.stack(result).astype(jnp.int32)


def steps_of(rng, dims, cuts, smallest, high):
    factor_of, own = 1.0, jax.random.fold_in(rng, 6)
    for position, shards_of in cuts:
        draws = jnp.exp(jax.random.uniform(jax.random.fold_in(own, position), (shards_of,), jnp.float32, smallest / len(cuts), high / len(cuts)))
        factor_of = factor_of * jnp.repeat(draws, dims[position] // shards_of).reshape([-1 if axis == position else 1 for axis in range(len(dims))])
    return factor_of


def gaussian(rng, extent, spread, most, cuts=(), kind=jnp.bfloat16):
    array = jax.random.normal(rng, extent, jnp.float32) * spread
    if len(cuts) > 0:
        array = steps_of(rng, extent, cuts, -0.22, 0.18) * array
    return jnp.clip(array, min=-most, max=most).astype(kind)


def setup_inputs(seed: int = 0) -> dict:
    seeds = jax.random.split(jax.random.key(seed), 7)
    source = gaussian(seeds[0], (M, NY, NX), 1.0, 6.0, ((1, 8), (2, 4)), jnp.float32)
    guess = gaussian(seeds[1], (M, NY, NX), 1.0, 6.0, ((1, 8), (2, 4)), jnp.float32)
    conductivity = jnp.clip(jnp.exp(math.log(10.0) - 4.6051702 * jax.random.uniform(seeds[2], (NY, NX), jnp.float32) ** steps_of(seeds[2], (NY, NX), ((0, 8), (1, 4)), -0.2, 0.2)), 0.1, 10.0)
    storage = jnp.clip(jnp.exp(math.log(0.2) - 2.3025851 * jax.random.uniform(seeds[3], (NY, NX), jnp.float32) ** steps_of(seeds[3], (NY, NX), ((0, 8), (1, 4)), -0.2, 0.2)), 0.02, 0.2)
    aggregates = draw_aggregates(jax.random.fold_in(seeds[6], 71), 0)
    pair_maps = draw_pair_maps(jax.random.fold_in(seeds[6], 71), 0)
    return {"source": source, "guess": guess, "conductivity": conductivity, "storage": storage, "aggregates": aggregates, "pair_maps": pair_maps}


OMEGA_FINE = 0.8
OMEGA_COARSE = 0.6
HIGHEST = lax.Precision.HIGHEST

def face_values(cond):
    across = 2.0 * (cond[:, :-1] * cond[:, 1:]) / (cond[:, :-1] + cond[:, 1:])
    downward = 2.0 * (cond[:-1, :] * cond[1:, :]) / (cond[:-1, :] + cond[1:, :])
    east_face = jnp.pad(across, ((0, 0), (0, 1)))
    west_face = jnp.pad(across, ((0, 0), (1, 0)))
    south_face = jnp.pad(downward, ((0, 1), (0, 0)))
    north_face = jnp.pad(downward, ((1, 0), (0, 0)))
    return (east_face, west_face, south_face, north_face)

def mat_apply(vector, matrix):
    return jnp.matmul(vector, jnp.swapaxes(matrix, -1, -2), precision=HIGHEST)

def presmooth(rhs, apply_fn, diag_row):
    approx = OMEGA_COARSE * rhs / diag_row
    for sweep_index in range(SWEEPS - 1):
        approx = approx + OMEGA_COARSE * (rhs - apply_fn(approx)) / diag_row
    return approx

def postsmooth(rhs, approx, apply_fn, diag_row):
    for sweep_index in range(SWEEPS):
        approx = approx + OMEGA_COARSE * (rhs - apply_fn(approx)) / diag_row
    return approx

def solve_block(matrix, rhs):
    factor = jnp.linalg.cholesky(matrix)
    return jax.scipy.linalg.cho_solve((factor, True), rhs.T).T

def reference(source, guess, conductivity, storage, aggregates, pair_maps):
    east_face, west_face, south_face, north_face = face_values(conductivity)
    diagonal = storage + east_face + west_face + south_face + north_face

    def apply_fine(field):
        padded = jnp.pad(field, ((0, 0), (1, 1), (1, 1)))
        beside = east_face * padded[:, 1:-1, 2:] + west_face * padded[:, 1:-1, :-2] + south_face * padded[:, 2:, 1:-1] + north_face * padded[:, :-2, 1:-1]
        return diagonal * field - beside
    row_pos = jnp.arange(NY, dtype=jnp.int32)[:, None]
    col_pos = jnp.arange(NX, dtype=jnp.int32)[None, :]
    tile_id = row_pos // CY * N_COL + col_pos // CX
    base = tile_id * NA
    cell_key = (base + aggregates).reshape(-1)
    segments = N_ROW * N_COL * NA

    def restrict_all(field):
        summed = jax.ops.segment_sum(field.reshape(M, -1).T, cell_key, num_segments=segments)
        return summed.reshape(N_ROW, N_COL, NA, M).transpose(0, 1, 3, 2)

    def prolong_all(coarse):
        flat = coarse.transpose(2, 0, 1, 3).reshape(M, -1)
        return flat[:, cell_key].reshape(M, NY, NX)

    def level_one(coarse):
        return restrict_all(apply_fine(prolong_all(coarse)))
    right_agg = jnp.concatenate([aggregates[:, 1:], aggregates[:, :1]], axis=1)
    below_agg = jnp.concatenate([aggregates[1:, :], aggregates[:1, :]], axis=0)
    inner_east = jnp.where(col_pos % CX < CX - 1, east_face, 0.0)
    inner_south = jnp.where(row_pos % CY < CY - 1, south_face, 0.0)
    keys = jnp.concatenate([((base + aggregates) * NA + right_agg).reshape(-1), ((base + right_agg) * NA + aggregates).reshape(-1), ((base + aggregates) * NA + below_agg).reshape(-1), ((base + below_agg) * NA + aggregates).reshape(-1), ((base + aggregates) * NA + aggregates).reshape(-1)])
    values = jnp.concatenate([(-inner_east).reshape(-1), (-inner_east).reshape(-1), (-inner_south).reshape(-1), (-inner_south).reshape(-1), diagonal.reshape(-1)])
    self_block = jax.ops.segment_sum(values, keys, num_segments=N_ROW * N_COL * NA * NA).reshape(N_ROW, N_COL, NA, NA)
    solution = guess
    for sweep_index in range(SWEEPS):
        solution = solution + OMEGA_FINE * (source - apply_fine(solution)) / diagonal
    leftover = source - apply_fine(solution)
    rhs_list = [restrict_all(leftover)]
    mat_list = [self_block]
    diag_one = jnp.diagonal(self_block, axis1=-2, axis2=-1)[..., None, :]
    sol_list = [presmooth(rhs_list[0], level_one, diag_one)]
    remainder = rhs_list[0] - level_one(sol_list[0])
    own_maps = []
    labels = jnp.arange(NA, dtype=jnp.int32)
    for level in range(LEVELS):
        axis_num = 1 if level % 2 == 0 else 0
        bit = level // 2
        count = N_COL if axis_num == 1 else N_ROW
        positions = jnp.arange(count, dtype=jnp.int32)
        upper_bit = positions >> bit & 1
        lower_pos = positions - upper_bit * (1 << bit)
        upper_pos = lower_pos + (1 << bit)
        mat_lo = jnp.take(mat_list[-1], lower_pos, axis=axis_num)
        mat_hi = jnp.take(mat_list[-1], upper_pos, axis=axis_num)
        rhs_lo = jnp.take(remainder, lower_pos, axis=axis_num)
        rhs_hi = jnp.take(remainder, upper_pos, axis=axis_num)
        if axis_num == 1:
            flags = upper_bit[None, :, None, None]
        else:
            flags = upper_bit[:, None, None, None]
        chooser = (pair_maps[level][..., None] == labels).astype(jnp.float32)
        q_lo = chooser[..., :NA, :]
        q_hi = chooser[..., NA:, :]
        coarse_mat = jnp.matmul(jnp.swapaxes(q_lo, -1, -2), jnp.matmul(mat_lo, q_lo, precision=HIGHEST), precision=HIGHEST) + jnp.matmul(jnp.swapaxes(q_hi, -1, -2), jnp.matmul(mat_hi, q_hi, precision=HIGHEST), precision=HIGHEST)
        coarse_rhs = jnp.matmul(rhs_lo, q_lo, precision=HIGHEST) + jnp.matmul(rhs_hi, q_hi, precision=HIGHEST)
        own_maps.append(jnp.where(flags == 1, q_hi, q_lo))
        mat_list.append(coarse_mat)
        rhs_list.append(coarse_rhs)
        if level < LEVELS - 1:
            diag_row = jnp.diagonal(coarse_mat, axis1=-2, axis2=-1)[..., None, :]
            approx = presmooth(coarse_rhs, lambda vec, mat=coarse_mat: mat_apply(vec, mat), diag_row)
            remainder = coarse_rhs - mat_apply(approx, coarse_mat)
        else:
            flat = jax.vmap(solve_block)(coarse_mat.reshape(-1, NA, NA), coarse_rhs.reshape(-1, M, NA))
            approx = flat.reshape(N_ROW, N_COL, M, NA)
        sol_list.append(approx)
    for level in reversed(range(LEVELS)):
        updated = sol_list[level] + mat_apply(sol_list[level + 1], own_maps[level])
        if level > 0:
            matrix = mat_list[level]
            diag_row = jnp.diagonal(matrix, axis1=-2, axis2=-1)[..., None, :]
            updated = postsmooth(rhs_list[level], updated, lambda vec, mat=matrix: mat_apply(vec, mat), diag_row)
        else:
            updated = postsmooth(rhs_list[0], updated, level_one, diag_one)
        sol_list[level] = updated
    solution = solution + prolong_all(sol_list[0])
    for sweep_index in range(SWEEPS):
        solution = solution + OMEGA_FINE * (source - apply_fine(solution)) / diagonal
    residual = source - apply_fine(solution)
    return (solution, residual)
```

```python
import functools

import jax
import jax.numpy as jnp
from jax import lax
from jax.experimental import pallas as pl
from jax.experimental.pallas import tpu as pltpu
from jax.sharding import PartitionSpec as P

NA = 64
SWEEPS = 3
LEVELS = 4
OMEGA_FINE = 0.8
OMEGA_COARSE = 0.6
F32 = jnp.float32
BF16 = jnp.bfloat16
MESH = pl.DeviceIdType.MESH
OPP = (1, 0, 3, 2, 7, 6, 5, 4)
WIDE = SWEEPS + 1
GROUP = 2 * WIDE
NX0 = 2 * SWEEPS
VMEM_LIMIT = 24 * 1024 * 1024
NN = (((1,), (0,)), ((), ()))
NT = (((1,), (1,)), ((), ()))


def dg(a, b, dims):
    return lax.dot_general(a, b, dims, preferred_element_type=F32)


def split2(x):
    hi = x.astype(BF16)
    return hi, (x - hi.astype(F32)).astype(BF16)


def split3(x):
    hi = x.astype(BF16)
    rest = x - hi.astype(F32)
    mid = rest.astype(BF16)
    return hi, mid, (rest - mid.astype(F32)).astype(BF16)


def dot_parts(x, w_hi, w_lo, dims=NN):
    hi, lo = split2(x)
    return dg(hi, w_hi, dims) + (dg(lo, w_hi, dims) + dg(hi, w_lo, dims))


def dot_hot(x, hot, dims):
    hi, mid, lo = split3(x)
    return dg(hi, hot, dims) + (dg(mid, hot, dims) + dg(lo, hot, dims))


def hot_dot(hot, x, dims):
    hi, mid, lo = split3(x)
    return dg(hot, hi, dims) + (dg(hot, mid, dims) + dg(hot, lo, dims))


def kernel(n_row, n_col, src_in, guess_in, cond_in, sto_in, agg_in, pm_in, sol, res,
           u, se, left, mo, gmat, rlhs, xt, crecv, srecv, ccorn, scorn, arecv, rowbuf, colbuf, corner,
           rsend, csend, xsend, xrecv, msend, mrecv, vsend, vrecv, wmat, fmat, gfin, qts,
           cond, sto, agg, pm, ssem, rsem, lsem):
    members, rows, cols = guess_in.shape
    half_m = members // 2
    ext = rows + GROUP
    row = lax.axis_index("row")
    col = lax.axis_index("col")
    has = [row > 0, row < n_row - 1, col > 0, col < n_col - 1]
    dev = [(row - 1, col), (row + 1, col), (row, col - 1), (row, col + 1)]
    for v in (0, 1):
        for h in (2, 3):
            has.append(jnp.logical_and(has[v], has[h]))
            dev.append((dev[v][0], dev[h][1]))
    col_bit = col % 2
    row_bit = row % 2
    col_bit2 = col // 2 % 2
    row_bit2 = row // 2 % 2
    upper = (col_bit, row_bit, col_bit2, row_bit2)
    flip_col = (0, 1 - 2 * col_bit, 2 - 4 * col_bit2, 3 - 2 * col_bit - 4 * col_bit2)
    flip_row = (0, 1 - 2 * row_bit, 2 - 4 * row_bit2, 3 - 2 * row_bit - 4 * row_bit2)

    def mate(j):
        return (row + flip_row[j // 2 % 2 + 2 * (j // 8)], col + flip_col[j % 2 + 2 * (j // 4 % 2)])

    loads = [
        pltpu.make_async_copy(source, target, lsem.at[i])
        for i, (source, target) in enumerate((
            (guess_in, u.at[:, pl.ds(0, rows)]), (src_in, se.at[:, pl.ds(0, rows)]),
            (cond_in, cond), (agg_in, agg), (sto_in, sto), (pm_in, pm)))
    ]
    for load in loads:
        load.start()

    barrier = pltpu.get_barrier_semaphore()
    count = jnp.int32(3)
    for d in range(8):
        count = count + has[d].astype(jnp.int32)

        @pl.when(has[d])
        def _():
            pl.semaphore_signal(barrier, inc=1, device_id=dev[d], device_id_type=MESH)

    for j in (4, 8, 12):
        pl.semaphore_signal(barrier, inc=1, device_id=mate(j), device_id_type=MESH)

    def copy(source, target, slot, device):
        return pltpu.make_async_remote_copy(
            src_ref=source, dst_ref=target, send_sem=ssem.at[slot], recv_sem=rsem.at[slot],
            device_id=device, device_id_type=MESH)

    sent = []

    def start(d, source, target, slot):
        @pl.when(has[d])
        def _():
            copy(source, target, slot, dev[d]).start()

        sent.append((d, source, target, slot))

    def arrive(d, source, target, slot):
        @pl.when(has[OPP[d]])
        def _():
            copy(source, target, slot, dev[d]).wait_recv()

    for d in range(8):
        @pl.when(jnp.logical_not(has[OPP[d]]))
        def _():
            for got, got_corner in ((crecv, ccorn), (srecv, scorn)):
                if d < 4:
                    got[d] = jnp.ones((rows, cols), F32)
                else:
                    got_corner[d - 4] = jnp.ones((GROUP, cols), F32)
            if d < 4:
                arecv[d] = jnp.zeros((rows, cols), jnp.int32)
                for e in range(NX0):
                    xrecv[e, d] = jnp.zeros((half_m, cols), F32)
            for p in range(3):
                if d < 2:
                    rowbuf[p, d] = jnp.zeros((WIDE * members, cols), F32)
                elif d < 4:
                    colbuf[p, d - 2] = jnp.zeros((rows, cols), F32)
                else:
                    corner[p, d - 4] = jnp.zeros((GROUP, cols), F32)

    lane = lax.broadcasted_iota(jnp.int32, (ext, cols), 1)
    sub = lax.broadcasted_iota(jnp.int32, (ext, cols), 0)
    l8 = lane % GROUP
    owner = lane // GROUP
    lane8 = lane[0:GROUP]
    sub8 = sub[0:GROUP]

    def mirror(x):
        where = lax.broadcasted_iota(jnp.int32, x.shape, 1)
        bit = 1
        while bit < GROUP:
            x = jnp.where(where // bit % 2 == 0, pltpu.roll(x, cols - bit, 1), pltpu.roll(x, bit, 1))
            bit *= 2
        return x

    def repeat(x):
        width = GROUP
        while width < cols:
            x = x + pltpu.roll(x, width, 1)
            width *= 2
        return x

    def halo_ref(p, d):
        source = rsend.at[p, d] if d < 2 else csend.at[p] if d < 4 else csend.at[
            p, pl.ds(0 if d < 6 else rows - GROUP, GROUP)]
        target = rowbuf.at[p, d] if d < 2 else colbuf.at[p, d - 2] if d < 4 else corner.at[p, d - 4]
        return d, source, target, 20 + 8 * p + d

    def part_ref(value, plane, corners, d, slot):
        if d in (2, 3):
            return d, value, plane.at[d], slot
        source = value.at[pl.ds(0 if d in (0, 4, 5) else rows - GROUP, GROUP)]
        target = plane.at[d, pl.ds(0, GROUP)] if d < 2 else corners.at[d - 4]
        return d, source, target, slot

    def pack(p, field_of):
        packed = jnp.zeros((rows, cols), F32)
        for m in range(members):
            v = field_of(m)
            packed = jnp.where(owner[0:rows] == m, pltpu.roll(v, (GROUP * m + WIDE) % cols, 1), packed)
            rsend[p, 0, WIDE * m : WIDE * (m + 1), :] = v[0:WIDE]
            rsend[p, 1, WIDE * m : WIDE * (m + 1), :] = v[rows - WIDE : rows]
        csend[p] = mirror(packed)

    order = (2, 3, 4, 5, 6, 7, 0, 1)

    def halo_start(p):
        for d in order:
            start(*halo_ref(p, d))

    def halo_arrive(p):
        for d in range(8):
            arrive(*halo_ref(p, d))

    def under(south, north):
        return jnp.where(sub8 < WIDE, south, north)

    def halo_fill(p, field):
        for m in range(members):
            field[m, rows : rows + WIDE, :] = rowbuf[p, 0, WIDE * m : WIDE * (m + 1), :]
            field[m, rows + WIDE : ext, :] = rowbuf[p, 1, WIDE * m : WIDE * (m + 1), :]
        side_e = jnp.concatenate([colbuf[p, 0], under(corner[p, 0], corner[p, 2])], axis=0)
        side_w = jnp.concatenate([colbuf[p, 1], under(corner[p, 1], corner[p, 3])], axis=0)
        return jnp.where(l8 < WIDE, side_e, side_w)

    def cond_parts(d):
        return part_ref(cond, crecv, ccorn, d, d)

    def sto_parts(d):
        return part_ref(sto, srecv, scorn, d, 8 + d)

    for load in loads:
        load.wait()
    pack(0, lambda m: u[m, 0:rows])
    pack(1, lambda m: se[m, 0:rows])
    pl.semaphore_wait(barrier, count)
    for d in order:
        start(*cond_parts(d))
    for d in range(4):
        start(d, agg, arecv.at[d], 16 + d)
    for d in order:
        start(*sto_parts(d))
    halo_start(0)
    halo_start(1)

    agg_v = agg[...]
    sub64 = lax.broadcasted_iota(jnp.int32, (NA, cols), 0)
    for r in range(rows):
        hot = jnp.where(sub64 == agg_v[r : r + 1], 1.0, 0.0).astype(BF16)
        mo[0:NA, r * cols : (r + 1) * cols] = hot
        mo[NA : 2 * NA, r * cols : (r + 1) * cols] = hot
    xt[...] = jnp.zeros(xt.shape, F32)
    iota128 = lax.broadcasted_iota(jnp.int32, (cols, cols), 0)
    lane128 = lax.broadcasted_iota(jnp.int32, (cols, cols), 1)
    for k in range(LEVELS):
        pmk = pm[k : k + 1, :]
        pmk = jnp.where(upper[k] == 1, pltpu.roll(pmk, NA, 1), pmk)
        qts[k] = jnp.where(jnp.logical_and(iota128 == pmk, lane128 < NA), 1.0, 0.0).astype(BF16)

    def face(a, b):
        return 2.0 * (a * b) / (a + b)

    last = rows - 1
    c = cond[...]
    in_east = jnp.where(lane[0:rows] < cols - 1, face(c, pltpu.roll(c, cols - 1, 1)), 0.0)
    in_south = jnp.where(sub[0:rows] < last, face(c, pltpu.roll(c, last, 0)), 0.0)
    right = pltpu.roll(agg_v, cols - 1, 1)
    below = pltpu.roll(agg_v, last, 0)
    half = 0.5 * (sto[...] + in_east + pltpu.roll(in_east, 1, 1) + in_south + pltpu.roll(in_south, 1, 0))
    for r in range(rows):
        s = slice(r, r + 1)
        g = (jnp.where(sub64 == right[s], in_east[s], 0.0)
             + jnp.where(sub64 == below[s], in_south[s], 0.0)
             - jnp.where(sub64 == agg_v[s], half[s], 0.0))
        for i, part in enumerate(split3(g)):
            gmat[i * NA : (i + 1) * NA, r * cols : (r + 1) * cols] = part
    gx = dg(gmat[...], mo[0:NA], NT)
    xt[0:NA, 0:NA] = gx[0:NA] + (gx[NA : 2 * NA] + gx[2 * NA : 3 * NA])
    xfull = xt[...]
    inner = -(xfull + xfull.T)[0:NA]

    lane_c = lax.broadcasted_iota(jnp.int32, (NA, cols), 1)
    lane_1 = lax.broadcasted_iota(jnp.int32, (1, cols), 1)
    eye = jnp.where(lane_c == sub64, 1.0, 0.0)

    def squeeze(k, mat):
        qt = qts[k]
        return hot_dot(qt[0:NA, 0:NA], dot_hot(mat[:, 0:NA], qt[:, 0:NA], NT), NN)

    inner_1 = squeeze(0, inner)
    inner_2 = squeeze(1, inner_1)

    for d in range(8):
        arrive(*cond_parts(d))
        arrive(*sto_parts(d))

    def extend(value, plane, corners):
        main = jnp.concatenate([value[...], under(plane[0, 0:GROUP], plane[1, 0:GROUP])], axis=0)
        side_e = jnp.concatenate([plane[2], under(corners[0], corners[2])], axis=0)
        side_w = jnp.concatenate([plane[3], under(corners[1], corners[3])], axis=0)
        base = jnp.where(lane < WIDE, pltpu.roll(side_w, WIDE, 1), pltpu.roll(side_e, WIDE, 1))
        side = mirror(repeat(jnp.where(lane < GROUP, base, 0.0)))
        return main, side

    cm, cs = extend(cond, crecv, ccorn)
    sm, ss = extend(sto, srecv, scorn)
    hasi = [h.astype(jnp.int32) for h in has[0:4]]

    def vertical(x):
        down = jnp.where(jnp.logical_and(sub == last, hasi[1] == 0), 0.0, face(x, pltpu.roll(x, ext - 1, 0)))
        up = jnp.where(jnp.logical_and(sub == 0, hasi[0] == 0), 0.0, face(x, pltpu.roll(x, 1, 0)))
        return down, up

    side_at = pltpu.roll(cs, cols - WIDE, 1)
    rim = jnp.logical_and(lane >= WIDE - 1, lane <= WIDE)
    main_at = repeat(jnp.where(rim, pltpu.roll(cm, WIDE, 1), 0.0))
    east = face(cm, jnp.where(lane == cols - 1, side_at, pltpu.roll(cm, cols - 1, 1)))
    west = face(cm, jnp.where(lane == 0, side_at, pltpu.roll(cm, 1, 1)))
    east = jnp.where(lane < cols - 1 + hasi[3], east, 0.0)
    west = jnp.where(lane >= 1 - hasi[2], west, 0.0)
    south, north = vertical(cm)
    diag = sm + east + west + south + north
    step = OMEGA_FINE / diag
    s_west = face(cs, jnp.where(l8 == WIDE - 1, main_at, pltpu.roll(cs, cols - 1, 1)))
    s_east = face(cs, jnp.where(l8 == WIDE, main_at, pltpu.roll(cs, 1, 1)))
    s_west = jnp.where(jnp.logical_and(l8 == WIDE - 1, hasi[3] == 0), 0.0, s_west)
    s_east = jnp.where(jnp.logical_and(l8 == WIDE, hasi[2] == 0), 0.0, s_east)
    s_south, s_north = vertical(cs)
    s_diag = ss + s_east + s_west + s_south + s_north
    s_step = OMEGA_FINE / s_diag

    def apply_field(side, n, finish):
        lane_n = lane[0:n]
        edge = jnp.zeros((ext, cols), F32)
        for m in range(members):
            v = u[m]
            hm = pltpu.roll(side, (2 * cols - GROUP * m - WIDE) % cols, 1)[0:n]
            vn = v[0:n]
            from_w = jnp.where(lane_n == 0, hm, pltpu.roll(vn, 1, 1))
            from_e = jnp.where(lane_n == cols - 1, hm, pltpu.roll(vn, cols - 1, 1))
            from_s = pltpu.roll(v, ext - 1, 0)[0:n]
            from_n = pltpu.roll(v, 1, 0)[0:n]
            rest = se[m, 0:n] - (diag[0:n] * vn - (
                east[0:n] * from_e + west[0:n] * from_w + south[0:n] * from_s + north[0:n] * from_n))
            if n == ext:
                edge = jnp.where(owner == m, pltpu.roll(v, (GROUP * m + WIDE) % cols, 1), edge)
            finish(m, vn, rest)
        return edge

    def sweep(side, s_src):
        def finish(m, v, rest):
            u[m] = v + step * rest

        edge = apply_field(side, ext, finish)
        from_w = jnp.where(l8 == WIDE - 1, edge, pltpu.roll(side, cols - 1, 1))
        from_e = jnp.where(l8 == WIDE, edge, pltpu.roll(side, 1, 1))
        rest = s_src - (s_diag * side - (s_east * from_e + s_west * from_w
                        + s_south * pltpu.roll(side, ext - 1, 0) + s_north * pltpu.roll(side, 1, 0)))
        return side + s_step * rest


    for d in range(4):
        arrive(d, agg, arecv.at[d], 16 + d)
    agg_t = agg_v.astype(F32).T.astype(jnp.int32)

    def put(ref, slot, block):
        both = jnp.concatenate([block, pltpu.roll(block, NA, 1)], axis=0)
        hi, lo = split2(both)
        ref[0, slot * cols : (slot + 1) * cols] = hi
        ref[1, slot * cols : (slot + 1) * cols] = lo

    def couple(slot, own_ids, other_ids, faces, width):
        own = jnp.where(lax.broadcasted_iota(jnp.int32, (cols, width), 0) == own_ids, 1.0, 0.0).astype(BF16)
        other = jnp.where(lax.broadcasted_iota(jnp.int32, (NA, width), 0) == other_ids, faces, 0.0)
        links = dot_hot(other, own, NT)
        put(wmat, slot, -links)
        return jnp.sum(links, axis=0, keepdims=True)

    outer = couple(1, agg_v[last:rows], arecv[0][0:1], south[last:rows], cols)
    outer = outer + couple(2, agg_v[0:1], arecv[1][last : rows], north[0:1], cols)
    agg_e = arecv[2].astype(F32).T.astype(jnp.int32)
    agg_w = arecv[3].astype(F32).T.astype(jnp.int32)
    outer = outer + couple(3, agg_t[cols - 1 : cols], agg_e[0:1], east[0:rows].T[cols - 1 : cols], rows)
    outer = outer + couple(4, agg_t[0:1], agg_w[cols - 1 : cols], west[0:rows].T[0:1], rows)

    def mat_copy(i):
        j = (1, 2, 3, 4, 8, 12)[i]
        return copy(msend.at[(0, 1, 1, 2, 3, 3)[i]], mrecv.at[i], 44 + 4 * NX0 + i, mate(j))

    def vec_copy(j):
        low = j.bit_length() - 1
        part = pl.ds(low, LEVELS - low)
        return copy(vsend.at[part], vrecv.at[j - 1, part], 50 + 4 * NX0 + j - 1, mate(j))

    def weight(mat):
        d = jnp.sum(jnp.where(lane_c == sub64, mat, 0.0), axis=0, keepdims=True)
        ok = lane_1 < NA
        return jnp.where(ok, OMEGA_COARSE / jnp.where(ok, d, 1.0), 0.0)

    def smoother(mat):
        side_w = OMEGA_COARSE / jnp.sum(eye * mat, axis=1, keepdims=True)
        one = eye - mat * weight(mat)
        hi, lo = split2(one)
        two = dot_parts(one[:, 0:NA], hi, lo)
        return dot_parts(two[:, 0:NA], hi, lo), side_w * (eye + one + two)

    def apply_parts(a, b):
        return dot_parts(a[:, 0:NA], *split2(b))

    block = inner + jnp.where(lane_c == sub64, outer, 0.0)
    outer_1 = dot_hot(jnp.broadcast_to(outer[:, 0:NA], (8, NA)), qts[0][:, 0:NA], NT)
    outer_2 = dot_hot(outer_1[:, 0:NA], qts[1][:, 0:NA], NT)
    msend[0] = inner_1 + eye * outer_1[0:1]
    msend[1] = inner_2 + eye * outer_2[0:1]
    for i in range(3):
        mat_copy(i).start()
    put(wmat, 0, block)
    weights = weight(block)
    weights = weights + pltpu.roll(weights, NA, 1)

    halo_arrive(0)
    side = halo_fill(0, u)
    halo_arrive(1)
    s_src = halo_fill(1, se)
    for _ in range(SWEEPS):
        side = sweep(side, s_src)

    def keep_left(m, v, rest):
        left[m] = rest

    apply_field(side, rows, keep_left)
    for r in range(rows):
        for i, part in enumerate(split2(left[:, r, :])):
            rlhs[i * members : (i + 1) * members, r * cols : (r + 1) * cols] = part
    gr = dg(rlhs[...], mo[...], NT)
    gr = gr[0:members] + gr[members : 2 * members]
    lane_h = lax.broadcasted_iota(jnp.int32, (half_m, cols), 1)

    def fold(x):
        return jnp.where(lane_h < NA, x[0:half_m], x[half_m:members])

    y0 = fold(gr)

    def x_slot(e, d):
        return (d, xsend.at[e], xrecv.at[e, d], 44 + 4 * e + d)

    def level_one(e, x, between=None):
        xsend[e] = x
        for d in (2, 3, 1, 0):
            start(*x_slot(e, d))
        if between is not None:
            between()
        for d in range(4):
            arrive(*x_slot(e, d))
        every = jnp.concatenate([x] + [xrecv[e, d] for d in range(4)], axis=1)
        return dot_parts(every, wmat[0], wmat[1])

    keep = {}

    def first_mats():
        for i in range(3):
            mat_copy(i).wait_recv()
        mat_1 = msend[0] + mrecv[0]
        mat_2 = squeeze(1, mat_1) + (mrecv[1] + mrecv[2])
        mat_3 = squeeze(2, mat_2)
        msend[2] = mat_3
        msend[3] = squeeze(3, mat_3)
        for i in range(3, 6):
            mat_copy(i).start()
        keep["mats"] = [mat_1, mat_2]

    def chains():
        smooth = [smoother(mat) for mat in keep["mats"]]
        for i in range(3, 6):
            mat_copy(i).wait_recv()
        mat_3 = msend[2] + mrecv[3]
        mat_4 = squeeze(3, mat_3) + (mrecv[4] + mrecv[5])
        smooth.append(smoother(mat_3))
        chain = qts[0][0:NA].astype(F32)
        for k in range(LEVELS):
            put(fmat, k, chain)
            if k + 1 < LEVELS:
                cube, pre = smooth[k]
                moved = apply_parts(cube, chain)
                put(gfin, k, apply_parts(pre, chain + moved))
                chain = hot_dot(qts[k + 1][0:NA, 0:NA], moved, NN)
        keep["solve"] = jnp.where(lane_c < NA, mat_4, pltpu.roll(chain, NA, 1))

    def eliminate(first, end):
        mat = keep["solve"]
        for k in range(first, end, 2):
            r0, r1 = mat[k : k + 1], mat[k + 1 : k + 2]
            a, b = r0[:, k : k + 1], r0[:, k + 1 : k + 2]
            c, d = r1[:, k : k + 1], r1[:, k + 1 : k + 2]
            scale = 1.0 / (a * d - b * c)
            p0 = (d * r0 - b * r1) * scale
            p1 = (a * r1 - c * r0) * scale
            out = mat - mat[:, k : k + 1] * p0 - mat[:, k + 1 : k + 2] * p1
            mat = jnp.where(sub64 == k, p0, jnp.where(sub64 == k + 1, p1, out))
        keep["solve"] = mat

    x = y0 * weights
    x = x + (y0 - level_one(0, x, first_mats)) * weights
    x = x + (y0 - level_one(1, x, chains)) * weights
    rem = y0 - level_one(2, x, lambda: eliminate(0, NA // 2))
    up = dot_parts(rem, fmat[0], fmat[1], NT)
    for k in range(LEVELS):
        vsend[k] = up[:, k * cols : (k + 1) * cols]
    for j in reversed(range(1, 2 ** LEVELS)):
        vec_copy(j).start()
    eliminate(NA // 2, NA)
    put(gfin, LEVELS - 1, jnp.where(lane_c < NA, pltpu.roll(keep["solve"], NA, 1), 0.0))
    for j in range(1, 2 ** LEVELS):
        vec_copy(j).wait_recv()
    ys = []
    for k in range(LEVELS):
        y = vsend[k]
        for j in range(1, 2 ** (k + 1)):
            y = y + vrecv[j - 1, k]
        ys.append(y)
    x = x + dot_parts(jnp.concatenate(ys, axis=1), gfin[0], gfin[1])
    for i in range(SWEEPS):
        x = x + (y0 - level_one(SWEEPS + i, x)) * weights

    whole = jnp.concatenate([x, pltpu.roll(x, NA, 1)], axis=0)
    whole_hi = whole.astype(BF16).astype(F32)
    lane_m = lax.broadcasted_iota(jnp.int32, (members, cols), 1)
    spread = jnp.where(lane_m < NA, whole_hi, pltpu.roll(whole - whole_hi, NA, 1)).astype(BF16)
    for r in range(rows):
        part = dg(spread, mo[:, r * cols : (r + 1) * cols], NN)
        u[:, r, :] = u[:, r, :] + part
    pack(2, lambda m: u[m, 0:rows])
    halo_start(2)
    halo_arrive(2)
    side = halo_fill(2, u)
    for _ in range(SWEEPS):
        side = sweep(side, s_src)

    def out(m, v, rest):
        sol[m] = v
        res[m] = rest

    apply_field(side, rows, out)
    for d, source, target, slot in sent:
        @pl.when(has[d])
        def _():
            copy(source, target, slot, dev[d]).wait_send()

    for i in range(6):
        mat_copy(i).wait_send()
    for j in range(1, 2 ** LEVELS):
        vec_copy(j).wait_send()


def shards(n_row, n_col, source, guess, conductivity, storage, aggregates, pair_maps):
    members, rows, cols = source.shape
    cells = rows * cols
    ext = rows + GROUP
    vm = pl.BlockSpec(memory_space=pltpu.VMEM)
    half_m = members // 2
    mates = 2 ** LEVELS - 1
    slots = 50 + 4 * NX0 + mates
    hbm = pl.BlockSpec(memory_space=pltpu.HBM)
    return pl.pallas_call(
        functools.partial(kernel, n_row, n_col),
        out_shape=(jax.ShapeDtypeStruct(source.shape, F32),) * 2,
        in_specs=[hbm] * 6,
        out_specs=(vm, vm),
        scratch_shapes=[
            pltpu.VMEM((members, ext, cols), F32),
            pltpu.VMEM((members, ext, cols), F32),
            pltpu.VMEM((members, rows, cols), F32),
            pltpu.VMEM((2 * NA, cells), BF16),
            pltpu.VMEM((3 * NA, cells), BF16),
            pltpu.VMEM((2 * members, cells), BF16),
            pltpu.VMEM((cols, cols), F32),
            pltpu.VMEM((4, rows, cols), F32),
            pltpu.VMEM((4, rows, cols), F32),
            pltpu.VMEM((4, GROUP, cols), F32),
            pltpu.VMEM((4, GROUP, cols), F32),
            pltpu.VMEM((4, rows, cols), jnp.int32),
            pltpu.VMEM((3, 2, WIDE * members, cols), F32),
            pltpu.VMEM((3, 2, rows, cols), F32),
            pltpu.VMEM((3, 4, GROUP, cols), F32),
            pltpu.VMEM((3, 2, WIDE * members, cols), F32),
            pltpu.VMEM((3, rows, cols), F32),
            pltpu.VMEM((NX0, half_m, cols), F32),
            pltpu.VMEM((NX0, 4, half_m, cols), F32),
            pltpu.VMEM((LEVELS, NA, cols), F32),
            pltpu.VMEM((6, NA, cols), F32),
            pltpu.VMEM((LEVELS, half_m, cols), F32),
            pltpu.VMEM((mates, LEVELS, half_m, cols), F32),
            pltpu.VMEM((2, 5 * cols, cols), BF16),
            pltpu.VMEM((2, LEVELS * cols, cols), BF16),
            pltpu.VMEM((2, LEVELS * cols, cols), BF16),
            pltpu.VMEM((LEVELS, cols, cols), BF16),
            pltpu.VMEM((rows, cols), F32),
            pltpu.VMEM((rows, cols), F32),
            pltpu.VMEM((rows, cols), jnp.int32),
            pltpu.VMEM((LEVELS, cols), jnp.int32),
            pltpu.SemaphoreType.DMA((slots,)),
            pltpu.SemaphoreType.DMA((slots,)),
            pltpu.SemaphoreType.DMA((6,)),
        ],
        compiler_params=pltpu.CompilerParams(collective_id=0, has_side_effects=True, vmem_limit_bytes=VMEM_LIMIT),
    )(*(pltpu.with_memory_space_constraint(a, pltpu.HBM) for a in (
        source, guess, conductivity, storage, aggregates, pair_maps.reshape(LEVELS, -1))))


def solution(mesh):
    placed = (
        P(None, "row", "col"),
        P(None, "row", "col"),
        P("row", "col"),
        P("row", "col"),
        P("row", "col"),
        P(None, "row", "col", None),
    )
    return jax.shard_map(
        functools.partial(shards, mesh.shape["row"], mesh.shape["col"]),
        mesh=mesh,
        in_specs=placed,
        out_specs=(P(None, "row", "col"), P(None, "row", "col")),
        check_vma=False,
    )
```

```python
import functools

import jax
import jax.numpy as jnp
from jax import lax
from jax.experimental import pallas as pl
from jax.experimental.pallas import tpu as pltpu
from jax.sharding import PartitionSpec as P

NA = 64
SWEEPS = 3
LEVELS = 4
OMEGA_FINE = 0.8
OMEGA_COARSE = 0.6
F32 = jnp.float32
BF16 = jnp.bfloat16
MESH = pl.DeviceIdType.MESH
OPP = (1, 0, 3, 2, 7, 6, 5, 4)
WIDE = SWEEPS + 1
GROUP = 2 * WIDE
NX0 = 2 * SWEEPS
VMEM_LIMIT = 24 * 1024 * 1024
NN = (((1,), (0,)), ((), ()))
NT = (((1,), (1,)), ((), ()))


def dg(a, b, dims):
    return lax.dot_general(a, b, dims, preferred_element_type=F32)


def split2(x):
    hi = x.astype(BF16)
    return hi, (x - hi.astype(F32)).astype(BF16)


def split3(x):
    hi = x.astype(BF16)
    rest = x - hi.astype(F32)
    mid = rest.astype(BF16)
    return hi, mid, (rest - mid.astype(F32)).astype(BF16)


def dot_parts(x, w_hi, w_lo, dims=NN):
    hi, lo = split2(x)
    return dg(hi, w_hi, dims) + (dg(lo, w_hi, dims) + dg(hi, w_lo, dims))


def dot_hot(x, hot, dims):
    hi, mid, lo = split3(x)
    return dg(hi, hot, dims) + (dg(mid, hot, dims) + dg(lo, hot, dims))


def hot_dot(hot, x, dims):
    hi, mid, lo = split3(x)
    return dg(hot, hi, dims) + (dg(hot, mid, dims) + dg(hot, lo, dims))


def kernel(n_row, n_col, src_in, guess_in, cond_in, sto_in, agg_in, pm_in, sol, res,
           u, se, left, mo, gmat, rlhs, xt, ksend, krecv, kcorn, krsend, krrecv, hsend, hrecv, hcorn, rowbuf,
           rsend, xsend, xrecv, msend, mrecv, vsend, vrecv, wmat, fmat, gfin, qts,
           cond, sto, agg, pm, ssem, rsem, lsem):
    members, rows, cols = guess_in.shape
    half_m = members // 2
    ext = rows + GROUP
    row = lax.axis_index("row")
    col = lax.axis_index("col")
    has = [row > 0, row < n_row - 1, col > 0, col < n_col - 1]
    dev = [(row - 1, col), (row + 1, col), (row, col - 1), (row, col + 1)]
    for v in (0, 1):
        for h in (2, 3):
            has.append(jnp.logical_and(has[v], has[h]))
            dev.append((dev[v][0], dev[h][1]))
    col_bit = col % 2
    row_bit = row % 2
    col_bit2 = col // 2 % 2
    row_bit2 = row // 2 % 2
    upper = (col_bit, row_bit, col_bit2, row_bit2)
    flip_col = (0, 1 - 2 * col_bit, 2 - 4 * col_bit2, 3 - 2 * col_bit - 4 * col_bit2)
    flip_row = (0, 1 - 2 * row_bit, 2 - 4 * row_bit2, 3 - 2 * row_bit - 4 * row_bit2)

    def mate(j):
        return (row + flip_row[j // 2 % 2 + 2 * (j // 8)], col + flip_col[j % 2 + 2 * (j // 4 % 2)])

    loads = [
        pltpu.make_async_copy(source, target, lsem.at[i])
        for i, (source, target) in enumerate((
            (guess_in, u.at[:, pl.ds(0, rows)]), (src_in, se.at[:, pl.ds(0, rows)]),
            (cond_in, cond), (agg_in, agg), (sto_in, sto), (pm_in, pm)))
    ]
    for load in loads:
        load.start()

    barrier = pltpu.get_barrier_semaphore()
    count = jnp.int32(3)
    for d in range(8):
        count = count + has[d].astype(jnp.int32)

        @pl.when(has[d])
        def _():
            pl.semaphore_signal(barrier, inc=1, device_id=dev[d], device_id_type=MESH)

    for j in (4, 8, 12):
        pl.semaphore_signal(barrier, inc=1, device_id=mate(j), device_id_type=MESH)

    def copy(source, target, slot, device):
        return pltpu.make_async_remote_copy(
            src_ref=source, dst_ref=target, send_sem=ssem.at[slot], recv_sem=rsem.at[slot],
            device_id=device, device_id_type=MESH)

    sent = []

    def start(d, source, target, slot):
        @pl.when(has[d])
        def _():
            copy(source, target, slot, dev[d]).start()

        sent.append((d, source, target, slot))

    def arrive(d, source, target, slot):
        @pl.when(has[OPP[d]])
        def _():
            copy(source, target, slot, dev[d]).wait_recv()

    for d in range(8):
        @pl.when(jnp.logical_not(has[OPP[d]]))
        def _():
            if d < 2:
                krrecv[d] = jnp.ones((2 * GROUP, cols), F32)
                for p in range(3):
                    rowbuf[p, d] = jnp.zeros((WIDE * members, cols), F32)
            elif d < 4:
                krecv[d - 2] = jnp.ones((rows, cols), F32)
                for p in range(2):
                    hrecv[p, d - 2] = jnp.zeros((rows, cols), F32)
            else:
                kcorn[d - 4] = jnp.ones((GROUP, cols), F32)
                for p in range(2):
                    hcorn[p, d - 4] = jnp.zeros((GROUP, cols), F32)
            if d < 4:
                for e in range(NX0):
                    xrecv[e, d] = jnp.zeros((half_m, cols), F32)

    lane = lax.broadcasted_iota(jnp.int32, (ext, cols), 1)
    sub = lax.broadcasted_iota(jnp.int32, (ext, cols), 0)
    l8 = lane % GROUP
    owner = lane // GROUP
    lane8 = lane[0:GROUP]
    sub8 = sub[0:GROUP]

    def mirror(x):
        where = lax.broadcasted_iota(jnp.int32, x.shape, 1)
        bit = 1
        while bit < GROUP:
            x = jnp.where(where // bit % 2 == 0, pltpu.roll(x, cols - bit, 1), pltpu.roll(x, bit, 1))
            bit *= 2
        return x

    def repeat(x):
        width = GROUP
        while width < cols:
            x = x + pltpu.roll(x, width, 1)
            width *= 2
        return x

    def side_ref(source, target, corners, d, slot):
        if d < 4:
            return d, source, target.at[d - 2], slot + d
        return d, source.at[pl.ds(0 if d < 6 else rows - GROUP, GROUP)], corners.at[d - 4], slot + d

    def row_ref(p, d):
        return d, rsend.at[p, d], rowbuf.at[p, d], 16 + 2 * p + d

    def field_ref(d):
        return side_ref(hsend.at[0 if d % 2 == 0 else 1], hrecv.at[0], hcorn.at[0], d, 8)

    def again_ref(d):
        if d < 2:
            return row_ref(2, d)
        return side_ref(hsend.at[2], hrecv.at[1], hcorn.at[1], d, 20)

    def coef_ref(d):
        if d < 2:
            return d, krsend.at[d], krrecv.at[d], d
        return side_ref(ksend, krecv, kcorn, d, 0)

    def pack_sides(fields):
        packed = jnp.zeros((rows, cols), F32)
        for m, v in enumerate(fields):
            packed = jnp.where(owner[0:rows] == m, pltpu.roll(v, (GROUP * m + WIDE) % cols, 1), packed)
        return mirror(packed)

    def pack_rows(p, field):
        for m in range(members):
            rsend[p, 0, WIDE * m : WIDE * (m + 1), :] = field[m, 0:WIDE]
            rsend[p, 1, WIDE * m : WIDE * (m + 1), :] = field[m, rows - WIDE : rows]

    order = (2, 3, 1, 0, 4, 5, 6, 7)

    def under(south, north):
        return jnp.where(sub8 < WIDE, south, north)

    def fill_rows(p, field):
        for m in range(members):
            field[m, rows : rows + WIDE, :] = rowbuf[p, 0, WIDE * m : WIDE * (m + 1), :]
            field[m, rows + WIDE : ext, :] = rowbuf[p, 1, WIDE * m : WIDE * (m + 1), :]

    def sides(planes, corners):
        return (jnp.concatenate([planes[0], under(corners[0], corners[2])], axis=0),
                jnp.concatenate([planes[1], under(corners[1], corners[3])], axis=0))

    for load in loads:
        load.wait()
    aggf = agg[...].astype(F32)
    ksend[...] = pack_sides([cond[...], sto[...], aggf])
    for d, near, wide in ((0, 0, 0), (1, rows - WIDE, rows - GROUP)):
        krsend[d, 0:WIDE] = cond[near : near + WIDE]
        krsend[d, WIDE:GROUP] = sto[near : near + WIDE]
        krsend[d, GROUP : 2 * GROUP] = aggf[wide : wide + GROUP]
    side_g = pack_sides([u[m, 0:rows] for m in range(members)])
    side_f = pack_sides([se[m, 0:rows] for m in range(members)])
    inward = l8[0:rows] < WIDE
    hsend[0] = jnp.where(inward, side_g, pltpu.roll(side_f, WIDE, 1))
    hsend[1] = jnp.where(inward, pltpu.roll(side_g, cols - WIDE, 1), side_f)
    pack_rows(0, u)
    pack_rows(1, se)
    pl.semaphore_wait(barrier, count)
    for d in order:
        start(*coef_ref(d))
    for d in (2, 3):
        start(*field_ref(d))
    for p in range(2):
        for d in (1, 0):
            start(*row_ref(p, d))
    for d in range(4, 8):
        start(*field_ref(d))

    agg_v = agg[...]
    sub64 = lax.broadcasted_iota(jnp.int32, (NA, cols), 0)
    for r in range(rows):
        hot = jnp.where(sub64 == agg_v[r : r + 1], 1.0, 0.0).astype(BF16)
        mo[0:NA, r * cols : (r + 1) * cols] = hot
        mo[NA : 2 * NA, r * cols : (r + 1) * cols] = hot
    xt[...] = jnp.zeros(xt.shape, F32)
    iota128 = lax.broadcasted_iota(jnp.int32, (cols, cols), 0)
    lane128 = lax.broadcasted_iota(jnp.int32, (cols, cols), 1)
    for k in range(LEVELS):
        pmk = pm[k : k + 1, :]
        pmk = jnp.where(upper[k] == 1, pltpu.roll(pmk, NA, 1), pmk)
        qts[k] = jnp.where(jnp.logical_and(iota128 == pmk, lane128 < NA), 1.0, 0.0).astype(BF16)

    def face(a, b):
        return 2.0 * (a * b) / (a + b)

    last = rows - 1
    c = cond[...]
    in_east = jnp.where(lane[0:rows] < cols - 1, face(c, pltpu.roll(c, cols - 1, 1)), 0.0)
    in_south = jnp.where(sub[0:rows] < last, face(c, pltpu.roll(c, last, 0)), 0.0)
    right = pltpu.roll(agg_v, cols - 1, 1)
    below = pltpu.roll(agg_v, last, 0)
    half = 0.5 * (sto[...] + in_east + pltpu.roll(in_east, 1, 1) + in_south + pltpu.roll(in_south, 1, 0))
    for r in range(rows):
        s = slice(r, r + 1)
        g = (jnp.where(sub64 == right[s], in_east[s], 0.0)
             + jnp.where(sub64 == below[s], in_south[s], 0.0)
             - jnp.where(sub64 == agg_v[s], half[s], 0.0))
        for i, part in enumerate(split3(g)):
            gmat[i * NA : (i + 1) * NA, r * cols : (r + 1) * cols] = part
    gx = dg(gmat[...], mo[0:NA], NT)
    xt[0:NA, 0:NA] = gx[0:NA] + (gx[NA : 2 * NA] + gx[2 * NA : 3 * NA])
    xfull = xt[...]
    inner = -(xfull + xfull.T)[0:NA]

    lane_c = lax.broadcasted_iota(jnp.int32, (NA, cols), 1)
    lane_1 = lax.broadcasted_iota(jnp.int32, (1, cols), 1)
    eye = jnp.where(lane_c == sub64, 1.0, 0.0)

    def squeeze(k, mat):
        qt = qts[k]
        return hot_dot(qt[0:NA, 0:NA], dot_hot(mat[:, 0:NA], qt[:, 0:NA], NT), NN)

    inner_1 = squeeze(0, inner)
    inner_2 = squeeze(1, inner_1)

    for d in range(8):
        arrive(*coef_ref(d))

    k_east, k_west = sides(krecv, kcorn)
    k_side = jnp.where(l8 < WIDE, k_east, k_west)

    def extend(value, at):
        main = jnp.concatenate([value[...]] + [krrecv[d, at * WIDE : (at + 1) * WIDE] for d in range(2)], axis=0)
        return main, repeat(jnp.where(lane < GROUP, pltpu.roll(k_side, (cols - at * GROUP) % cols, 1), 0.0))

    cm, cs = extend(cond, 0)
    sm, ss = extend(sto, 1)
    hasi = [h.astype(jnp.int32) for h in has[0:4]]

    def vertical(x):
        down = jnp.where(jnp.logical_and(sub == last, hasi[1] == 0), 0.0, face(x, pltpu.roll(x, ext - 1, 0)))
        up = jnp.where(jnp.logical_and(sub == 0, hasi[0] == 0), 0.0, face(x, pltpu.roll(x, 1, 0)))
        return down, up

    side_at = pltpu.roll(cs, cols - WIDE, 1)
    rim = jnp.logical_and(lane >= WIDE - 1, lane <= WIDE)
    main_at = repeat(jnp.where(rim, pltpu.roll(cm, WIDE, 1), 0.0))
    east = face(cm, jnp.where(lane == cols - 1, side_at, pltpu.roll(cm, cols - 1, 1)))
    west = face(cm, jnp.where(lane == 0, side_at, pltpu.roll(cm, 1, 1)))
    east = jnp.where(lane < cols - 1 + hasi[3], east, 0.0)
    west = jnp.where(lane >= 1 - hasi[2], west, 0.0)
    south, north = vertical(cm)
    diag = sm + east + west + south + north
    step = OMEGA_FINE / diag
    s_west = face(cs, jnp.where(l8 == WIDE - 1, main_at, pltpu.roll(cs, cols - 1, 1)))
    s_east = face(cs, jnp.where(l8 == WIDE, main_at, pltpu.roll(cs, 1, 1)))
    s_west = jnp.where(jnp.logical_and(l8 == WIDE - 1, hasi[3] == 0), 0.0, s_west)
    s_east = jnp.where(jnp.logical_and(l8 == WIDE, hasi[2] == 0), 0.0, s_east)
    s_south, s_north = vertical(cs)
    s_diag = ss + s_east + s_west + s_south + s_north
    s_step = OMEGA_FINE / s_diag

    def apply_field(side, n, finish):
        lane_n = lane[0:n]
        edge = jnp.zeros((ext, cols), F32)
        for m in range(members):
            v = u[m]
            hm = pltpu.roll(side, (2 * cols - GROUP * m - WIDE) % cols, 1)[0:n]
            vn = v[0:n]
            from_w = jnp.where(lane_n == 0, hm, pltpu.roll(vn, 1, 1))
            from_e = jnp.where(lane_n == cols - 1, hm, pltpu.roll(vn, cols - 1, 1))
            from_s = pltpu.roll(v, ext - 1, 0)[0:n]
            from_n = pltpu.roll(v, 1, 0)[0:n]
            rest = se[m, 0:n] - (diag[0:n] * vn - (
                east[0:n] * from_e + west[0:n] * from_w + south[0:n] * from_s + north[0:n] * from_n))
            if n == ext:
                edge = jnp.where(owner == m, pltpu.roll(v, (GROUP * m + WIDE) % cols, 1), edge)
            finish(m, vn, rest)
        return edge

    def sweep(side, s_src):
        def finish(m, v, rest):
            u[m] = v + step * rest

        edge = apply_field(side, ext, finish)
        from_w = jnp.where(l8 == WIDE - 1, edge, pltpu.roll(side, cols - 1, 1))
        from_e = jnp.where(l8 == WIDE, edge, pltpu.roll(side, 1, 1))
        rest = s_src - (s_diag * side - (s_east * from_e + s_west * from_w
                        + s_south * pltpu.roll(side, ext - 1, 0) + s_north * pltpu.roll(side, 1, 0)))
        return side + s_step * rest


    agg_t = agg_v.astype(F32).T.astype(jnp.int32)

    def put(ref, slot, block):
        both = jnp.concatenate([block, pltpu.roll(block, NA, 1)], axis=0)
        hi, lo = split2(both)
        ref[0, slot * cols : (slot + 1) * cols] = hi
        ref[1, slot * cols : (slot + 1) * cols] = lo

    def couple(slot, own_ids, other_ids, faces, width):
        own = jnp.where(lax.broadcasted_iota(jnp.int32, (cols, width), 0) == own_ids, 1.0, 0.0).astype(BF16)
        other = jnp.where(lax.broadcasted_iota(jnp.int32, (NA, width), 0) == other_ids, faces, 0.0)
        links = dot_hot(other, own, NT)
        put(wmat, slot, -links)
        return jnp.sum(links, axis=0, keepdims=True)

    row_ids = [krrecv[d].astype(jnp.int32) for d in range(2)]
    outer = couple(1, agg_v[last:rows], row_ids[0][GROUP : GROUP + 1], south[last:rows], cols)
    outer = outer + couple(2, agg_v[0:1], row_ids[1][2 * GROUP - 1 : 2 * GROUP], north[0:1], cols)
    k_ids = k_side[0:rows].T.astype(jnp.int32)
    near_e = 2 * GROUP + WIDE - 1
    outer = outer + couple(3, agg_t[cols - 1 : cols], k_ids[near_e : near_e + 1], east[0:rows].T[cols - 1 : cols], rows)
    outer = outer + couple(4, agg_t[0:1], k_ids[near_e + 1 : near_e + 2], west[0:rows].T[0:1], rows)

    def mat_copy(i):
        j = (1, 2, 3, 4, 8, 12)[i]
        return copy(msend.at[(0, 1, 1, 2, 3, 3)[i]], mrecv.at[i], 28 + 4 * NX0 + i, mate(j))

    def vec_copy(j):
        low = j.bit_length() - 1
        part = pl.ds(low, LEVELS - low)
        return copy(vsend.at[part], vrecv.at[j - 1, part], 34 + 4 * NX0 + j - 1, mate(j))

    def weight(mat):
        d = jnp.sum(jnp.where(lane_c == sub64, mat, 0.0), axis=0, keepdims=True)
        ok = lane_1 < NA
        return jnp.where(ok, OMEGA_COARSE / jnp.where(ok, d, 1.0), 0.0)

    def smoother(mat):
        side_w = OMEGA_COARSE / jnp.sum(eye * mat, axis=1, keepdims=True)
        one = eye - mat * weight(mat)
        hi, lo = split2(one)
        two = dot_parts(one[:, 0:NA], hi, lo)
        return dot_parts(two[:, 0:NA], hi, lo), side_w * (eye + one + two)

    def apply_parts(a, b):
        return dot_parts(a[:, 0:NA], *split2(b))

    block = inner + jnp.where(lane_c == sub64, outer, 0.0)
    outer_1 = dot_hot(jnp.broadcast_to(outer[:, 0:NA], (8, NA)), qts[0][:, 0:NA], NT)
    outer_2 = dot_hot(outer_1[:, 0:NA], qts[1][:, 0:NA], NT)
    msend[0] = inner_1 + eye * outer_1[0:1]
    msend[1] = inner_2 + eye * outer_2[0:1]
    for i in range(3):
        mat_copy(i).start()
    put(wmat, 0, block)
    weights = weight(block)
    weights = weights + pltpu.roll(weights, NA, 1)

    for d in range(2, 8):
        arrive(*field_ref(d))
    for p in range(2):
        for d in range(2):
            arrive(*row_ref(p, d))
    fill_rows(0, u)
    fill_rows(1, se)
    h_east, h_west = sides(hrecv[0], hcorn[0])
    side = jnp.where(l8 < WIDE, h_east, pltpu.roll(h_west, WIDE, 1))
    s_src = jnp.where(l8 < WIDE, pltpu.roll(h_east, cols - WIDE, 1), h_west)
    for _ in range(SWEEPS):
        side = sweep(side, s_src)

    def keep_left(m, v, rest):
        left[m] = rest

    apply_field(side, rows, keep_left)
    for r in range(rows):
        for i, part in enumerate(split2(left[:, r, :])):
            rlhs[i * members : (i + 1) * members, r * cols : (r + 1) * cols] = part
    gr = dg(rlhs[...], mo[...], NT)
    gr = gr[0:members] + gr[members : 2 * members]
    lane_h = lax.broadcasted_iota(jnp.int32, (half_m, cols), 1)

    def fold(x):
        return jnp.where(lane_h < NA, x[0:half_m], x[half_m:members])

    y0 = fold(gr)

    def x_slot(e, d):
        return (d, xsend.at[e], xrecv.at[e, d], 28 + 4 * e + d)

    def level_one(e, x, between=None):
        xsend[e] = x
        for d in (2, 3, 1, 0):
            start(*x_slot(e, d))
        if between is not None:
            between()
        for d in range(4):
            arrive(*x_slot(e, d))
        every = jnp.concatenate([x] + [xrecv[e, d] for d in range(4)], axis=1)
        return dot_parts(every, wmat[0], wmat[1])

    keep = {}

    def first_mats():
        for i in range(3):
            mat_copy(i).wait_recv()
        mat_1 = msend[0] + mrecv[0]
        mat_2 = squeeze(1, mat_1) + (mrecv[1] + mrecv[2])
        mat_3 = squeeze(2, mat_2)
        msend[2] = mat_3
        msend[3] = squeeze(3, mat_3)
        for i in range(3, 6):
            mat_copy(i).start()
        keep["mats"] = [mat_1, mat_2]

    def chains():
        smooth = [smoother(mat) for mat in keep["mats"]]
        for i in range(3, 6):
            mat_copy(i).wait_recv()
        mat_3 = msend[2] + mrecv[3]
        mat_4 = squeeze(3, mat_3) + (mrecv[4] + mrecv[5])
        smooth.append(smoother(mat_3))
        chain = qts[0][0:NA].astype(F32)
        for k in range(LEVELS):
            put(fmat, k, chain)
            if k + 1 < LEVELS:
                cube, pre = smooth[k]
                moved = apply_parts(cube, chain)
                put(gfin, k, apply_parts(pre, chain + moved))
                chain = hot_dot(qts[k + 1][0:NA, 0:NA], moved, NN)
        solve = jnp.where(lane_c < NA, mat_4, pltpu.roll(chain, NA, 1))
        keep["solve"] = [solve[k : k + GROUP] for k in range(0, NA, GROUP)]

    sub_g = lax.broadcasted_iota(jnp.int32, (GROUP, cols), 0)

    def lanes_of(v, k):
        return jnp.broadcast_to(v[:, k : k + 1], (GROUP, cols))

    def row_of(v, r):
        return jnp.broadcast_to(v[r : r + 1], (GROUP, cols))

    def pair_product(a, b):
        return [[a[i][0] * b[0][j] + a[i][1] * b[1][j] for j in range(2)] for i in range(2)]

    def pair_inverse(a):
        scale = 1.0 / (a[0][0] * a[1][1] - a[0][1] * a[1][0])
        return [[a[1][1] * scale, -a[0][1] * scale], [-a[1][0] * scale, a[0][0] * scale]]

    def quad_inverse(a):
        first = pair_inverse([a[i][0:2] for i in range(2)])
        right = pair_product(first, [a[i][2:4] for i in range(2)])
        below = [a[i][0:2] for i in range(2, 4)]
        moved = pair_product(below, right)
        second = pair_inverse([[a[2 + i][2 + j] - moved[i][j] for j in range(2)] for i in range(2)])
        down = pair_product(second, pair_product(below, first))
        back = pair_product(right, down)
        over = pair_product(right, second)
        return ([[first[i][j] + back[i][j] for j in range(2)] + [-over[i][j] for j in range(2)] for i in range(2)]
                + [[-down[i][j] for j in range(2)] + second[i] for i in range(2)])

    def eliminate(first, end):
        blocks = keep["solve"]
        for k in range(first, end, 4):
            q, r = k // GROUP, k % GROUP
            across = [[lanes_of(v, k + j) for v in blocks] for j in range(4)]
            inv = quad_inverse([[row_of(across[j][q], r + i) for j in range(4)] for i in range(4)])
            held = [row_of(blocks[q], r + i) for i in range(4)]
            pivots = [(inv[i][0] * held[0] + inv[i][1] * held[1]) + (inv[i][2] * held[2] + inv[i][3] * held[3])
                      for i in range(4)]
            blocks = [v - ((across[0][i] * pivots[0] + across[1][i] * pivots[1])
                           + (across[2][i] * pivots[2] + across[3][i] * pivots[3])) for i, v in enumerate(blocks)]
            for i in range(4):
                blocks[q] = jnp.where(sub_g == r + i, pivots[i], blocks[q])
        keep["solve"] = blocks

    x = y0 * weights
    x = x + (y0 - level_one(0, x, first_mats)) * weights
    x = x + (y0 - level_one(1, x, chains)) * weights
    rem = y0 - level_one(2, x, lambda: eliminate(0, NA // 2))
    up = dot_parts(rem, fmat[0], fmat[1], NT)
    for k in range(LEVELS):
        vsend[k] = up[:, k * cols : (k + 1) * cols]
    for j in reversed(range(1, 2 ** LEVELS)):
        vec_copy(j).start()
    eliminate(NA // 2, NA)
    put(gfin, LEVELS - 1, jnp.where(
        lane_c < NA, pltpu.roll(jnp.concatenate(keep["solve"], axis=0), NA, 1), 0.0))
    for j in range(1, 2 ** LEVELS):
        vec_copy(j).wait_recv()
    ys = []
    for k in range(LEVELS):
        y = vsend[k]
        for j in range(1, 2 ** (k + 1)):
            y = y + vrecv[j - 1, k]
        ys.append(y)
    x = x + dot_parts(jnp.concatenate(ys, axis=1), gfin[0], gfin[1])
    for i in range(SWEEPS):
        x = x + (y0 - level_one(SWEEPS + i, x)) * weights

    whole = jnp.concatenate([x, pltpu.roll(x, NA, 1)], axis=0)
    whole_hi = whole.astype(BF16).astype(F32)
    lane_m = lax.broadcasted_iota(jnp.int32, (members, cols), 1)
    spread = jnp.where(lane_m < NA, whole_hi, pltpu.roll(whole - whole_hi, NA, 1)).astype(BF16)
    for r in range(rows):
        part = dg(spread, mo[:, r * cols : (r + 1) * cols], NN)
        u[:, r, :] = u[:, r, :] + part
    hsend[2] = pack_sides([u[m, 0:rows] for m in range(members)])
    pack_rows(2, u)
    for d in order:
        start(*again_ref(d))
    for d in range(8):
        arrive(*again_ref(d))
    fill_rows(2, u)
    h_east, h_west = sides(hrecv[1], hcorn[1])
    side = jnp.where(l8 < WIDE, h_east, h_west)
    for _ in range(SWEEPS):
        side = sweep(side, s_src)

    def out(m, v, rest):
        sol[m] = v
        res[m] = rest

    apply_field(side, rows, out)
    for d, source, target, slot in sent:
        @pl.when(has[d])
        def _():
            copy(source, target, slot, dev[d]).wait_send()

    for i in range(6):
        mat_copy(i).wait_send()
    for j in range(1, 2 ** LEVELS):
        vec_copy(j).wait_send()


def shards(n_row, n_col, source, guess, conductivity, storage, aggregates, pair_maps):
    members, rows, cols = source.shape
    cells = rows * cols
    ext = rows + GROUP
    vm = pl.BlockSpec(memory_space=pltpu.VMEM)
    half_m = members // 2
    mates = 2 ** LEVELS - 1
    slots = 34 + 4 * NX0 + mates
    hbm = pl.BlockSpec(memory_space=pltpu.HBM)
    return pl.pallas_call(
        functools.partial(kernel, n_row, n_col),
        out_shape=(jax.ShapeDtypeStruct(source.shape, F32),) * 2,
        in_specs=[hbm] * 6,
        out_specs=(vm, vm),
        scratch_shapes=[
            pltpu.VMEM((members, ext, cols), F32),
            pltpu.VMEM((members, ext, cols), F32),
            pltpu.VMEM((members, rows, cols), F32),
            pltpu.VMEM((2 * NA, cells), BF16),
            pltpu.VMEM((3 * NA, cells), BF16),
            pltpu.VMEM((2 * members, cells), BF16),
            pltpu.VMEM((cols, cols), F32),
            pltpu.VMEM((rows, cols), F32),
            pltpu.VMEM((2, rows, cols), F32),
            pltpu.VMEM((4, GROUP, cols), F32),
            pltpu.VMEM((2, 2 * GROUP, cols), F32),
            pltpu.VMEM((2, 2 * GROUP, cols), F32),
            pltpu.VMEM((3, rows, cols), F32),
            pltpu.VMEM((2, 2, rows, cols), F32),
            pltpu.VMEM((2, 4, GROUP, cols), F32),
            pltpu.VMEM((3, 2, WIDE * members, cols), F32),
            pltpu.VMEM((3, 2, WIDE * members, cols), F32),
            pltpu.VMEM((NX0, half_m, cols), F32),
            pltpu.VMEM((NX0, 4, half_m, cols), F32),
            pltpu.VMEM((LEVELS, NA, cols), F32),
            pltpu.VMEM((6, NA, cols), F32),
            pltpu.VMEM((LEVELS, half_m, cols), F32),
            pltpu.VMEM((mates, LEVELS, half_m, cols), F32),
            pltpu.VMEM((2, 5 * cols, cols), BF16),
            pltpu.VMEM((2, LEVELS * cols, cols), BF16),
            pltpu.VMEM((2, LEVELS * cols, cols), BF16),
            pltpu.VMEM((LEVELS, cols, cols), BF16),
            pltpu.VMEM((rows, cols), F32),
            pltpu.VMEM((rows, cols), F32),
            pltpu.VMEM((rows, cols), jnp.int32),
            pltpu.VMEM((LEVELS, cols), jnp.int32),
            pltpu.SemaphoreType.DMA((slots,)),
            pltpu.SemaphoreType.DMA((slots,)),
            pltpu.SemaphoreType.DMA((6,)),
        ],
        compiler_params=pltpu.CompilerParams(collective_id=0, has_side_effects=True, vmem_limit_bytes=VMEM_LIMIT),
    )(*(pltpu.with_memory_space_constraint(a, pltpu.HBM) for a in (
        source, guess, conductivity, storage, aggregates, pair_maps.reshape(LEVELS, -1))))


def solution(mesh):
    placed = (
        P(None, "row", "col"),
        P(None, "row", "col"),
        P("row", "col"),
        P("row", "col"),
        P("row", "col"),
        P(None, "row", "col", None),
    )
    return jax.shard_map(
        functools.partial(shards, mesh.shape["row"], mesh.shape["col"]),
        mesh=mesh,
        in_specs=placed,
        out_specs=(P(None, "row", "col"), P(None, "row", "col")),
        check_vma=False,
    )
```

```python
import functools

import jax
import jax.numpy as jnp
from jax import lax
from jax.experimental import pallas as pl
from jax.experimental.pallas import tpu as pltpu
from jax.sharding import PartitionSpec as P

NA = 64
SWEEPS = 3
LEVELS = 4
OMEGA_FINE = 0.8
OMEGA_COARSE = 0.6
F32 = jnp.float32
BF16 = jnp.bfloat16
MESH = pl.DeviceIdType.MESH
OPP = (1, 0, 3, 2, 7, 6, 5, 4, 9, 8, 11, 10)
WIDE = SWEEPS + 1
GROUP = 2 * WIDE
HOPS = 28
NEAR = HOPS + 32
MATS = NEAR + 4
VECS = MATS + 6
NX0 = 2
CORNERS = ((1, 3), (1, 2), (0, 3), (0, 2))
VMEM_LIMIT = 24 * 1024 * 1024
NN = (((1,), (0,)), ((), ()))
NT = (((1,), (1,)), ((), ()))


def dg(a, b, dims):
    return lax.dot_general(a, b, dims, preferred_element_type=F32)


def split2(x):
    hi = x.astype(BF16)
    return hi, (x - hi.astype(F32)).astype(BF16)


def split3(x):
    hi = x.astype(BF16)
    rest = x - hi.astype(F32)
    mid = rest.astype(BF16)
    return hi, mid, (rest - mid.astype(F32)).astype(BF16)


def dot_parts(x, w_hi, w_lo, dims=NN):
    hi, lo = split2(x)
    return dg(hi, w_hi, dims) + (dg(lo, w_hi, dims) + dg(hi, w_lo, dims))


def stacked(x):
    hi = x.astype(BF16).astype(F32)
    return jnp.concatenate([hi, x - hi], axis=0).astype(BF16)


def times(x, weights):
    n, wide = x.shape[0], weights.shape[1] // 2
    full = dg(stacked(x), weights, NN)
    return full[0:n, 0:wide] + (full[n:, 0:wide] + full[0:n, wide:])


def times_t(x, weights):
    n = x.shape[0]
    both = stacked(x)
    full = dg(jnp.concatenate([both, both], axis=1), weights, NT)
    return full[0:n] + full[n:]


def dot_hot(x, hot, dims):
    hi, mid, lo = split3(x)
    return dg(hi, hot, dims) + (dg(mid, hot, dims) + dg(lo, hot, dims))


def hot_dot(hot, x, dims):
    hi, mid, lo = split3(x)
    return dg(hot, hi, dims) + (dg(hot, mid, dims) + dg(hot, lo, dims))


def kernel(n_row, n_col, src_in, guess_in, cond_in, sto_in, agg_in, pm_in, sol, res,
           u, se, left, mo, gmat, rlhs, xt, ksend, krecv, kcorn, krsend, krrecv, hsend, hrecv, hcorn, rowbuf,
           rsend, xsend, xrecv, nsend, nrecv, tsend, trecv, csend, crecv, srecv, msend, mrecv, vsend, vrecv, wmat, fmat, gfin, qts,
           cond, sto, agg, pm, ssem, rsem, lsem):
    members, rows, cols = guess_in.shape
    half_m = members // 2
    ext = rows + GROUP
    row = lax.axis_index("row")
    col = lax.axis_index("col")
    has = [row > 0, row < n_row - 1, col > 0, col < n_col - 1]
    dev = [(row - 1, col), (row + 1, col), (row, col - 1), (row, col + 1)]
    for v in (0, 1):
        for h in (2, 3):
            has.append(jnp.logical_and(has[v], has[h]))
            dev.append((dev[v][0], dev[h][1]))
    far_has = [row > 1, row < n_row - 2, col > 1, col < n_col - 2]
    far_dev = [(row - 2, col), (row + 2, col), (row, col - 2), (row, col + 2)]
    has += far_has
    dev += far_dev
    col_bit = col % 2
    row_bit = row % 2
    col_bit2 = col // 2 % 2
    row_bit2 = row // 2 % 2
    upper = (col_bit, row_bit, col_bit2, row_bit2)
    flip_col = (0, 1 - 2 * col_bit, 2 - 4 * col_bit2, 3 - 2 * col_bit - 4 * col_bit2)
    flip_row = (0, 1 - 2 * row_bit, 2 - 4 * row_bit2, 3 - 2 * row_bit - 4 * row_bit2)

    def mate(j):
        return (row + flip_row[j // 2 % 2 + 2 * (j // 8)], col + flip_col[j % 2 + 2 * (j // 4 % 2)])

    loads = [
        pltpu.make_async_copy(source, target, lsem.at[i])
        for i, (source, target) in enumerate((
            (guess_in, u.at[:, pl.ds(0, rows)]), (src_in, se.at[:, pl.ds(0, rows)]),
            (cond_in, cond), (agg_in, agg), (sto_in, sto), (pm_in, pm)))
    ]
    for load in loads:
        load.start()

    barrier = pltpu.get_barrier_semaphore()
    count = jnp.int32(0)
    for d in range(8):
        count = count + has[d].astype(jnp.int32)

        @pl.when(has[d])
        def _():
            pl.semaphore_signal(barrier, inc=1, device_id=dev[d], device_id_type=MESH)

    def copy(source, target, slot, device):
        return pltpu.make_async_remote_copy(
            src_ref=source, dst_ref=target, send_sem=ssem.at[slot], recv_sem=rsem.at[slot],
            device_id=device, device_id_type=MESH)

    sent = []

    def start(d, source, target, slot):
        @pl.when(has[d])
        def _():
            copy(source, target, slot, dev[d]).start()

        sent.append((d, source, target, slot))

    def arrive(d, source, target, slot):
        @pl.when(has[OPP[d]])
        def _():
            copy(source, target, slot, dev[d]).wait_recv()

    for d in range(12):
        @pl.when(jnp.logical_not(has[OPP[d]]))
        def _():
            if d < 2:
                krrecv[d] = jnp.ones((2 * GROUP, cols), F32)
                for p in range(3):
                    rowbuf[p, d] = jnp.zeros((WIDE * members, cols), F32)
            elif d < 4:
                krecv[d - 2] = jnp.ones((rows, cols), F32)
                for p in range(2):
                    hrecv[p, d - 2] = jnp.zeros((rows, cols), F32)
            elif d < 8:
                kcorn[d - 4] = jnp.ones((GROUP, cols), F32)
                for p in range(2):
                    hcorn[p, d - 4] = jnp.zeros((GROUP, cols), F32)
            for e in range(NX0):
                if d < 4:
                    xrecv[e, d] = jnp.zeros((half_m, cols), F32)
                    trecv[e, d] = jnp.zeros((2 * half_m, cols), F32)
                elif d < 8:
                    crecv[e, d - 4] = jnp.zeros((2 * half_m, cols), F32)
                else:
                    srecv[e, d - 8] = jnp.zeros((half_m, cols), F32)
            if d < 4:
                nrecv[d] = jnp.zeros((half_m, cols), F32)

    lane = lax.broadcasted_iota(jnp.int32, (ext, cols), 1)
    sub = lax.broadcasted_iota(jnp.int32, (ext, cols), 0)
    l8 = lane % GROUP
    owner = lane // GROUP
    lane8 = lane[0:GROUP]
    sub8 = sub[0:GROUP]

    def mirror(x):
        where = lax.broadcasted_iota(jnp.int32, x.shape, 1)
        bit = 1
        while bit < GROUP:
            x = jnp.where(where // bit % 2 == 0, pltpu.roll(x, cols - bit, 1), pltpu.roll(x, bit, 1))
            bit *= 2
        return x

    def repeat(x):
        width = GROUP
        while width < cols:
            x = x + pltpu.roll(x, width, 1)
            width *= 2
        return x

    def side_ref(source, target, corners, d, slot):
        if d < 4:
            return d, source, target.at[d - 2], slot + d
        return d, source.at[pl.ds(0 if d < 6 else rows - GROUP, GROUP)], corners.at[d - 4], slot + d

    def row_ref(p, d):
        return d, rsend.at[p, d], rowbuf.at[p, d], 16 + 2 * p + d

    def field_ref(d):
        return side_ref(hsend.at[0 if d % 2 == 0 else 1], hrecv.at[0], hcorn.at[0], d, 8)

    def again_ref(d):
        if d < 2:
            return row_ref(2, d)
        return side_ref(hsend.at[2], hrecv.at[1], hcorn.at[1], d, 20)

    def coef_ref(d):
        if d < 2:
            return d, krsend.at[d], krrecv.at[d], d
        return side_ref(ksend, krecv, kcorn, d, 0)

    def pack_sides(fields):
        packed = jnp.zeros((rows, cols), F32)
        for m, v in enumerate(fields):
            packed = jnp.where(owner[0:rows] == m, pltpu.roll(v, (GROUP * m + WIDE) % cols, 1), packed)
        return mirror(packed)

    def pack_rows(p, field):
        for m in range(members):
            rsend[p, 0, WIDE * m : WIDE * (m + 1), :] = field[m, 0:WIDE]
            rsend[p, 1, WIDE * m : WIDE * (m + 1), :] = field[m, rows - WIDE : rows]

    order = (2, 3, 1, 0, 4, 5, 6, 7)

    def under(south, north):
        return jnp.where(sub8 < WIDE, south, north)

    def fill_rows(p, field):
        for m in range(members):
            field[m, rows : rows + WIDE, :] = rowbuf[p, 0, WIDE * m : WIDE * (m + 1), :]
            field[m, rows + WIDE : ext, :] = rowbuf[p, 1, WIDE * m : WIDE * (m + 1), :]

    def sides(planes, corners):
        return (jnp.concatenate([planes[0], under(corners[0], corners[2])], axis=0),
                jnp.concatenate([planes[1], under(corners[1], corners[3])], axis=0))

    for load in loads:
        load.wait()
    aggf = agg[...].astype(F32)
    ksend[...] = pack_sides([cond[...], sto[...], aggf])
    for d, near, wide in ((0, 0, 0), (1, rows - WIDE, rows - GROUP)):
        krsend[d, 0:WIDE] = cond[near : near + WIDE]
        krsend[d, WIDE:GROUP] = sto[near : near + WIDE]
        krsend[d, GROUP : 2 * GROUP] = aggf[wide : wide + GROUP]
    side_g = pack_sides([u[m, 0:rows] for m in range(members)])
    side_f = pack_sides([se[m, 0:rows] for m in range(members)])
    inward = l8[0:rows] < WIDE
    hsend[0] = jnp.where(inward, side_g, pltpu.roll(side_f, WIDE, 1))
    hsend[1] = jnp.where(inward, pltpu.roll(side_g, cols - WIDE, 1), side_f)
    pack_rows(0, u)
    pack_rows(1, se)
    pl.semaphore_wait(barrier, count)
    for d in order:
        start(*coef_ref(d))
    for d in (2, 3):
        start(*field_ref(d))
    for p in range(2):
        for d in (1, 0):
            start(*row_ref(p, d))
    for d in range(4, 8):
        start(*field_ref(d))

    agg_v = agg[...]
    sub64 = lax.broadcasted_iota(jnp.int32, (NA, cols), 0)
    for r in range(rows):
        hot = jnp.where(sub64 == agg_v[r : r + 1], 1.0, 0.0).astype(BF16)
        mo[0:NA, r * cols : (r + 1) * cols] = hot
        mo[NA : 2 * NA, r * cols : (r + 1) * cols] = hot
    xt[...] = jnp.zeros(xt.shape, F32)
    iota128 = lax.broadcasted_iota(jnp.int32, (cols, cols), 0)
    lane128 = lax.broadcasted_iota(jnp.int32, (cols, cols), 1)
    for k in range(LEVELS):
        pmk = pm[k : k + 1, :]
        pmk = jnp.where(upper[k] == 1, pltpu.roll(pmk, NA, 1), pmk)
        qts[k] = jnp.where(jnp.logical_and(iota128 == pmk, lane128 < NA), 1.0, 0.0).astype(BF16)

    def face(a, b):
        return 2.0 * (a * b) / (a + b)

    last = rows - 1
    c = cond[...]
    in_east = jnp.where(lane[0:rows] < cols - 1, face(c, pltpu.roll(c, cols - 1, 1)), 0.0)
    in_south = jnp.where(sub[0:rows] < last, face(c, pltpu.roll(c, last, 0)), 0.0)
    right = pltpu.roll(agg_v, cols - 1, 1)
    below = pltpu.roll(agg_v, last, 0)
    half = 0.5 * (sto[...] + in_east + pltpu.roll(in_east, 1, 1) + in_south + pltpu.roll(in_south, 1, 0))
    for r in range(rows):
        s = slice(r, r + 1)
        g = (jnp.where(sub64 == right[s], in_east[s], 0.0)
             + jnp.where(sub64 == below[s], in_south[s], 0.0)
             - jnp.where(sub64 == agg_v[s], half[s], 0.0))
        for i, part in enumerate(split3(g)):
            gmat[i * NA : (i + 1) * NA, r * cols : (r + 1) * cols] = part
    gx = dg(gmat[...], mo[0:NA], NT)
    xt[0:NA, 0:NA] = gx[0:NA] + (gx[NA : 2 * NA] + gx[2 * NA : 3 * NA])
    xfull = xt[...]
    inner = -(xfull + xfull.T)[0:NA]

    lane_c = lax.broadcasted_iota(jnp.int32, (NA, cols), 1)
    lane_1 = lax.broadcasted_iota(jnp.int32, (1, cols), 1)
    eye = jnp.where(lane_c == sub64, 1.0, 0.0)

    def squeeze(k, mat):
        qt = qts[k]
        return hot_dot(qt[0:NA, 0:NA], dot_hot(mat[:, 0:NA], qt[:, 0:NA], NT), NN)

    inner_1 = squeeze(0, inner)
    inner_2 = squeeze(1, inner_1)

    for d in range(8):
        arrive(*coef_ref(d))

    k_east, k_west = sides(krecv, kcorn)
    k_side = jnp.where(l8 < WIDE, k_east, k_west)

    def extend(value, at):
        main = jnp.concatenate([value[...]] + [krrecv[d, at * WIDE : (at + 1) * WIDE] for d in range(2)], axis=0)
        return main, repeat(jnp.where(lane < GROUP, pltpu.roll(k_side, (cols - at * GROUP) % cols, 1), 0.0))

    cm, cs = extend(cond, 0)
    sm, ss = extend(sto, 1)
    hasi = [h.astype(jnp.int32) for h in has[0:4]]

    def vertical(x):
        down = jnp.where(jnp.logical_and(sub == last, hasi[1] == 0), 0.0, face(x, pltpu.roll(x, ext - 1, 0)))
        up = jnp.where(jnp.logical_and(sub == 0, hasi[0] == 0), 0.0, face(x, pltpu.roll(x, 1, 0)))
        return down, up

    side_at = pltpu.roll(cs, cols - WIDE, 1)
    rim = jnp.logical_and(lane >= WIDE - 1, lane <= WIDE)
    main_at = repeat(jnp.where(rim, pltpu.roll(cm, WIDE, 1), 0.0))
    east = face(cm, jnp.where(lane == cols - 1, side_at, pltpu.roll(cm, cols - 1, 1)))
    west = face(cm, jnp.where(lane == 0, side_at, pltpu.roll(cm, 1, 1)))
    east = jnp.where(lane < cols - 1 + hasi[3], east, 0.0)
    west = jnp.where(lane >= 1 - hasi[2], west, 0.0)
    south, north = vertical(cm)
    diag = sm + east + west + south + north
    step = OMEGA_FINE / diag
    s_west = face(cs, jnp.where(l8 == WIDE - 1, main_at, pltpu.roll(cs, cols - 1, 1)))
    s_east = face(cs, jnp.where(l8 == WIDE, main_at, pltpu.roll(cs, 1, 1)))
    s_west = jnp.where(jnp.logical_and(l8 == WIDE - 1, hasi[3] == 0), 0.0, s_west)
    s_east = jnp.where(jnp.logical_and(l8 == WIDE, hasi[2] == 0), 0.0, s_east)
    s_south, s_north = vertical(cs)
    s_diag = ss + s_east + s_west + s_south + s_north
    s_step = OMEGA_FINE / s_diag

    def apply_field(side, n, finish):
        lane_n = lane[0:n]
        edge = jnp.zeros((ext, cols), F32)
        for m in range(members):
            v = u[m]
            hm = pltpu.roll(side, (2 * cols - GROUP * m - WIDE) % cols, 1)[0:n]
            vn = v[0:n]
            from_w = jnp.where(lane_n == 0, hm, pltpu.roll(vn, 1, 1))
            from_e = jnp.where(lane_n == cols - 1, hm, pltpu.roll(vn, cols - 1, 1))
            from_s = pltpu.roll(v, ext - 1, 0)[0:n]
            from_n = pltpu.roll(v, 1, 0)[0:n]
            rest = se[m, 0:n] - (diag[0:n] * vn - (
                east[0:n] * from_e + west[0:n] * from_w + south[0:n] * from_s + north[0:n] * from_n))
            if n == ext:
                edge = jnp.where(owner == m, pltpu.roll(v, (GROUP * m + WIDE) % cols, 1), edge)
            finish(m, vn, rest)
        return edge

    def sweep(side, s_src):
        def finish(m, v, rest):
            u[m] = v + step * rest

        edge = apply_field(side, ext, finish)
        from_w = jnp.where(l8 == WIDE - 1, edge, pltpu.roll(side, cols - 1, 1))
        from_e = jnp.where(l8 == WIDE, edge, pltpu.roll(side, 1, 1))
        rest = s_src - (s_diag * side - (s_east * from_e + s_west * from_w
                        + s_south * pltpu.roll(side, ext - 1, 0) + s_north * pltpu.roll(side, 1, 0)))
        return side + s_step * rest


    agg_t = agg_v.astype(F32).T.astype(jnp.int32)

    def put(ref, slot, block):
        both = jnp.concatenate([block, pltpu.roll(block, NA, 1)], axis=0)
        hi, lo = split2(both)
        ref[slot * cols : (slot + 1) * cols, 0:cols] = hi
        ref[slot * cols : (slot + 1) * cols, cols : 2 * cols] = lo

    def couple(slot, own_ids, other_ids, faces, width):
        own = jnp.where(lax.broadcasted_iota(jnp.int32, (cols, width), 0) == own_ids, 1.0, 0.0).astype(BF16)
        other = jnp.where(lax.broadcasted_iota(jnp.int32, (NA, width), 0) == other_ids, faces, 0.0)
        links = dot_hot(other, own, NT)
        put(wmat, slot, -links)
        return jnp.sum(links, axis=0, keepdims=True)

    row_ids = [krrecv[d].astype(jnp.int32) for d in range(2)]
    outer = couple(1, agg_v[last:rows], row_ids[0][GROUP : GROUP + 1], south[last:rows], cols)
    outer = outer + couple(2, agg_v[0:1], row_ids[1][2 * GROUP - 1 : 2 * GROUP], north[0:1], cols)
    k_ids = k_side[0:rows].T.astype(jnp.int32)
    near_e = 2 * GROUP + WIDE - 1
    outer = outer + couple(3, agg_t[cols - 1 : cols], k_ids[near_e : near_e + 1], east[0:rows].T[cols - 1 : cols], rows)
    outer = outer + couple(4, agg_t[0:1], k_ids[near_e + 1 : near_e + 2], west[0:rows].T[0:1], rows)

    def mat_copy(i):
        j = (1, 2, 3, 4, 8, 12)[i]
        return copy(msend.at[(0, 1, 1, 2, 3, 3)[i]], mrecv.at[i], MATS + i, mate(j))

    def vec_copy(j):
        low = j.bit_length() - 1
        part = pl.ds(low, LEVELS - low)
        return copy(vsend.at[part], vrecv.at[j - 1, part], VECS + j - 1, mate(j))

    def weight(mat):
        d = jnp.sum(jnp.where(lane_c == sub64, mat, 0.0), axis=0, keepdims=True)
        ok = lane_1 < NA
        return jnp.where(ok, OMEGA_COARSE / jnp.where(ok, d, 1.0), 0.0)

    def smoother(mat):
        side_w = OMEGA_COARSE / jnp.sum(eye * mat, axis=1, keepdims=True)
        one = eye - mat * weight(mat)
        hi, lo = split2(one)
        two = dot_parts(one[:, 0:NA], hi, lo)
        return dot_parts(two[:, 0:NA], hi, lo), side_w * (eye + one + two)

    def apply_parts(a, b):
        return dot_parts(a[:, 0:NA], *split2(b))

    block = inner + jnp.where(lane_c == sub64, outer, 0.0)
    outer_1 = dot_hot(jnp.broadcast_to(outer[:, 0:NA], (8, NA)), qts[0][:, 0:NA], NT)
    outer_2 = dot_hot(outer_1[:, 0:NA], qts[1][:, 0:NA], NT)
    msend[0] = inner_1 + eye * outer_1[0:1]
    msend[1] = inner_2 + eye * outer_2[0:1]
    for i in range(3):
        mat_copy(i).start()
    put(wmat, 0, block)
    weights = weight(block)
    weights = jnp.broadcast_to(weights + pltpu.roll(weights, NA, 1), (half_m, cols))
    nsend[...] = weights

    def near_ref(d):
        return d, nsend, nrecv.at[d], NEAR + d

    for d in (2, 3, 1, 0):
        start(*near_ref(d))

    for d in range(2, 8):
        arrive(*field_ref(d))
    for p in range(2):
        for d in range(2):
            arrive(*row_ref(p, d))
    fill_rows(0, u)
    fill_rows(1, se)
    h_east, h_west = sides(hrecv[0], hcorn[0])
    side = jnp.where(l8 < WIDE, h_east, pltpu.roll(h_west, WIDE, 1))
    s_src = jnp.where(l8 < WIDE, pltpu.roll(h_east, cols - WIDE, 1), h_west)
    for _ in range(SWEEPS):
        side = sweep(side, s_src)

    def keep_left(m, v, rest):
        left[m] = rest

    apply_field(side, rows, keep_left)
    for r in range(rows):
        for i, part in enumerate(split2(left[:, r, :])):
            rlhs[i * members : (i + 1) * members, r * cols : (r + 1) * cols] = part
    gr = dg(rlhs[...], mo[...], NT)
    gr = gr[0:members] + gr[members : 2 * members]
    lane_h = lax.broadcasted_iota(jnp.int32, (half_m, cols), 1)

    def fold(x):
        return jnp.where(lane_h < NA, x[0:half_m], x[half_m:members])

    y0 = fold(gr)

    def x_slot(e, d):
        return (d, xsend.at[e], xrecv.at[e, d], HOPS + 16 * e + d)

    def level_one(e, x, between=None):
        xsend[e] = x
        for d in (2, 3, 1, 0):
            start(*x_slot(e, d))
        own = times(x, wmat[0:cols])
        if between is not None:
            between()
        for d in range(4):
            arrive(*x_slot(e, d))
        every = jnp.concatenate([xrecv[e, d] for d in range(4)], axis=1)
        return own + times(every, wmat[cols : 5 * cols])

    def t_slot(e, d):
        slot = HOPS + 16 * e + 4 + d
        if d < 4:
            return d, tsend.at[e, OPP[d]], trecv.at[e, d], slot
        if d < 8:
            return d, csend.at[e, d - 4], crecv.at[e, d - 4], slot
        return d, tsend.at[e, OPP[d - 8], pl.ds(half_m, half_m)], srecv.at[e, d - 8], slot

    def two_sweeps(e, x, between=None):
        full = times_t(x, wmat[...])
        first = x + (y0 - full[:, 0:cols]) * weights
        out = [full[:, (n + 1) * cols : (n + 2) * cols] * nrecv[n] for n in range(4)]
        for n in range(4):
            tsend[e, n, 0:half_m] = first
            tsend[e, n, half_m : 2 * half_m] = out[n]
        for i, (v, h) in enumerate(CORNERS):
            csend[e, i, 0:half_m] = out[v]
            csend[e, i, half_m : 2 * half_m] = out[h]
        for d in (4, 5, 6, 7, 8, 9, 10, 11, 2, 3, 1, 0):
            start(*t_slot(e, d))
        if between is not None:
            between()
        for d in range(12):
            arrive(*t_slot(e, d))
        got = [trecv[e, d, half_m : 2 * half_m] for d in range(4)]
        tiles = [first - ((got[0] + got[1]) + (got[2] + got[3]))]
        for n in range(4):
            tiles.append(trecv[e, n, 0:half_m] - (out[n] + srecv[e, n]))
        for i, (v, h) in enumerate(CORNERS):
            tiles[1 + OPP[h]] = tiles[1 + OPP[h]] - crecv[e, i, 0:half_m]
            tiles[1 + OPP[v]] = tiles[1 + OPP[v]] - crecv[e, i, half_m : 2 * half_m]
        return tiles[0] + (y0 - times(jnp.concatenate(tiles, axis=1), wmat[...])) * weights

    for d in range(4):
        arrive(*near_ref(d))
    keep = {}

    def first_mats():
        for i in range(3):
            mat_copy(i).wait_recv()
        mat_1 = msend[0] + mrecv[0]
        mat_2 = squeeze(1, mat_1) + (mrecv[1] + mrecv[2])
        mat_3 = squeeze(2, mat_2)
        msend[2] = mat_3
        msend[3] = squeeze(3, mat_3)
        for i in range(3, 6):
            mat_copy(i).start()
        keep["mats"] = [mat_1, mat_2]

    def chains():
        smooth = [smoother(mat) for mat in keep["mats"]]
        for i in range(3, 6):
            mat_copy(i).wait_recv()
        mat_3 = msend[2] + mrecv[3]
        mat_4 = squeeze(3, mat_3) + (mrecv[4] + mrecv[5])
        smooth.append(smoother(mat_3))
        chain = qts[0][0:NA].astype(F32)
        for k in range(LEVELS):
            put(fmat, k, chain)
            if k + 1 < LEVELS:
                cube, pre = smooth[k]
                moved = apply_parts(cube, chain)
                put(gfin, k, apply_parts(pre, chain + moved))
                chain = hot_dot(qts[k + 1][0:NA, 0:NA], moved, NN)
        solve = jnp.where(lane_c < NA, mat_4, pltpu.roll(chain, NA, 1))
        keep["solve"] = [solve[k : k + GROUP] for k in range(0, NA, GROUP)]

    sub_g = lax.broadcasted_iota(jnp.int32, (GROUP, cols), 0)

    def lanes_of(v, k):
        return jnp.broadcast_to(v[:, k : k + 1], (GROUP, cols))

    def row_of(v, r):
        return jnp.broadcast_to(v[r : r + 1], (GROUP, cols))

    def pair_product(a, b):
        return [[a[i][0] * b[0][j] + a[i][1] * b[1][j] for j in range(2)] for i in range(2)]

    def pair_inverse(a):
        scale = 1.0 / (a[0][0] * a[1][1] - a[0][1] * a[1][0])
        return [[a[1][1] * scale, -a[0][1] * scale], [-a[1][0] * scale, a[0][0] * scale]]

    def quad_inverse(a):
        first = pair_inverse([a[i][0:2] for i in range(2)])
        right = pair_product(first, [a[i][2:4] for i in range(2)])
        below = [a[i][0:2] for i in range(2, 4)]
        moved = pair_product(below, right)
        second = pair_inverse([[a[2 + i][2 + j] - moved[i][j] for j in range(2)] for i in range(2)])
        down = pair_product(second, pair_product(below, first))
        back = pair_product(right, down)
        over = pair_product(right, second)
        return ([[first[i][j] + back[i][j] for j in range(2)] + [-over[i][j] for j in range(2)] for i in range(2)]
                + [[-down[i][j] for j in range(2)] + second[i] for i in range(2)])

    def eliminate(first, end):
        blocks = keep["solve"]
        for k in range(first, end, 4):
            q, r = k // GROUP, k % GROUP
            across = [[lanes_of(v, k + j) for v in blocks] for j in range(4)]
            inv = quad_inverse([[row_of(across[j][q], r + i) for j in range(4)] for i in range(4)])
            held = [row_of(blocks[q], r + i) for i in range(4)]
            pivots = [(inv[i][0] * held[0] + inv[i][1] * held[1]) + (inv[i][2] * held[2] + inv[i][3] * held[3])
                      for i in range(4)]
            blocks = [v - ((across[0][i] * pivots[0] + across[1][i] * pivots[1])
                           + (across[2][i] * pivots[2] + across[3][i] * pivots[3])) for i, v in enumerate(blocks)]
            for i in range(4):
                blocks[q] = jnp.where(sub_g == r + i, pivots[i], blocks[q])
        keep["solve"] = blocks

    x = two_sweeps(0, y0 * weights, first_mats)
    rem = y0 - level_one(0, x, lambda: (chains(), eliminate(0, NA // 2)))
    up = times_t(rem, fmat[...])
    for k in range(LEVELS):
        vsend[k] = up[:, k * cols : (k + 1) * cols]
    for j in reversed(range(1, 2 ** LEVELS)):
        vec_copy(j).start()
    eliminate(NA // 2, NA)
    put(gfin, LEVELS - 1, jnp.where(
        lane_c < NA, pltpu.roll(jnp.concatenate(keep["solve"], axis=0), NA, 1), 0.0))
    for j in range(1, 2 ** LEVELS):
        vec_copy(j).wait_recv()
    ys = []
    for k in range(LEVELS):
        y = vsend[k]
        for j in range(1, 2 ** (k + 1)):
            y = y + vrecv[j - 1, k]
        ys.append(y)
    x = two_sweeps(1, x + times(jnp.concatenate(ys, axis=1), gfin[...]))
    x = x + (y0 - level_one(1, x)) * weights

    whole = jnp.concatenate([x, pltpu.roll(x, NA, 1)], axis=0)
    whole_hi = whole.astype(BF16).astype(F32)
    lane_m = lax.broadcasted_iota(jnp.int32, (members, cols), 1)
    spread = jnp.where(lane_m < NA, whole_hi, pltpu.roll(whole - whole_hi, NA, 1)).astype(BF16)
    for r in range(rows):
        part = dg(spread, mo[:, r * cols : (r + 1) * cols], NN)
        u[:, r, :] = u[:, r, :] + part
    hsend[2] = pack_sides([u[m, 0:rows] for m in range(members)])
    pack_rows(2, u)
    for d in order:
        start(*again_ref(d))
    for d in range(8):
        arrive(*again_ref(d))
    fill_rows(2, u)
    h_east, h_west = sides(hrecv[1], hcorn[1])
    side = jnp.where(l8 < WIDE, h_east, h_west)
    for _ in range(SWEEPS):
        side = sweep(side, s_src)

    def out(m, v, rest):
        sol[m] = v
        res[m] = rest

    apply_field(side, rows, out)
    for d, source, target, slot in sent:
        @pl.when(has[d])
        def _():
            copy(source, target, slot, dev[d]).wait_send()

    for i in range(6):
        mat_copy(i).wait_send()
    for j in range(1, 2 ** LEVELS):
        vec_copy(j).wait_send()


def shards(n_row, n_col, source, guess, conductivity, storage, aggregates, pair_maps):
    members, rows, cols = source.shape
    cells = rows * cols
    ext = rows + GROUP
    vm = pl.BlockSpec(memory_space=pltpu.VMEM)
    half_m = members // 2
    mates = 2 ** LEVELS - 1
    slots = VECS + mates
    hbm = pl.BlockSpec(memory_space=pltpu.HBM)
    return pl.pallas_call(
        functools.partial(kernel, n_row, n_col),
        out_shape=(jax.ShapeDtypeStruct(source.shape, F32),) * 2,
        in_specs=[hbm] * 6,
        out_specs=(vm, vm),
        scratch_shapes=[
            pltpu.VMEM((members, ext, cols), F32),
            pltpu.VMEM((members, ext, cols), F32),
            pltpu.VMEM((members, rows, cols), F32),
            pltpu.VMEM((2 * NA, cells), BF16),
            pltpu.VMEM((3 * NA, cells), BF16),
            pltpu.VMEM((2 * members, cells), BF16),
            pltpu.VMEM((cols, cols), F32),
            pltpu.VMEM((rows, cols), F32),
            pltpu.VMEM((2, rows, cols), F32),
            pltpu.VMEM((4, GROUP, cols), F32),
            pltpu.VMEM((2, 2 * GROUP, cols), F32),
            pltpu.VMEM((2, 2 * GROUP, cols), F32),
            pltpu.VMEM((3, rows, cols), F32),
            pltpu.VMEM((2, 2, rows, cols), F32),
            pltpu.VMEM((2, 4, GROUP, cols), F32),
            pltpu.VMEM((3, 2, WIDE * members, cols), F32),
            pltpu.VMEM((3, 2, WIDE * members, cols), F32),
            pltpu.VMEM((NX0, half_m, cols), F32),
            pltpu.VMEM((NX0, 4, half_m, cols), F32),
            pltpu.VMEM((half_m, cols), F32),
            pltpu.VMEM((4, half_m, cols), F32),
            pltpu.VMEM((NX0, 4, 2 * half_m, cols), F32),
            pltpu.VMEM((NX0, 4, 2 * half_m, cols), F32),
            pltpu.VMEM((NX0, 4, 2 * half_m, cols), F32),
            pltpu.VMEM((NX0, 4, 2 * half_m, cols), F32),
            pltpu.VMEM((NX0, 4, half_m, cols), F32),
            pltpu.VMEM((LEVELS, NA, cols), F32),
            pltpu.VMEM((6, NA, cols), F32),
            pltpu.VMEM((LEVELS, half_m, cols), F32),
            pltpu.VMEM((mates, LEVELS, half_m, cols), F32),
            pltpu.VMEM((5 * cols, 2 * cols), BF16),
            pltpu.VMEM((LEVELS * cols, 2 * cols), BF16),
            pltpu.VMEM((LEVELS * cols, 2 * cols), BF16),
            pltpu.VMEM((LEVELS, cols, cols), BF16),
            pltpu.VMEM((rows, cols), F32),
            pltpu.VMEM((rows, cols), F32),
            pltpu.VMEM((rows, cols), jnp.int32),
            pltpu.VMEM((LEVELS, cols), jnp.int32),
            pltpu.SemaphoreType.DMA((slots,)),
            pltpu.SemaphoreType.DMA((slots,)),
            pltpu.SemaphoreType.DMA((6,)),
        ],
        compiler_params=pltpu.CompilerParams(collective_id=0, has_side_effects=True, vmem_limit_bytes=VMEM_LIMIT),
    )(*(pltpu.with_memory_space_constraint(a, pltpu.HBM) for a in (
        source, guess, conductivity, storage, aggregates, pair_maps.reshape(LEVELS, -1))))


def solution(mesh):
    placed = (
        P(None, "row", "col"),
        P(None, "row", "col"),
        P("row", "col"),
        P("row", "col"),
        P("row", "col"),
        P(None, "row", "col", None),
    )
    return jax.shard_map(
        functools.partial(shards, mesh.shape["row"], mesh.shape["col"]),
        mesh=mesh,
        in_specs=placed,
        out_specs=(P(None, "row", "col"), P(None, "row", "col")),
        check_vma=False,
    )
```

```python
import functools

import jax
import jax.numpy as jnp
from jax import lax
from jax.experimental import pallas as pl
from jax.experimental.pallas import tpu as pltpu
from jax.sharding import PartitionSpec as P

NA = 64
SWEEPS = 3
LEVELS = 4
OMEGA_FINE = 0.8
OMEGA_COARSE = 0.6
F32 = jnp.float32
BF16 = jnp.bfloat16
MESH = pl.DeviceIdType.MESH
OPP = (1, 0, 3, 2, 7, 6, 5, 4, 9, 8, 11, 10)
WIDE = SWEEPS + 1
GROUP = 2 * WIDE
HOPS = 28
NEAR = HOPS + 32
MATS = NEAR + 4
VECS = MATS + 6
OUTS = VECS + 2 ** LEVELS - 1
SPLIT = 32
NX0 = 2
CORNERS = ((1, 3), (1, 2), (0, 3), (0, 2))
VMEM_LIMIT = 24 * 1024 * 1024
NN = (((1,), (0,)), ((), ()))
NT = (((1,), (1,)), ((), ()))


def dg(a, b, dims):
    return lax.dot_general(a, b, dims, preferred_element_type=F32)


def split2(x):
    hi = x.astype(BF16)
    return hi, (x - hi.astype(F32)).astype(BF16)


def split3(x):
    hi = x.astype(BF16)
    rest = x - hi.astype(F32)
    mid = rest.astype(BF16)
    return hi, mid, (rest - mid.astype(F32)).astype(BF16)


def stacked(x):
    hi = x.astype(BF16).astype(F32)
    return jnp.concatenate([hi, x - hi], axis=0).astype(BF16)


def times(x, weights):
    n, wide = x.shape[0], weights.shape[1] // 2
    full = dg(stacked(x), weights, NN)
    return full[0:n, 0:wide] + (full[n:, 0:wide] + full[0:n, wide:])


def times_t(x, weights):
    n = x.shape[0]
    both = stacked(x)
    full = dg(jnp.concatenate([both, both], axis=1), weights, NT)
    return full[0:n] + full[n:]


def dot_hot(x, hot, dims):
    n = x.shape[0]
    hi = x.astype(BF16).astype(F32)
    mid = (x - hi).astype(BF16).astype(F32)
    full = dg(jnp.concatenate([hi, mid, x - hi - mid], axis=0).astype(BF16), hot, dims)
    return full[0:n] + (full[n : 2 * n] + full[2 * n :])


def hot_dot(hot, x, dims):
    hi, mid, lo = split3(x)
    return dg(hot, hi, dims) + (dg(hot, mid, dims) + dg(hot, lo, dims))


def kernel(n_row, n_col, src_in, guess_in, cond_in, sto_in, agg_in, pm_in, result,
           u, se, left, mo, gmat, rlhs, xt, ksend, krecv, kcorn, krsend, krrecv, hsend, hrecv, hcorn, rowbuf,
           rsend, xsend, xrecv, nsend, nrecv, tsend, trecv, csend, crecv, srecv, msend, mrecv, hsum, hrest, held, solve, osend, orecv, vsend, vrecv, wmat, fmat, gfin, qts,
           cond, sto, agg, pm, ssem, rsem, lsem):
    members, rows, cols = guess_in.shape
    half_m = members // 2
    ext = rows + GROUP
    row = lax.axis_index("row")
    col = lax.axis_index("col")
    has = [row > 0, row < n_row - 1, col > 0, col < n_col - 1]
    dev = [(row - 1, col), (row + 1, col), (row, col - 1), (row, col + 1)]
    for v in (0, 1):
        for h in (2, 3):
            has.append(jnp.logical_and(has[v], has[h]))
            dev.append((dev[v][0], dev[h][1]))
    far_has = [row > 1, row < n_row - 2, col > 1, col < n_col - 2]
    far_dev = [(row - 2, col), (row + 2, col), (row, col - 2), (row, col + 2)]
    has += far_has
    dev += far_dev
    col_bit = col % 2
    row_bit = row % 2
    col_bit2 = col // 2 % 2
    row_bit2 = row // 2 % 2
    upper = (col_bit, row_bit, col_bit2, row_bit2)
    flip_col = (0, 1 - 2 * col_bit, 2 - 4 * col_bit2, 3 - 2 * col_bit - 4 * col_bit2)
    flip_row = (0, 1 - 2 * row_bit, 2 - 4 * row_bit2, 3 - 2 * row_bit - 4 * row_bit2)

    def mate(j):
        return (row + flip_row[j // 2 % 2 + 2 * (j // 8)], col + flip_col[j % 2 + 2 * (j // 4 % 2)])

    loads = [
        pltpu.make_async_copy(source, target, lsem.at[i])
        for i, (source, target) in enumerate((
            (guess_in, u.at[:, pl.ds(0, rows)]), (src_in, se.at[:, pl.ds(0, rows)]),
            (cond_in, cond), (agg_in, agg), (sto_in, sto), (pm_in, pm)))
    ]
    for load in loads:
        load.start()

    barrier = pltpu.get_barrier_semaphore()
    count = jnp.int32(0)
    for d in range(8):
        count = count + has[d].astype(jnp.int32)

        @pl.when(has[d])
        def _():
            pl.semaphore_signal(barrier, inc=1, device_id=dev[d], device_id_type=MESH)

    def copy(source, target, slot, device):
        return pltpu.make_async_remote_copy(
            src_ref=source, dst_ref=target, send_sem=ssem.at[slot], recv_sem=rsem.at[slot],
            device_id=device, device_id_type=MESH)

    sent = []

    def start(d, source, target, slot):
        @pl.when(has[d])
        def _():
            copy(source, target, slot, dev[d]).start()

        sent.append((d, source, target, slot))

    def arrive(d, source, target, slot):
        @pl.when(has[OPP[d]])
        def _():
            copy(source, target, slot, dev[d]).wait_recv()

    for d in range(12):
        @pl.when(jnp.logical_not(has[OPP[d]]))
        def _():
            if d < 2:
                krrecv[d] = jnp.ones((2 * GROUP, cols), F32)
                for p in range(3):
                    rowbuf[p, d] = jnp.zeros((WIDE * members, cols), F32)
            elif d < 4:
                krecv[d - 2] = jnp.ones((rows, cols), F32)
                for p in range(2):
                    hrecv[p, d - 2] = jnp.zeros((rows, cols), F32)
            elif d < 8:
                kcorn[d - 4] = jnp.ones((GROUP, cols), F32)
                for p in range(2):
                    hcorn[p, d - 4] = jnp.zeros((GROUP, cols), F32)
            for e in range(NX0):
                if d < 4:
                    xrecv[e, d] = jnp.zeros((half_m, cols), F32)
                    trecv[e, d] = jnp.zeros((2 * half_m, cols), F32)
                elif d < 8:
                    crecv[e, d - 4] = jnp.zeros((2 * half_m, cols), F32)
                else:
                    srecv[e, d - 8] = jnp.zeros((half_m, cols), F32)
            if d < 4:
                nrecv[d] = jnp.zeros((half_m, cols), F32)

    lane = lax.broadcasted_iota(jnp.int32, (ext, cols), 1)
    sub = lax.broadcasted_iota(jnp.int32, (ext, cols), 0)
    l8 = lane % GROUP
    owner = lane // GROUP
    lane8 = lane[0:GROUP]
    sub8 = sub[0:GROUP]

    def mirror(x):
        where = lax.broadcasted_iota(jnp.int32, x.shape, 1)
        bit = 1
        while bit < GROUP:
            x = jnp.where(where // bit % 2 == 0, pltpu.roll(x, cols - bit, 1), pltpu.roll(x, bit, 1))
            bit *= 2
        return x

    def repeat(x):
        width = GROUP
        while width < cols:
            x = x + pltpu.roll(x, width, 1)
            width *= 2
        return x

    def side_ref(source, target, corners, d, slot):
        if d < 4:
            return d, source, target.at[d - 2], slot + d
        return d, source.at[pl.ds(0 if d < 6 else rows - GROUP, GROUP)], corners.at[d - 4], slot + d

    def row_ref(p, d):
        return d, rsend.at[p, d], rowbuf.at[p, d], 16 + 2 * p + d

    def field_ref(d):
        return side_ref(hsend.at[0 if d % 2 == 0 else 1], hrecv.at[0], hcorn.at[0], d, 8)

    def again_ref(d):
        if d < 2:
            return row_ref(2, d)
        return side_ref(hsend.at[2], hrecv.at[1], hcorn.at[1], d, 20)

    def coef_ref(d):
        if d < 2:
            return d, krsend.at[d], krrecv.at[d], d
        return side_ref(ksend, krecv, kcorn, d, 0)

    def pack_sides(fields):
        packed = jnp.zeros((rows, cols), F32)
        for m, v in enumerate(fields):
            packed = jnp.where(owner[0:rows] == m, pltpu.roll(v, (GROUP * m + WIDE) % cols, 1), packed)
        return mirror(packed)

    def pack_rows(p, field):
        for m in range(members):
            rsend[p, 0, WIDE * m : WIDE * (m + 1), :] = field[m, 0:WIDE]
            rsend[p, 1, WIDE * m : WIDE * (m + 1), :] = field[m, rows - WIDE : rows]

    order = (2, 3, 1, 0, 4, 5, 6, 7)

    def under(south, north):
        return jnp.where(sub8 < WIDE, south, north)

    def fill_rows(p, field):
        for m in range(members):
            field[m, rows : rows + WIDE, :] = rowbuf[p, 0, WIDE * m : WIDE * (m + 1), :]
            field[m, rows + WIDE : ext, :] = rowbuf[p, 1, WIDE * m : WIDE * (m + 1), :]

    def sides(planes, corners):
        return (jnp.concatenate([planes[0], under(corners[0], corners[2])], axis=0),
                jnp.concatenate([planes[1], under(corners[1], corners[3])], axis=0))

    for load in loads:
        load.wait()
    agg_v = agg[...]
    sub64 = lax.broadcasted_iota(jnp.int32, (NA, cols), 0)
    for r in range(rows):
        hot = jnp.where(sub64 == agg_v[r : r + 1], 1.0, 0.0).astype(BF16)
        mo[0:NA, r * cols : (r + 1) * cols] = hot
        mo[NA : 2 * NA, r * cols : (r + 1) * cols] = hot
    xt[...] = jnp.zeros(xt.shape, F32)
    iota128 = lax.broadcasted_iota(jnp.int32, (cols, cols), 0)
    lane128 = lax.broadcasted_iota(jnp.int32, (cols, cols), 1)
    for k in range(LEVELS):
        pmk = pm[k : k + 1, :]
        pmk = jnp.where(upper[k] == 1, pltpu.roll(pmk, NA, 1), pmk)
        qts[k] = jnp.where(jnp.logical_and(iota128 == pmk, lane128 < NA), 1.0, 0.0).astype(BF16)

    def face(a, b):
        return 2.0 * (a * b) / (a + b)

    last = rows - 1
    c = cond[...]
    in_east = jnp.where(lane[0:rows] < cols - 1, face(c, pltpu.roll(c, cols - 1, 1)), 0.0)
    in_south = jnp.where(sub[0:rows] < last, face(c, pltpu.roll(c, last, 0)), 0.0)
    right = pltpu.roll(agg_v, cols - 1, 1)
    below = pltpu.roll(agg_v, last, 0)
    half = 0.5 * (sto[...] + in_east + pltpu.roll(in_east, 1, 1) + in_south + pltpu.roll(in_south, 1, 0))
    for r in range(rows):
        s = slice(r, r + 1)
        g = (jnp.where(sub64 == right[s], in_east[s], 0.0)
             + jnp.where(sub64 == below[s], in_south[s], 0.0)
             - jnp.where(sub64 == agg_v[s], half[s], 0.0))
        for i, part in enumerate(split3(g)):
            gmat[i * NA : (i + 1) * NA, r * cols : (r + 1) * cols] = part
    gx = dg(gmat[...], mo[0:NA], NT)
    xt[0:NA, 0:NA] = gx[0:NA] + (gx[NA : 2 * NA] + gx[2 * NA : 3 * NA])
    xfull = xt[...]
    inner = -(xfull + xfull.T)[0:NA]

    lane_c = lax.broadcasted_iota(jnp.int32, (NA, cols), 1)
    lane_1 = lax.broadcasted_iota(jnp.int32, (1, cols), 1)
    eye = jnp.where(lane_c == sub64, 1.0, 0.0)

    def squeeze(mat, pair):
        right = dot_hot(mat[:, 0:NA], pair, NT)
        full = hot_dot(pair, right, NN)
        both = jnp.where(lane_c < NA, full[0:NA], full[NA : 2 * NA])
        half = jnp.where(lane_c[0 : NA // 2] < NA, pltpu.roll(both[0 : NA // 2], NA, 1), both[NA // 2 : NA])
        return both, half

    def lower(both):
        return jnp.where(lane_c < NA, both, 0.0)

    def higher(both, halves):
        halves = jnp.concatenate([halves, pltpu.roll(halves, NA, 1)], axis=0)
        return jnp.where(lane_c < NA, pltpu.roll(both, NA, 1) + halves, 0.0)

    hots = [qts[k][0:NA, 0:NA] for k in range(LEVELS)]

    def onward(a, b):
        return dg(a, b, NN).astype(BF16)

    pair_12 = jnp.concatenate([hots[0], onward(hots[1], hots[0])], axis=0)
    pair_34 = jnp.concatenate([hots[2], onward(hots[3], hots[2])], axis=0)
    pair_all = jnp.concatenate([pair_12, onward(pair_34, pair_12[NA : 2 * NA])], axis=0)
    msend[0], hsum[0] = squeeze(inner, pair_12)

    aggf = agg[...].astype(F32)
    ksend[...] = pack_sides([cond[...], sto[...], aggf])
    for d, near, wide in ((0, 0, 0), (1, rows - WIDE, rows - GROUP)):
        krsend[d, 0:WIDE] = cond[near : near + WIDE]
        krsend[d, WIDE:GROUP] = sto[near : near + WIDE]
        krsend[d, GROUP : 2 * GROUP] = aggf[wide : wide + GROUP]
    side_g = pack_sides([u[m, 0:rows] for m in range(members)])
    side_f = pack_sides([se[m, 0:rows] for m in range(members)])
    inward = l8[0:rows] < WIDE
    hsend[0] = jnp.where(inward, side_g, pltpu.roll(side_f, WIDE, 1))
    hsend[1] = jnp.where(inward, pltpu.roll(side_g, cols - WIDE, 1), side_f)
    pack_rows(0, u)
    pack_rows(1, se)
    pl.semaphore_wait(barrier, count)
    def mat_copy(i):
        at = i // 3
        mates = mate((1, 2, 3, 4, 8, 12)[i])
        if i % 3 == 0:
            return copy(msend.at[at], mrecv.at[at], MATS + i, mates)
        return copy(hsum.at[at], hrest.at[2 * at + i % 3 - 1], MATS + i, mates)

    for d in order:
        start(*coef_ref(d))
    for d in (2, 3):
        start(*field_ref(d))
    for p in range(2):
        for d in (1, 0):
            start(*row_ref(p, d))
    for d in range(4, 8):
        start(*field_ref(d))
    for i in range(3):
        mat_copy(i).start()

    for d in range(8):
        arrive(*coef_ref(d))

    k_east, k_west = sides(krecv, kcorn)
    k_side = jnp.where(l8 < WIDE, k_east, k_west)

    def extend(value, at):
        main = jnp.concatenate([value[...]] + [krrecv[d, at * WIDE : (at + 1) * WIDE] for d in range(2)], axis=0)
        return main, repeat(jnp.where(lane < GROUP, pltpu.roll(k_side, (cols - at * GROUP) % cols, 1), 0.0))

    cm, cs = extend(cond, 0)
    sm, ss = extend(sto, 1)
    hasi = [h.astype(jnp.int32) for h in has[0:4]]

    def vertical(x):
        down = jnp.where(jnp.logical_and(sub == last, hasi[1] == 0), 0.0, face(x, pltpu.roll(x, ext - 1, 0)))
        up = jnp.where(jnp.logical_and(sub == 0, hasi[0] == 0), 0.0, face(x, pltpu.roll(x, 1, 0)))
        return down, up

    side_at = pltpu.roll(cs, cols - WIDE, 1)
    rim = jnp.logical_and(lane >= WIDE - 1, lane <= WIDE)
    main_at = repeat(jnp.where(rim, pltpu.roll(cm, WIDE, 1), 0.0))
    east = face(cm, jnp.where(lane == cols - 1, side_at, pltpu.roll(cm, cols - 1, 1)))
    west = face(cm, jnp.where(lane == 0, side_at, pltpu.roll(cm, 1, 1)))
    east = jnp.where(lane < cols - 1 + hasi[3], east, 0.0)
    west = jnp.where(lane >= 1 - hasi[2], west, 0.0)
    south, north = vertical(cm)
    diag = sm + east + west + south + north
    step = OMEGA_FINE / diag
    s_west = face(cs, jnp.where(l8 == WIDE - 1, main_at, pltpu.roll(cs, cols - 1, 1)))
    s_east = face(cs, jnp.where(l8 == WIDE, main_at, pltpu.roll(cs, 1, 1)))
    s_west = jnp.where(jnp.logical_and(l8 == WIDE - 1, hasi[3] == 0), 0.0, s_west)
    s_east = jnp.where(jnp.logical_and(l8 == WIDE, hasi[2] == 0), 0.0, s_east)
    s_south, s_north = vertical(cs)
    s_diag = ss + s_east + s_west + s_south + s_north
    s_step = OMEGA_FINE / s_diag

    def apply_field(side, n, finish):
        lane_n = lane[0:n]
        edge = jnp.zeros((ext, cols), F32)
        for m in range(members):
            v = u[m]
            hm = pltpu.roll(side, (2 * cols - GROUP * m - WIDE) % cols, 1)[0:n]
            vn = v[0:n]
            from_w = jnp.where(lane_n == 0, hm, pltpu.roll(vn, 1, 1))
            from_e = jnp.where(lane_n == cols - 1, hm, pltpu.roll(vn, cols - 1, 1))
            from_s = pltpu.roll(v, ext - 1, 0)[0:n]
            from_n = pltpu.roll(v, 1, 0)[0:n]
            rest = se[m, 0:n] - (diag[0:n] * vn - (
                east[0:n] * from_e + west[0:n] * from_w + south[0:n] * from_s + north[0:n] * from_n))
            if n == ext:
                edge = jnp.where(owner == m, pltpu.roll(v, (GROUP * m + WIDE) % cols, 1), edge)
            finish(m, vn, rest)
        return edge

    def sweep(side, s_src):
        def finish(m, v, rest):
            u[m] = v + step * rest

        edge = apply_field(side, ext, finish)
        from_w = jnp.where(l8 == WIDE - 1, edge, pltpu.roll(side, cols - 1, 1))
        from_e = jnp.where(l8 == WIDE, edge, pltpu.roll(side, 1, 1))
        rest = s_src - (s_diag * side - (s_east * from_e + s_west * from_w
                        + s_south * pltpu.roll(side, ext - 1, 0) + s_north * pltpu.roll(side, 1, 0)))
        return side + s_step * rest


    agg_t = agg_v.astype(F32).T.astype(jnp.int32)

    def put(ref, slot, block):
        both = jnp.concatenate([block, pltpu.roll(block, NA, 1)], axis=0)
        hi, lo = split2(both)
        ref[slot * cols : (slot + 1) * cols, 0:cols] = hi
        ref[slot * cols : (slot + 1) * cols, cols : 2 * cols] = lo

    def couple(slot, own_ids, other_ids, faces, width):
        own = jnp.where(lax.broadcasted_iota(jnp.int32, (cols, width), 0) == own_ids, 1.0, 0.0).astype(BF16)
        other = jnp.where(lax.broadcasted_iota(jnp.int32, (NA, width), 0) == other_ids, faces, 0.0)
        links = dot_hot(other, own, NT)
        put(wmat, slot, -links)
        return jnp.sum(links, axis=0, keepdims=True)

    row_ids = [krrecv[d].astype(jnp.int32) for d in range(2)]
    outer = couple(1, agg_v[last:rows], row_ids[0][GROUP : GROUP + 1], south[last:rows], cols)
    outer = outer + couple(2, agg_v[0:1], row_ids[1][2 * GROUP - 1 : 2 * GROUP], north[0:1], cols)
    k_ids = k_side[0:rows].T.astype(jnp.int32)
    near_e = 2 * GROUP + WIDE - 1
    outer = outer + couple(3, agg_t[cols - 1 : cols], k_ids[near_e : near_e + 1], east[0:rows].T[cols - 1 : cols], rows)
    outer = outer + couple(4, agg_t[0:1], k_ids[near_e + 1 : near_e + 2], west[0:rows].T[0:1], rows)

    def vec_copy(j):
        return copy(vsend.at[j.bit_length() - 1], vrecv.at[j - 1], VECS + j - 1, mate(j))

    def out_copy(i):
        return copy(osend.at[i // 3], orecv.at[i], OUTS + i, mate((1, 2, 3, 4, 8, 12)[i]))

    def weight(mat):
        d = jnp.sum(jnp.where(lane_c == sub64, mat, 0.0), axis=0, keepdims=True)
        ok = lane_1 < NA
        return jnp.where(ok, OMEGA_COARSE / jnp.where(ok, d, 1.0), 0.0)

    def parted(b):
        hi = b.astype(BF16).astype(F32)
        return jnp.where(lane_c < NA, hi, pltpu.roll(b - hi, NA, 1)).astype(BF16)

    def product(a, b):
        full = dg(stacked(a[:, 0:NA]), b, NN)
        part = full[0:NA] + jnp.where(lane_c < NA, full[NA : 2 * NA], 0.0)
        return jnp.where(lane_c < NA, part + pltpu.roll(part, NA, 1), 0.0)

    def smoother(mat):
        side_w = OMEGA_COARSE / jnp.sum(eye * mat, axis=1, keepdims=True)
        one = eye - mat * weight(mat)
        parts = parted(one)
        two = product(one, parts)
        return product(two, parts), side_w * (eye + one + two)

    block = inner + jnp.where(lane_c == sub64, outer, 0.0)
    outers = dot_hot(jnp.broadcast_to(outer[:, 0:NA], (GROUP, NA)), pair_all, NT)
    outers = [outers[:, 0:cols], outers[:, cols : 2 * cols]]
    level = jnp.zeros((GROUP, cols), F32)
    for k in range(LEVELS):
        level = jnp.where(sub8 == k, pltpu.roll(outers[k // 2], NA, 1) if k % 2 else outers[k // 2], level)
    osend[0] = jnp.where(lane8 < NA, level, 0.0)
    for i in range(3):
        out_copy(i).start()
    put(wmat, 0, block)
    weights = weight(block)
    weights = jnp.broadcast_to(weights + pltpu.roll(weights, NA, 1), (half_m, cols))
    nsend[...] = weights

    def near_ref(d):
        return d, nsend, nrecv.at[d], NEAR + d

    for d in (2, 3, 1, 0):
        start(*near_ref(d))

    for d in range(2, 8):
        arrive(*field_ref(d))
    for p in range(2):
        for d in range(2):
            arrive(*row_ref(p, d))
    fill_rows(0, u)
    fill_rows(1, se)
    h_east, h_west = sides(hrecv[0], hcorn[0])
    side = jnp.where(l8 < WIDE, h_east, pltpu.roll(h_west, WIDE, 1))
    s_src = jnp.where(l8 < WIDE, pltpu.roll(h_east, cols - WIDE, 1), h_west)
    for _ in range(SWEEPS):
        side = sweep(side, s_src)

    def keep_left(m, v, rest):
        left[m] = rest

    apply_field(side, rows, keep_left)
    for r in range(rows):
        for i, part in enumerate(split2(left[:, r, :])):
            rlhs[i * members : (i + 1) * members, r * cols : (r + 1) * cols] = part
    gr = dg(rlhs[...], mo[...], NT)
    gr = gr[0:members] + gr[members : 2 * members]
    lane_h = lax.broadcasted_iota(jnp.int32, (half_m, cols), 1)

    def fold(x):
        return jnp.where(lane_h < NA, x[0:half_m], x[half_m:members])

    y0 = fold(gr)

    def x_slot(e, d):
        return (d, xsend.at[e], xrecv.at[e, d], HOPS + 16 * e + d)

    def level_one(e, x, between=None):
        xsend[e] = x
        for d in (2, 3, 1, 0):
            start(*x_slot(e, d))
        own = times(x, wmat[0:cols])
        if between is not None:
            between()
        for d in range(4):
            arrive(*x_slot(e, d))
        every = jnp.concatenate([xrecv[e, d] for d in range(4)], axis=1)
        return own + times(every, wmat[cols : 5 * cols])

    def t_slot(e, d):
        slot = HOPS + 16 * e + 4 + d
        if d < 4:
            return d, tsend.at[e, OPP[d]], trecv.at[e, d], slot
        if d < 8:
            return d, csend.at[e, d - 4], crecv.at[e, d - 4], slot
        return d, tsend.at[e, OPP[d - 8], pl.ds(half_m, half_m)], srecv.at[e, d - 8], slot

    def two_sweeps(e, x, between=None):
        full = times_t(x, wmat[...])
        first = x + (y0 - full[:, 0:cols]) * weights
        out = [full[:, (n + 1) * cols : (n + 2) * cols] * nrecv[n] for n in range(4)]
        for n in range(4):
            tsend[e, n, 0:half_m] = first
            tsend[e, n, half_m : 2 * half_m] = out[n]
        for i, (v, h) in enumerate(CORNERS):
            csend[e, i, 0:half_m] = out[v]
            csend[e, i, half_m : 2 * half_m] = out[h]
        for d in (4, 5, 6, 7, 8, 9, 10, 11, 2, 3, 1, 0):
            start(*t_slot(e, d))
        if between is not None:
            between()
        for d in range(12):
            arrive(*t_slot(e, d))
        got = [trecv[e, d, half_m : 2 * half_m] for d in range(4)]
        tiles = [first - ((got[0] + got[1]) + (got[2] + got[3]))]
        for n in range(4):
            tiles.append(trecv[e, n, 0:half_m] - (out[n] + srecv[e, n]))
        for i, (v, h) in enumerate(CORNERS):
            tiles[1 + OPP[h]] = tiles[1 + OPP[h]] - crecv[e, i, 0:half_m]
            tiles[1 + OPP[v]] = tiles[1 + OPP[v]] - crecv[e, i, half_m : 2 * half_m]
        return tiles[0] + (y0 - times(jnp.concatenate(tiles, axis=1), wmat[...])) * weights

    for i in range(3):
        mat_copy(i).wait_recv()
    mat_1 = msend[0] + mrecv[0]
    mat_2 = higher(mat_1, hrest[0] + hrest[1])
    mat_1 = lower(mat_1)
    msend[1], hsum[1] = squeeze(mat_2, pair_34)
    for i in range(3, 6):
        mat_copy(i).start()
    for i in range(3):
        out_copy(i).wait_recv()
    outer_1 = osend[0] + orecv[0]
    osend[1] = outer_1 + jnp.where(sub8 > 0, orecv[1] + orecv[2], 0.0)
    for i in range(3, 6):
        out_copy(i).start()
    for d in range(4):
        arrive(*near_ref(d))
    def chains():
        chain = hots[0].astype(F32)
        chain = jnp.concatenate([chain, jnp.zeros((NA, cols - NA), F32)], axis=1)
        put(fmat, 0, chain)
        for k in range(LEVELS - 1):
            if k == 0:
                mat = mat_1 + eye * outer_1[0:1]
            elif k == 1:
                mat = mat_2 + eye * osend[1, 1:2]
            else:
                for i in range(3, 6):
                    mat_copy(i).wait_recv()
                for i in range(3, 6):
                    out_copy(i).wait_recv()
                sums = osend[1] + orecv[3]
                both = msend[1] + mrecv[1]
                mat = lower(both) + eye * sums[2:3]
            cube, pre = smoother(mat)
            moved = product(cube, parted(chain))
            held[k, 0] = cube
            held[k, 1] = pre
            held[k, 2] = chain + moved
            chain = hot_dot(hots[k + 1], moved, NN)
            put(fmat, k + 1, chain)
        sums = sums + (orecv[4] + orecv[5])
        mat = higher(both, hrest[2] + hrest[3]) + eye * sums[3:4]
        solve[...] = jnp.where(lane_c < NA, mat, pltpu.roll(chain, NA, 1))

    sub_g = lax.broadcasted_iota(jnp.int32, (GROUP, cols), 0)

    def lanes_of(v, k):
        return jnp.broadcast_to(v[:, k : k + 1], (GROUP, cols))

    def row_of(v, r):
        return jnp.broadcast_to(v[r : r + 1], (GROUP, cols))

    def pair_product(a, b):
        return [[a[i][0] * b[0][j] + a[i][1] * b[1][j] for j in range(2)] for i in range(2)]

    def pair_inverse(a):
        scale = 1.0 / (a[0][0] * a[1][1] - a[0][1] * a[1][0])
        return [[a[1][1] * scale, -a[0][1] * scale], [-a[1][0] * scale, a[0][0] * scale]]

    def quad_inverse(a):
        first = pair_inverse([a[i][0:2] for i in range(2)])
        right = pair_product(first, [a[i][2:4] for i in range(2)])
        below = [a[i][0:2] for i in range(2, 4)]
        moved = pair_product(below, right)
        second = pair_inverse([[a[2 + i][2 + j] - moved[i][j] for j in range(2)] for i in range(2)])
        down = pair_product(second, pair_product(below, first))
        back = pair_product(right, down)
        over = pair_product(right, second)
        return ([[first[i][j] + back[i][j] for j in range(2)] + [-over[i][j] for j in range(2)] for i in range(2)]
                + [[-down[i][j] for j in range(2)] + second[i] for i in range(2)])

    def eliminate(first, end):
        blocks = [solve[k : k + GROUP] for k in range(0, NA, GROUP)]
        for k in range(first, end, 4):
            q, r = k // GROUP, k % GROUP
            across = [[lanes_of(v, k + j) for v in blocks] for j in range(4)]
            inv = quad_inverse([[row_of(across[j][q], r + i) for j in range(4)] for i in range(4)])
            lines = [row_of(blocks[q], r + i) for i in range(4)]
            pivots = [(inv[i][0] * lines[0] + inv[i][1] * lines[1]) + (inv[i][2] * lines[2] + inv[i][3] * lines[3])
                      for i in range(4)]
            blocks = [v - ((across[0][i] * pivots[0] + across[1][i] * pivots[1])
                           + (across[2][i] * pivots[2] + across[3][i] * pivots[3])) for i, v in enumerate(blocks)]
            for i in range(4):
                blocks[q] = jnp.where(sub_g == r + i, pivots[i], blocks[q])
        for i, v in enumerate(blocks):
            solve[GROUP * i : GROUP * (i + 1)] = v

    x = two_sweeps(0, y0 * weights, chains)
    rem = y0 - level_one(0, x, lambda: eliminate(0, SPLIT))
    up = times_t(rem, fmat[...])
    for k in range(LEVELS):
        vsend[k] = up[:, k * cols : (k + 1) * cols]
    for j in reversed(range(1, 2 ** LEVELS)):
        vec_copy(j).start()
    partial, back = [], []
    for k in range(LEVELS - 1):
        partial.append(product(held[k, 1], parted(held[k, 2])))
        onto = hot_dot(hots[k + 1], held[k, 0], NN)
        back.append(jnp.concatenate([onto, jnp.zeros((cols - NA, cols), F32)], axis=0).T[0:NA])
    eliminate(SPLIT, NA)
    final = jnp.where(lane_c < NA, pltpu.roll(solve[...], NA, 1), 0.0)
    put(gfin, LEVELS - 1, final)
    for k in reversed(range(LEVELS - 1)):
        final = partial[k] + product(back[k], parted(final))
        put(gfin, k, final)
    for j in range(1, 2 ** LEVELS):
        vec_copy(j).wait_recv()
    ys = []
    for k in range(LEVELS):
        y = [vrecv[j - 1] for j in range(2 ** k, 2 ** (k + 1))]
        y = y + [vsend[0]] if k == 0 else y
        while len(y) > 1:
            y = [a + b for a, b in zip(y[::2], y[1::2])]
        ys.append(y[0])
    x = two_sweeps(1, x + times(jnp.concatenate(ys, axis=1), gfin[...]))
    x = x + (y0 - level_one(1, x)) * weights

    whole = jnp.concatenate([x, pltpu.roll(x, NA, 1)], axis=0)
    whole_hi = whole.astype(BF16).astype(F32)
    lane_m = lax.broadcasted_iota(jnp.int32, (members, cols), 1)
    spread = jnp.where(lane_m < NA, whole_hi, pltpu.roll(whole - whole_hi, NA, 1)).astype(BF16)
    for r in range(rows):
        part = dg(spread, mo[:, r * cols : (r + 1) * cols], NN)
        u[:, r, :] = u[:, r, :] + part
    hsend[2] = pack_sides([u[m, 0:rows] for m in range(members)])
    pack_rows(2, u)
    for d in order:
        start(*again_ref(d))
    for d in range(8):
        arrive(*again_ref(d))
    fill_rows(2, u)
    h_east, h_west = sides(hrecv[1], hcorn[1])
    side = jnp.where(l8 < WIDE, h_east, h_west)
    for _ in range(SWEEPS):
        side = sweep(side, s_src)

    def out(m, v, rest):
        result[0, m] = v
        result[1, m] = rest

    apply_field(side, rows, out)
    for d, source, target, slot in sent:
        @pl.when(has[d])
        def _():
            copy(source, target, slot, dev[d]).wait_send()

    for i in range(6):
        mat_copy(i).wait_send()
        out_copy(i).wait_send()
    for j in range(1, 2 ** LEVELS):
        vec_copy(j).wait_send()


def shards(n_row, n_col, source, guess, conductivity, storage, aggregates, pair_maps):
    members, rows, cols = source.shape
    cells = rows * cols
    ext = rows + GROUP
    vm = pl.BlockSpec(memory_space=pltpu.VMEM)
    half_m = members // 2
    mates = 2 ** LEVELS - 1
    slots = OUTS + 6
    hbm = pl.BlockSpec(memory_space=pltpu.HBM)
    result = pl.pallas_call(
        functools.partial(kernel, n_row, n_col),
        out_shape=jax.ShapeDtypeStruct((2,) + source.shape, F32),
        in_specs=[hbm] * 6,
        out_specs=vm,
        scratch_shapes=[
            pltpu.VMEM((members, ext, cols), F32),
            pltpu.VMEM((members, ext, cols), F32),
            pltpu.VMEM((members, rows, cols), F32),
            pltpu.VMEM((2 * NA, cells), BF16),
            pltpu.VMEM((3 * NA, cells), BF16),
            pltpu.VMEM((2 * members, cells), BF16),
            pltpu.VMEM((cols, cols), F32),
            pltpu.VMEM((rows, cols), F32),
            pltpu.VMEM((2, rows, cols), F32),
            pltpu.VMEM((4, GROUP, cols), F32),
            pltpu.VMEM((2, 2 * GROUP, cols), F32),
            pltpu.VMEM((2, 2 * GROUP, cols), F32),
            pltpu.VMEM((3, rows, cols), F32),
            pltpu.VMEM((2, 2, rows, cols), F32),
            pltpu.VMEM((2, 4, GROUP, cols), F32),
            pltpu.VMEM((3, 2, WIDE * members, cols), F32),
            pltpu.VMEM((3, 2, WIDE * members, cols), F32),
            pltpu.VMEM((NX0, half_m, cols), F32),
            pltpu.VMEM((NX0, 4, half_m, cols), F32),
            pltpu.VMEM((half_m, cols), F32),
            pltpu.VMEM((4, half_m, cols), F32),
            pltpu.VMEM((NX0, 4, 2 * half_m, cols), F32),
            pltpu.VMEM((NX0, 4, 2 * half_m, cols), F32),
            pltpu.VMEM((NX0, 4, 2 * half_m, cols), F32),
            pltpu.VMEM((NX0, 4, 2 * half_m, cols), F32),
            pltpu.VMEM((NX0, 4, half_m, cols), F32),
            pltpu.VMEM((2, NA, cols), F32),
            pltpu.VMEM((2, NA, cols), F32),
            pltpu.VMEM((2, NA // 2, cols), F32),
            pltpu.VMEM((4, NA // 2, cols), F32),
            pltpu.VMEM((LEVELS - 1, 3, NA, cols), F32),
            pltpu.VMEM((NA, cols), F32),
            pltpu.VMEM((2, GROUP, cols), F32),
            pltpu.VMEM((6, GROUP, cols), F32),
            pltpu.VMEM((LEVELS, half_m, cols), F32),
            pltpu.VMEM((mates, half_m, cols), F32),
            pltpu.VMEM((5 * cols, 2 * cols), BF16),
            pltpu.VMEM((LEVELS * cols, 2 * cols), BF16),
            pltpu.VMEM((LEVELS * cols, 2 * cols), BF16),
            pltpu.VMEM((LEVELS, cols, cols), BF16),
            pltpu.VMEM((rows, cols), F32),
            pltpu.VMEM((rows, cols), F32),
            pltpu.VMEM((rows, cols), jnp.int32),
            pltpu.VMEM((LEVELS, cols), jnp.int32),
            pltpu.SemaphoreType.DMA((slots,)),
            pltpu.SemaphoreType.DMA((slots,)),
            pltpu.SemaphoreType.DMA((6,)),
        ],
        compiler_params=pltpu.CompilerParams(collective_id=0, has_side_effects=True, vmem_limit_bytes=VMEM_LIMIT),
    )(*(pltpu.with_memory_space_constraint(a, pltpu.HBM) for a in (
        source, guess, conductivity, storage, aggregates, pair_maps.reshape(LEVELS, -1))))
    return result[0], result[1]


def solution(mesh):
    placed = (
        P(None, "row", "col"),
        P(None, "row", "col"),
        P("row", "col"),
        P("row", "col"),
        P("row", "col"),
        P(None, "row", "col", None),
    )
    return jax.shard_map(
        functools.partial(shards, mesh.shape["row"], mesh.shape["col"]),
        mesh=mesh,
        in_specs=placed,
        out_specs=(P(None, "row", "col"), P(None, "row", "col")),
        check_vma=False,
    )
```

```python
import functools

import jax
import jax.numpy as jnp
from jax import lax
from jax.experimental import pallas as pl
from jax.experimental.pallas import tpu as pltpu
from jax.sharding import PartitionSpec as P

NA = 64
SWEEPS = 3
LEVELS = 4
OMEGA_FINE = 0.8
OMEGA_COARSE = 0.6
F32 = jnp.float32
BF16 = jnp.bfloat16
MESH = pl.DeviceIdType.MESH
OPP = (1, 0, 3, 2, 7, 6, 5, 4, 9, 8, 11, 10)
WIDE = SWEEPS + 1
GROUP = 2 * WIDE
HOPS = 28
NEAR = HOPS + 32
MATS = NEAR + 4
VECS = MATS + 6
OUTS = VECS + 2 ** LEVELS - 1
SPLIT = 36
NX0 = 2
CORNERS = ((1, 3), (1, 2), (0, 3), (0, 2))
VMEM_LIMIT = 24 * 1024 * 1024
NN = (((1,), (0,)), ((), ()))
NT = (((1,), (1,)), ((), ()))


def dg(a, b, dims):
    return lax.dot_general(a, b, dims, preferred_element_type=F32)


def split2(x):
    hi = x.astype(BF16)
    return hi, (x - hi.astype(F32)).astype(BF16)


def split3(x):
    hi = x.astype(BF16)
    rest = x - hi.astype(F32)
    mid = rest.astype(BF16)
    return hi, mid, (rest - mid.astype(F32)).astype(BF16)


def stacked(x):
    hi = x.astype(BF16).astype(F32)
    return jnp.concatenate([hi, x - hi], axis=0).astype(BF16)


def times(x, weights):
    n, wide = x.shape[0], weights.shape[1] // 2
    full = dg(stacked(x), weights, NN)
    return full[0:n, 0:wide] + (full[n:, 0:wide] + full[0:n, wide:])


def times_t(x, weights):
    n = x.shape[0]
    both = stacked(x)
    full = dg(jnp.concatenate([both, both], axis=1), weights, NT)
    return full[0:n] + full[n:]


def dot_hot(x, hot, dims):
    n = x.shape[0]
    hi = x.astype(BF16).astype(F32)
    mid = (x - hi).astype(BF16).astype(F32)
    full = dg(jnp.concatenate([hi, mid, x - hi - mid], axis=0).astype(BF16), hot, dims)
    return full[0:n] + (full[n : 2 * n] + full[2 * n :])


def hot_dot(hot, x, dims):
    hi, mid, lo = split3(x)
    return dg(hot, hi, dims) + (dg(hot, mid, dims) + dg(hot, lo, dims))


def kernel(n_row, n_col, src_in, guess_in, cond_in, sto_in, agg_in, pm_in, result,
           u, se, left, mo, gmat, rlhs, xt, ksend, krecv, kcorn, krsend, krrecv, hsend, hrecv, hcorn, rowbuf,
           rsend, xsend, xrecv, nsend, nrecv, tsend, trecv, csend, crecv, srecv, msend, mrecv, hsum, hrest, held, solve, coef, early, osend, orecv, vsend, vrecv, wmat, fmat, gfin, qts,
           cond, sto, agg, pm, ssem, rsem, lsem):
    members, rows, cols = guess_in.shape
    half_m = members // 2
    ext = rows + GROUP
    row = lax.axis_index("row")
    col = lax.axis_index("col")
    has = [row > 0, row < n_row - 1, col > 0, col < n_col - 1]
    dev = [(row - 1, col), (row + 1, col), (row, col - 1), (row, col + 1)]
    for v in (0, 1):
        for h in (2, 3):
            has.append(jnp.logical_and(has[v], has[h]))
            dev.append((dev[v][0], dev[h][1]))
    far_has = [row > 1, row < n_row - 2, col > 1, col < n_col - 2]
    far_dev = [(row - 2, col), (row + 2, col), (row, col - 2), (row, col + 2)]
    has += far_has
    dev += far_dev
    col_bit = col % 2
    row_bit = row % 2
    col_bit2 = col // 2 % 2
    row_bit2 = row // 2 % 2
    upper = (col_bit, row_bit, col_bit2, row_bit2)
    flip_col = (0, 1 - 2 * col_bit, 2 - 4 * col_bit2, 3 - 2 * col_bit - 4 * col_bit2)
    flip_row = (0, 1 - 2 * row_bit, 2 - 4 * row_bit2, 3 - 2 * row_bit - 4 * row_bit2)

    def mate(j):
        return (row + flip_row[j // 2 % 2 + 2 * (j // 8)], col + flip_col[j % 2 + 2 * (j // 4 % 2)])

    loads = [
        pltpu.make_async_copy(source, target, lsem.at[i])
        for i, (source, target) in enumerate((
            (guess_in, u.at[:, pl.ds(0, rows)]), (src_in, se.at[:, pl.ds(0, rows)]),
            (cond_in, cond), (agg_in, agg), (sto_in, sto), (pm_in, pm)))
    ]
    for load in loads:
        load.start()

    barrier = pltpu.get_barrier_semaphore()
    count = jnp.int32(0)
    for d in range(8):
        count = count + has[d].astype(jnp.int32)

        @pl.when(has[d])
        def _():
            pl.semaphore_signal(barrier, inc=1, device_id=dev[d], device_id_type=MESH)

    def copy(source, target, slot, device):
        return pltpu.make_async_remote_copy(
            src_ref=source, dst_ref=target, send_sem=ssem.at[slot], recv_sem=rsem.at[slot],
            device_id=device, device_id_type=MESH)

    sent = []

    def start(d, source, target, slot):
        @pl.when(has[d])
        def _():
            copy(source, target, slot, dev[d]).start()

        sent.append((d, source, target, slot))

    def arrive(d, source, target, slot):
        @pl.when(has[OPP[d]])
        def _():
            copy(source, target, slot, dev[d]).wait_recv()

    for d in range(12):
        @pl.when(jnp.logical_not(has[OPP[d]]))
        def _():
            if d < 2:
                krrecv[d] = jnp.ones((2 * GROUP, cols), F32)
                for p in range(3):
                    rowbuf[p, d] = jnp.zeros((WIDE * members, cols), F32)
            elif d < 4:
                krecv[d - 2] = jnp.ones((rows, cols), F32)
                for p in range(2):
                    hrecv[p, d - 2] = jnp.zeros((rows, cols), F32)
            elif d < 8:
                kcorn[d - 4] = jnp.ones((GROUP, cols), F32)
                for p in range(2):
                    hcorn[p, d - 4] = jnp.zeros((GROUP, cols), F32)
            for e in range(NX0):
                if d < 4:
                    xrecv[e, d] = jnp.zeros((half_m, cols), F32)
                    trecv[e, d] = jnp.zeros((2 * half_m, cols), F32)
                elif d < 8:
                    crecv[e, d - 4] = jnp.zeros((2 * half_m, cols), F32)
                else:
                    srecv[e, d - 8] = jnp.zeros((half_m, cols), F32)
            if d < 4:
                nrecv[d] = jnp.zeros((half_m, cols), F32)

    lane = lax.broadcasted_iota(jnp.int32, (ext, cols), 1)
    sub = lax.broadcasted_iota(jnp.int32, (ext, cols), 0)
    l8 = lane % GROUP
    owner = lane // GROUP
    lane8 = lane[0:GROUP]
    sub8 = sub[0:GROUP]

    def mirror(x):
        where = lax.broadcasted_iota(jnp.int32, x.shape, 1)
        bit = 1
        while bit < GROUP:
            x = jnp.where(where // bit % 2 == 0, pltpu.roll(x, cols - bit, 1), pltpu.roll(x, bit, 1))
            bit *= 2
        return x

    def repeat(x):
        width = GROUP
        while width < cols:
            x = x + pltpu.roll(x, width, 1)
            width *= 2
        return x

    def side_ref(source, target, corners, d, slot):
        if d < 4:
            return d, source, target.at[d - 2], slot + d
        return d, source.at[pl.ds(0 if d < 6 else rows - GROUP, GROUP)], corners.at[d - 4], slot + d

    def row_ref(p, d):
        return d, rsend.at[p, d], rowbuf.at[p, d], 16 + 2 * p + d

    def field_ref(d):
        return side_ref(hsend.at[0 if d % 2 == 0 else 1], hrecv.at[0], hcorn.at[0], d, 8)

    def again_ref(d):
        if d < 2:
            return row_ref(2, d)
        return side_ref(hsend.at[2], hrecv.at[1], hcorn.at[1], d, 20)

    def coef_ref(d):
        if d < 2:
            return d, krsend.at[d], krrecv.at[d], d
        return side_ref(ksend, krecv, kcorn, d, 0)

    def pack_sides(fields):
        packed = jnp.zeros((rows, cols), F32)
        for m, v in enumerate(fields):
            packed = jnp.where(owner[0:rows] == m, pltpu.roll(v, (GROUP * m + WIDE) % cols, 1), packed)
        return mirror(packed)

    def pack_rows(p, field):
        for m in range(members):
            rsend[p, 0, WIDE * m : WIDE * (m + 1), :] = field[m, 0:WIDE]
            rsend[p, 1, WIDE * m : WIDE * (m + 1), :] = field[m, rows - WIDE : rows]

    order = (2, 3, 1, 0, 4, 5, 6, 7)

    def under(south, north):
        return jnp.where(sub8 < WIDE, south, north)

    def fill_rows(p, field):
        for m in range(members):
            field[m, rows : rows + WIDE, :] = rowbuf[p, 0, WIDE * m : WIDE * (m + 1), :]
            field[m, rows + WIDE : ext, :] = rowbuf[p, 1, WIDE * m : WIDE * (m + 1), :]

    def sides(planes, corners):
        return (jnp.concatenate([planes[0], under(corners[0], corners[2])], axis=0),
                jnp.concatenate([planes[1], under(corners[1], corners[3])], axis=0))

    for load in loads:
        load.wait()
    agg_v = agg[...]
    sub64 = lax.broadcasted_iota(jnp.int32, (NA, cols), 0)
    for r in range(rows):
        hot = jnp.where(sub64 == agg_v[r : r + 1], 1.0, 0.0).astype(BF16)
        mo[0:NA, r * cols : (r + 1) * cols] = hot
        mo[NA : 2 * NA, r * cols : (r + 1) * cols] = hot
    xt[...] = jnp.zeros(xt.shape, F32)
    iota128 = lax.broadcasted_iota(jnp.int32, (cols, cols), 0)
    lane128 = lax.broadcasted_iota(jnp.int32, (cols, cols), 1)
    for k in range(LEVELS):
        pmk = pm[k : k + 1, :]
        pmk = jnp.where(upper[k] == 1, pltpu.roll(pmk, NA, 1), pmk)
        qts[k] = jnp.where(jnp.logical_and(iota128 == pmk, lane128 < NA), 1.0, 0.0).astype(BF16)

    def face(a, b):
        return 2.0 * (a * b) / (a + b)

    last = rows - 1
    c = cond[...]
    in_east = jnp.where(lane[0:rows] < cols - 1, face(c, pltpu.roll(c, cols - 1, 1)), 0.0)
    in_south = jnp.where(sub[0:rows] < last, face(c, pltpu.roll(c, last, 0)), 0.0)
    right = pltpu.roll(agg_v, cols - 1, 1)
    below = pltpu.roll(agg_v, last, 0)
    half = 0.5 * (sto[...] + in_east + pltpu.roll(in_east, 1, 1) + in_south + pltpu.roll(in_south, 1, 0))
    for r in range(rows):
        s = slice(r, r + 1)
        g = (jnp.where(sub64 == right[s], in_east[s], 0.0)
             + jnp.where(sub64 == below[s], in_south[s], 0.0)
             - jnp.where(sub64 == agg_v[s], half[s], 0.0))
        for i, part in enumerate(split3(g)):
            gmat[i * NA : (i + 1) * NA, r * cols : (r + 1) * cols] = part
    gx = dg(gmat[...], mo[0:NA], NT)
    xt[0:NA, 0:NA] = gx[0:NA] + (gx[NA : 2 * NA] + gx[2 * NA : 3 * NA])
    xfull = xt[...]
    inner = -(xfull + xfull.T)[0:NA]

    lane_c = lax.broadcasted_iota(jnp.int32, (NA, cols), 1)
    lane_1 = lax.broadcasted_iota(jnp.int32, (1, cols), 1)
    eye = jnp.where(lane_c == sub64, 1.0, 0.0)

    def squeeze(mat, pair):
        right = dot_hot(mat[:, 0:NA], pair, NT)
        full = hot_dot(pair, right, NN)
        both = jnp.where(lane_c < NA, full[0:NA], full[NA : 2 * NA])
        half = jnp.where(lane_c[0 : NA // 2] < NA, pltpu.roll(both[0 : NA // 2], NA, 1), both[NA // 2 : NA])
        return both, half

    def lower(both):
        return jnp.where(lane_c < NA, both, 0.0)

    def higher(both, halves):
        halves = jnp.concatenate([halves, pltpu.roll(halves, NA, 1)], axis=0)
        return jnp.where(lane_c < NA, pltpu.roll(both, NA, 1) + halves, 0.0)

    hots = [qts[k][0:NA, 0:NA] for k in range(LEVELS)]

    def onward(a, b):
        return dg(a, b, NN).astype(BF16)

    pair_12 = jnp.concatenate([hots[0], onward(hots[1], hots[0])], axis=0)
    pair_34 = jnp.concatenate([hots[2], onward(hots[3], hots[2])], axis=0)
    pair_all = jnp.concatenate([pair_12, onward(pair_34, pair_12[NA : 2 * NA])], axis=0)
    msend[0], hsum[0] = squeeze(inner, pair_12)

    aggf = agg[...].astype(F32)
    ksend[...] = pack_sides([cond[...], sto[...], aggf])
    for d, near, wide in ((0, 0, 0), (1, rows - WIDE, rows - GROUP)):
        krsend[d, 0:WIDE] = cond[near : near + WIDE]
        krsend[d, WIDE:GROUP] = sto[near : near + WIDE]
        krsend[d, GROUP : 2 * GROUP] = aggf[wide : wide + GROUP]
    side_g = pack_sides([u[m, 0:rows] for m in range(members)])
    side_f = pack_sides([se[m, 0:rows] for m in range(members)])
    inward = l8[0:rows] < WIDE
    hsend[0] = jnp.where(inward, side_g, pltpu.roll(side_f, WIDE, 1))
    hsend[1] = jnp.where(inward, pltpu.roll(side_g, cols - WIDE, 1), side_f)
    pack_rows(0, u)
    pack_rows(1, se)
    pl.semaphore_wait(barrier, count)
    def mat_copy(i):
        at = i // 3
        mates = mate((1, 2, 3, 4, 8, 12)[i])
        if i % 3 == 0:
            return copy(msend.at[at], mrecv.at[at], MATS + i, mates)
        return copy(hsum.at[at], hrest.at[2 * at + i % 3 - 1], MATS + i, mates)

    for d in order:
        start(*coef_ref(d))
    for d in (2, 3):
        start(*field_ref(d))
    for p in range(2):
        for d in (1, 0):
            start(*row_ref(p, d))
    for d in range(4, 8):
        start(*field_ref(d))
    for i in range(3):
        mat_copy(i).start()

    for d in range(8):
        arrive(*coef_ref(d))

    k_east, k_west = sides(krecv, kcorn)
    k_side = jnp.where(l8 < WIDE, k_east, k_west)

    def extend(value, at):
        main = jnp.concatenate([value[...]] + [krrecv[d, at * WIDE : (at + 1) * WIDE] for d in range(2)], axis=0)
        return main, repeat(jnp.where(lane < GROUP, pltpu.roll(k_side, (cols - at * GROUP) % cols, 1), 0.0))

    cm, cs = extend(cond, 0)
    sm, ss = extend(sto, 1)
    hasi = [h.astype(jnp.int32) for h in has[0:4]]

    def vertical(x):
        down = jnp.where(jnp.logical_and(sub == last, hasi[1] == 0), 0.0, face(x, pltpu.roll(x, ext - 1, 0)))
        up = jnp.where(jnp.logical_and(sub == 0, hasi[0] == 0), 0.0, face(x, pltpu.roll(x, 1, 0)))
        return down, up

    side_at = pltpu.roll(cs, cols - WIDE, 1)
    rim = jnp.logical_and(lane >= WIDE - 1, lane <= WIDE)
    main_at = repeat(jnp.where(rim, pltpu.roll(cm, WIDE, 1), 0.0))
    east = face(cm, jnp.where(lane == cols - 1, side_at, pltpu.roll(cm, cols - 1, 1)))
    west = face(cm, jnp.where(lane == 0, side_at, pltpu.roll(cm, 1, 1)))
    east = jnp.where(lane < cols - 1 + hasi[3], east, 0.0)
    west = jnp.where(lane >= 1 - hasi[2], west, 0.0)
    south, north = vertical(cm)
    diag = sm + east + west + south + north
    step = OMEGA_FINE / diag
    s_west = face(cs, jnp.where(l8 == WIDE - 1, main_at, pltpu.roll(cs, cols - 1, 1)))
    s_east = face(cs, jnp.where(l8 == WIDE, main_at, pltpu.roll(cs, 1, 1)))
    s_west = jnp.where(jnp.logical_and(l8 == WIDE - 1, hasi[3] == 0), 0.0, s_west)
    s_east = jnp.where(jnp.logical_and(l8 == WIDE, hasi[2] == 0), 0.0, s_east)
    s_south, s_north = vertical(cs)
    s_diag = ss + s_east + s_west + s_south + s_north
    s_step = OMEGA_FINE / s_diag
    for i, value in enumerate((east, west, south, north, diag, step)):
        coef[i] = value
    for i, value in enumerate((s_east, s_west, s_south, s_north, s_diag, s_step)):
        coef[6 + i] = value

    def apply_field(side, n, finish):
        lane_n = lane[0:n]
        edge = jnp.zeros((ext, cols), F32)
        for m in range(members):
            v = u[m]
            hm = pltpu.roll(side, (2 * cols - GROUP * m - WIDE) % cols, 1)[0:n]
            vn = v[0:n]
            from_w = jnp.where(lane_n == 0, hm, pltpu.roll(vn, 1, 1))
            from_e = jnp.where(lane_n == cols - 1, hm, pltpu.roll(vn, cols - 1, 1))
            from_s = pltpu.roll(v, ext - 1, 0)[0:n]
            from_n = pltpu.roll(v, 1, 0)[0:n]
            rest = se[m, 0:n] - (coef[4, 0:n] * vn - (
                coef[0, 0:n] * from_e + coef[1, 0:n] * from_w + coef[2, 0:n] * from_s + coef[3, 0:n] * from_n))
            if n == ext:
                edge = jnp.where(owner == m, pltpu.roll(v, (GROUP * m + WIDE) % cols, 1), edge)
            finish(m, vn, rest)
        return edge

    def sweep(side, s_src):
        def finish(m, v, rest):
            u[m] = v + coef[5] * rest

        edge = apply_field(side, ext, finish)
        from_w = jnp.where(l8 == WIDE - 1, edge, pltpu.roll(side, cols - 1, 1))
        from_e = jnp.where(l8 == WIDE, edge, pltpu.roll(side, 1, 1))
        rest = s_src - (coef[10] * side - (coef[6] * from_e + coef[7] * from_w
                        + coef[8] * pltpu.roll(side, ext - 1, 0) + coef[9] * pltpu.roll(side, 1, 0)))
        return side + coef[11] * rest


    agg_t = agg_v.astype(F32).T.astype(jnp.int32)

    def put(ref, slot, block):
        both = jnp.concatenate([block, pltpu.roll(block, NA, 1)], axis=0)
        hi, lo = split2(both)
        ref[slot * cols : (slot + 1) * cols, 0:cols] = hi
        ref[slot * cols : (slot + 1) * cols, cols : 2 * cols] = lo

    joined = []

    def couple(slot, own_ids, other_ids, faces, width):
        own = jnp.where(lax.broadcasted_iota(jnp.int32, (cols, width), 0) == own_ids, 1.0, 0.0).astype(BF16)
        other = jnp.where(lax.broadcasted_iota(jnp.int32, (NA, width), 0) == other_ids, faces, 0.0)
        links = dot_hot(other, own, NT)
        joined.append((slot, -links))
        return jnp.sum(links, axis=0, keepdims=True)

    row_ids = [krrecv[d].astype(jnp.int32) for d in range(2)]
    outer = couple(1, agg_v[last:rows], row_ids[0][GROUP : GROUP + 1], south[last:rows], cols)
    outer = outer + couple(2, agg_v[0:1], row_ids[1][2 * GROUP - 1 : 2 * GROUP], north[0:1], cols)
    k_ids = k_side[0:rows].T.astype(jnp.int32)
    near_e = 2 * GROUP + WIDE - 1
    outer = outer + couple(3, agg_t[cols - 1 : cols], k_ids[near_e : near_e + 1], east[0:rows].T[cols - 1 : cols], rows)
    outer = outer + couple(4, agg_t[0:1], k_ids[near_e + 1 : near_e + 2], west[0:rows].T[0:1], rows)

    def vec_copy(j):
        return copy(vsend.at[j.bit_length() - 1], vrecv.at[j - 1], VECS + j - 1, mate(j))

    def out_copy(i):
        return copy(osend.at[i // 3], orecv.at[i], OUTS + i, mate((1, 2, 3, 4, 8, 12)[i]))

    def weight(mat):
        d = jnp.sum(jnp.where(lane_c == sub64, mat, 0.0), axis=0, keepdims=True)
        ok = lane_1 < NA
        return jnp.where(ok, OMEGA_COARSE / jnp.where(ok, d, 1.0), 0.0)

    def parted(b):
        hi = b.astype(BF16).astype(F32)
        return jnp.where(lane_c < NA, hi, pltpu.roll(b - hi, NA, 1)).astype(BF16)

    def product(a, b):
        full = dg(stacked(a[:, 0:NA]), b, NN)
        part = full[0:NA] + jnp.where(lane_c < NA, full[NA : 2 * NA], 0.0)
        return jnp.where(lane_c < NA, part + pltpu.roll(part, NA, 1), 0.0)

    def smoother(mat):
        side_w = OMEGA_COARSE / jnp.sum(eye * mat, axis=1, keepdims=True)
        one = eye - mat * weight(mat)
        parts = parted(one)
        two = product(one, parts)
        return product(two, parts), side_w * (eye + one + two)

    block = inner + jnp.where(lane_c == sub64, outer, 0.0)
    outers = dot_hot(jnp.broadcast_to(outer[:, 0:NA], (GROUP, NA)), pair_all, NT)
    outers = [outers[:, 0:cols], outers[:, cols : 2 * cols]]
    level = jnp.zeros((GROUP, cols), F32)
    for k in range(LEVELS):
        level = jnp.where(sub8 == k, pltpu.roll(outers[k // 2], NA, 1) if k % 2 else outers[k // 2], level)
    osend[0] = jnp.where(lane8 < NA, level, 0.0)
    for i in range(3):
        out_copy(i).start()
    weights = weight(block)
    weights = jnp.broadcast_to(weights + pltpu.roll(weights, NA, 1), (half_m, cols))
    nsend[...] = weights

    def near_ref(d):
        return d, nsend, nrecv.at[d], NEAR + d

    for d in (2, 3, 1, 0):
        start(*near_ref(d))
    put(wmat, 0, block)
    for slot, links in joined:
        put(wmat, slot, links)

    for d in range(2, 8):
        arrive(*field_ref(d))
    for p in range(2):
        for d in range(2):
            arrive(*row_ref(p, d))
    fill_rows(0, u)
    fill_rows(1, se)
    h_east, h_west = sides(hrecv[0], hcorn[0])
    side = jnp.where(l8 < WIDE, h_east, pltpu.roll(h_west, WIDE, 1))
    s_src = jnp.where(l8 < WIDE, pltpu.roll(h_east, cols - WIDE, 1), h_west)
    for _ in range(SWEEPS):
        side = sweep(side, s_src)

    def keep_left(m, v, rest):
        left[m] = rest

    apply_field(side, rows, keep_left)
    for r in range(rows):
        for i, part in enumerate(split2(left[:, r, :])):
            rlhs[i * members : (i + 1) * members, r * cols : (r + 1) * cols] = part
    gr = dg(rlhs[...], mo[...], NT)
    gr = gr[0:members] + gr[members : 2 * members]
    lane_h = lax.broadcasted_iota(jnp.int32, (half_m, cols), 1)

    def fold(x):
        return jnp.where(lane_h < NA, x[0:half_m], x[half_m:members])

    y0 = fold(gr)

    def x_slot(e, d):
        return (d, xsend.at[e], xrecv.at[e, d], HOPS + 16 * e + d)

    def level_one(e, x, sweep_it, between=None):
        xsend[e] = x
        for d in (2, 3, 1, 0):
            start(*x_slot(e, d))
        early[...] = x + (y0 - times(x, wmat[0:cols])) * weights if sweep_it else y0 - times(x, wmat[0:cols])
        if between is not None:
            between()
        for d in range(4):
            arrive(*x_slot(e, d))
        every = jnp.concatenate([xrecv[e, d] for d in range(4)], axis=1)
        near = times(every, wmat[cols : 5 * cols])
        return early[...] - (near * weights if sweep_it else near)

    def t_slot(e, d):
        slot = HOPS + 16 * e + 4 + d
        if d < 4:
            return d, tsend.at[e, OPP[d]], trecv.at[e, d], slot
        if d < 8:
            return d, csend.at[e, d - 4], crecv.at[e, d - 4], slot
        return d, tsend.at[e, OPP[d - 8], pl.ds(half_m, half_m)], srecv.at[e, d - 8], slot

    def two_sweeps(e, x, between=None):
        full = times_t(x, wmat[...])
        first = x + (y0 - full[:, 0:cols]) * weights
        out = [full[:, (n + 1) * cols : (n + 2) * cols] * nrecv[n] for n in range(4)]
        for n in range(4):
            tsend[e, n, 0:half_m] = first
            tsend[e, n, half_m : 2 * half_m] = out[n]
        for i, (v, h) in enumerate(CORNERS):
            csend[e, i, 0:half_m] = out[v]
            csend[e, i, half_m : 2 * half_m] = out[h]
        for d in (4, 5, 6, 7, 8, 9, 10, 11, 2, 3, 1, 0):
            start(*t_slot(e, d))
        if between is not None:
            between()
        for d in range(12):
            arrive(*t_slot(e, d))
        got = [trecv[e, d, half_m : 2 * half_m] for d in range(4)]
        tiles = [first - ((got[0] + got[1]) + (got[2] + got[3]))]
        for n in range(4):
            tiles.append(trecv[e, n, 0:half_m] - (out[n] + srecv[e, n]))
        for i, (v, h) in enumerate(CORNERS):
            tiles[1 + OPP[h]] = tiles[1 + OPP[h]] - crecv[e, i, 0:half_m]
            tiles[1 + OPP[v]] = tiles[1 + OPP[v]] - crecv[e, i, half_m : 2 * half_m]
        return tiles[0] + (y0 - times(jnp.concatenate(tiles, axis=1), wmat[...])) * weights

    for i in range(3):
        mat_copy(i).wait_recv()
    mat_1 = msend[0] + mrecv[0]
    mat_2 = higher(mat_1, hrest[0] + hrest[1])
    mat_1 = lower(mat_1)
    msend[1], hsum[1] = squeeze(mat_2, pair_34)
    for i in range(3, 6):
        mat_copy(i).start()
    for i in range(3):
        out_copy(i).wait_recv()
    outer_1 = osend[0] + orecv[0]
    osend[1] = outer_1 + jnp.where(sub8 > 0, orecv[1] + orecv[2], 0.0)
    for i in range(3, 6):
        out_copy(i).start()
    for d in range(4):
        arrive(*near_ref(d))
    def lift(k):
        onto = hot_dot(hots[k + 1], held[k, 0], NN)
        held[k, 1] = product(held[k, 1], parted(held[k, 2]))
        held[k, 0] = jnp.concatenate([onto, jnp.zeros((cols - NA, cols), F32)], axis=0).T[0:NA]

    def link(k, mat, chain):
        cube, pre = smoother(mat)
        moved = product(cube, parted(chain))
        held[k, 0] = cube
        held[k, 1] = pre
        held[k, 2] = chain + moved
        chain = hot_dot(hots[k + 1], moved, NN)
        put(fmat, k + 1, chain)
        return chain

    def early_chains():
        chain = hots[0].astype(F32)
        chain = jnp.concatenate([chain, jnp.zeros((NA, cols - NA), F32)], axis=1)
        put(fmat, 0, chain)
        chain = link(0, mat_1 + eye * outer_1[0:1], chain)
        solve[...] = link(1, mat_2 + eye * osend[1, 1:2], chain)
        for k in range(LEVELS - 2):
            lift(k)

    def late_chains():
        for i in range(3, 6):
            mat_copy(i).wait_recv()
        for i in range(3, 6):
            out_copy(i).wait_recv()
        sums = osend[1] + orecv[3]
        both = msend[1] + mrecv[1]
        chain = link(2, lower(both) + eye * sums[2:3], solve[...])
        sums = sums + (orecv[4] + orecv[5])
        mat = higher(both, hrest[2] + hrest[3]) + eye * sums[3:4]
        solve[...] = jnp.where(lane_c < NA, mat, pltpu.roll(chain, NA, 1))

    sub_g = lax.broadcasted_iota(jnp.int32, (GROUP, cols), 0)

    def lanes_of(v, k):
        return jnp.broadcast_to(v[:, k : k + 1], (GROUP, cols))

    def row_of(v, r):
        return jnp.broadcast_to(v[r : r + 1], (GROUP, cols))

    def pair_product(a, b):
        return [[a[i][0] * b[0][j] + a[i][1] * b[1][j] for j in range(2)] for i in range(2)]

    def pair_inverse(a):
        scale = 1.0 / (a[0][0] * a[1][1] - a[0][1] * a[1][0])
        return [[a[1][1] * scale, -a[0][1] * scale], [-a[1][0] * scale, a[0][0] * scale]]

    def quad_inverse(a):
        first = pair_inverse([a[i][0:2] for i in range(2)])
        right = pair_product(first, [a[i][2:4] for i in range(2)])
        below = [a[i][0:2] for i in range(2, 4)]
        moved = pair_product(below, right)
        second = pair_inverse([[a[2 + i][2 + j] - moved[i][j] for j in range(2)] for i in range(2)])
        down = pair_product(second, pair_product(below, first))
        back = pair_product(right, down)
        over = pair_product(right, second)
        return ([[first[i][j] + back[i][j] for j in range(2)] + [-over[i][j] for j in range(2)] for i in range(2)]
                + [[-down[i][j] for j in range(2)] + second[i] for i in range(2)])

    def eliminate(first, end):
        blocks = [solve[k : k + GROUP] for k in range(0, NA, GROUP)]
        for k in range(first, end, 4):
            q, r = k // GROUP, k % GROUP
            across = [[lanes_of(v, k + j) for v in blocks] for j in range(4)]
            inv = quad_inverse([[row_of(across[j][q], r + i) for j in range(4)] for i in range(4)])
            lines = [row_of(blocks[q], r + i) for i in range(4)]
            pivots = [(inv[i][0] * lines[0] + inv[i][1] * lines[1]) + (inv[i][2] * lines[2] + inv[i][3] * lines[3])
                      for i in range(4)]
            blocks = [v - ((across[0][i] * pivots[0] + across[1][i] * pivots[1])
                           + (across[2][i] * pivots[2] + across[3][i] * pivots[3])) for i, v in enumerate(blocks)]
            for i in range(4):
                blocks[q] = jnp.where(sub_g == r + i, pivots[i], blocks[q])
        for i, v in enumerate(blocks):
            solve[GROUP * i : GROUP * (i + 1)] = v

    x = two_sweeps(0, y0 * weights, early_chains)
    rem = level_one(0, x, False, lambda: (late_chains(), eliminate(0, SPLIT)))
    up = times_t(rem, fmat[...])
    for k in range(LEVELS):
        vsend[k] = up[:, k * cols : (k + 1) * cols]
    for j in reversed(range(1, 2 ** LEVELS)):
        vec_copy(j).start()
    lift(LEVELS - 2)
    eliminate(SPLIT, NA)
    final = jnp.where(lane_c < NA, pltpu.roll(solve[...], NA, 1), 0.0)
    put(gfin, LEVELS - 1, final)
    for k in reversed(range(LEVELS - 1)):
        final = held[k, 1] + product(held[k, 0], parted(final))
        put(gfin, k, final)
    for j in range(1, 2 ** LEVELS):
        vec_copy(j).wait_recv()
    ys = []
    for k in range(LEVELS):
        y = [vrecv[j - 1] for j in range(2 ** k, 2 ** (k + 1))]
        y = y + [vsend[0]] if k == 0 else y
        while len(y) > 1:
            y = [a + b for a, b in zip(y[::2], y[1::2])]
        ys.append(y[0])
    x = two_sweeps(1, x + times(jnp.concatenate(ys, axis=1), gfin[...]))
    x = level_one(1, x, True)

    whole = jnp.concatenate([x, pltpu.roll(x, NA, 1)], axis=0)
    whole_hi = whole.astype(BF16).astype(F32)
    lane_m = lax.broadcasted_iota(jnp.int32, (members, cols), 1)
    spread = jnp.where(lane_m < NA, whole_hi, pltpu.roll(whole - whole_hi, NA, 1)).astype(BF16)
    for q in range(0, rows, 4):
        part = dg(spread, mo[:, q * cols : (q + 4) * cols], NN)
        for r in range(q, q + 4):
            u[:, r, :] = u[:, r, :] + part[:, (r - q) * cols : (r - q + 1) * cols]
    hsend[2] = pack_sides([u[m, 0:rows] for m in range(members)])
    pack_rows(2, u)
    for d in order:
        start(*again_ref(d))
    for d in range(8):
        arrive(*again_ref(d))
    fill_rows(2, u)
    h_east, h_west = sides(hrecv[1], hcorn[1])
    side = jnp.where(l8 < WIDE, h_east, h_west)
    for _ in range(SWEEPS):
        side = sweep(side, s_src)

    def out(m, v, rest):
        result[0, m] = v
        result[1, m] = rest

    apply_field(side, rows, out)
    for d, source, target, slot in sent:
        @pl.when(has[d])
        def _():
            copy(source, target, slot, dev[d]).wait_send()

    for i in range(6):
        mat_copy(i).wait_send()
        out_copy(i).wait_send()
    for j in range(1, 2 ** LEVELS):
        vec_copy(j).wait_send()


def shards(n_row, n_col, source, guess, conductivity, storage, aggregates, pair_maps):
    members, rows, cols = source.shape
    cells = rows * cols
    ext = rows + GROUP
    vm = pl.BlockSpec(memory_space=pltpu.VMEM)
    half_m = members // 2
    mates = 2 ** LEVELS - 1
    slots = OUTS + 6
    hbm = pl.BlockSpec(memory_space=pltpu.HBM)
    result = pl.pallas_call(
        functools.partial(kernel, n_row, n_col),
        out_shape=jax.ShapeDtypeStruct((2,) + source.shape, F32),
        in_specs=[hbm] * 6,
        out_specs=vm,
        scratch_shapes=[
            pltpu.VMEM((members, ext, cols), F32),
            pltpu.VMEM((members, ext, cols), F32),
            pltpu.VMEM((members, rows, cols), F32),
            pltpu.VMEM((2 * NA, cells), BF16),
            pltpu.VMEM((3 * NA, cells), BF16),
            pltpu.VMEM((2 * members, cells), BF16),
            pltpu.VMEM((cols, cols), F32),
            pltpu.VMEM((rows, cols), F32),
            pltpu.VMEM((2, rows, cols), F32),
            pltpu.VMEM((4, GROUP, cols), F32),
            pltpu.VMEM((2, 2 * GROUP, cols), F32),
            pltpu.VMEM((2, 2 * GROUP, cols), F32),
            pltpu.VMEM((3, rows, cols), F32),
            pltpu.VMEM((2, 2, rows, cols), F32),
            pltpu.VMEM((2, 4, GROUP, cols), F32),
            pltpu.VMEM((3, 2, WIDE * members, cols), F32),
            pltpu.VMEM((3, 2, WIDE * members, cols), F32),
            pltpu.VMEM((NX0, half_m, cols), F32),
            pltpu.VMEM((NX0, 4, half_m, cols), F32),
            pltpu.VMEM((half_m, cols), F32),
            pltpu.VMEM((4, half_m, cols), F32),
            pltpu.VMEM((NX0, 4, 2 * half_m, cols), F32),
            pltpu.VMEM((NX0, 4, 2 * half_m, cols), F32),
            pltpu.VMEM((NX0, 4, 2 * half_m, cols), F32),
            pltpu.VMEM((NX0, 4, 2 * half_m, cols), F32),
            pltpu.VMEM((NX0, 4, half_m, cols), F32),
            pltpu.VMEM((2, NA, cols), F32),
            pltpu.VMEM((2, NA, cols), F32),
            pltpu.VMEM((2, NA // 2, cols), F32),
            pltpu.VMEM((4, NA // 2, cols), F32),
            pltpu.VMEM((LEVELS - 1, 3, NA, cols), F32),
            pltpu.VMEM((NA, cols), F32),
            pltpu.VMEM((12, ext, cols), F32),
            pltpu.VMEM((half_m, cols), F32),
            pltpu.VMEM((2, GROUP, cols), F32),
            pltpu.VMEM((6, GROUP, cols), F32),
            pltpu.VMEM((LEVELS, half_m, cols), F32),
            pltpu.VMEM((mates, half_m, cols), F32),
            pltpu.VMEM((5 * cols, 2 * cols), BF16),
            pltpu.VMEM((LEVELS * cols, 2 * cols), BF16),
            pltpu.VMEM((LEVELS * cols, 2 * cols), BF16),
            pltpu.VMEM((LEVELS, cols, cols), BF16),
            pltpu.VMEM((rows, cols), F32),
            pltpu.VMEM((rows, cols), F32),
            pltpu.VMEM((rows, cols), jnp.int32),
            pltpu.VMEM((LEVELS, cols), jnp.int32),
            pltpu.SemaphoreType.DMA((slots,)),
            pltpu.SemaphoreType.DMA((slots,)),
            pltpu.SemaphoreType.DMA((6,)),
        ],
        compiler_params=pltpu.CompilerParams(collective_id=0, has_side_effects=True, vmem_limit_bytes=VMEM_LIMIT),
    )(*(pltpu.with_memory_space_constraint(a, pltpu.HBM) for a in (
        source, guess, conductivity, storage, aggregates, pair_maps.reshape(LEVELS, -1))))
    return result[0], result[1]


def solution(mesh):
    placed = (
        P(None, "row", "col"),
        P(None, "row", "col"),
        P("row", "col"),
        P("row", "col"),
        P("row", "col"),
        P(None, "row", "col", None),
    )
    return jax.shard_map(
        functools.partial(shards, mesh.shape["row"], mesh.shape["col"]),
        mesh=mesh,
        in_specs=placed,
        out_specs=(P(None, "row", "col"), P(None, "row", "col")),
        check_vma=False,
    )
```

```python
import functools

import jax
import jax.numpy as jnp
from jax import lax
from jax.experimental import pallas as pl
from jax.experimental.pallas import tpu as pltpu
from jax.sharding import PartitionSpec as P

NA = 64
SWEEPS = 3
LEVELS = 4
OMEGA_FINE = 0.8
OMEGA_COARSE = 0.6
F32 = jnp.float32
BF16 = jnp.bfloat16
MESH = pl.DeviceIdType.MESH
OPP = (1, 0, 3, 2, 7, 6, 5, 4, 9, 8, 11, 10)
WIDE = SWEEPS + 1
GROUP = 2 * WIDE
HOPS = 28
NEAR = HOPS + 32
MATS = NEAR + 4
VECS = MATS + 6
OUTS = VECS + 2 ** LEVELS - 1
SPLIT = 36
NX0 = 2
CORNERS = ((1, 3), (1, 2), (0, 3), (0, 2))
VMEM_LIMIT = 24 * 1024 * 1024
NN = (((1,), (0,)), ((), ()))
NT = (((1,), (1,)), ((), ()))


def dg(a, b, dims):
    return lax.dot_general(a, b, dims, preferred_element_type=F32)


def split2(x):
    hi = x.astype(BF16)
    return hi, (x - hi.astype(F32)).astype(BF16)


def split3(x):
    hi = x.astype(BF16)
    rest = x - hi.astype(F32)
    mid = rest.astype(BF16)
    return hi, mid, (rest - mid.astype(F32)).astype(BF16)


def stacked(x):
    hi = x.astype(BF16).astype(F32)
    return jnp.concatenate([hi, x - hi], axis=0).astype(BF16)


def times(x, weights):
    n, wide = x.shape[0], weights.shape[1] // 2
    full = dg(stacked(x), weights, NN)
    return full[0:n, 0:wide] + (full[n:, 0:wide] + full[0:n, wide:])


def times_t(x, weights):
    n = x.shape[0]
    both = stacked(x)
    full = dg(jnp.concatenate([both, both], axis=1), weights, NT)
    return full[0:n] + full[n:]


def dot_hot(x, hot, dims):
    n = x.shape[0]
    hi = x.astype(BF16).astype(F32)
    mid = (x - hi).astype(BF16).astype(F32)
    full = dg(jnp.concatenate([hi, mid, x - hi - mid], axis=0).astype(BF16), hot, dims)
    return full[0:n] + (full[n : 2 * n] + full[2 * n :])


def hot_dot(hot, x, dims):
    hi, mid, lo = split3(x)
    return dg(hot, hi, dims) + (dg(hot, mid, dims) + dg(hot, lo, dims))


def kernel(n_row, n_col, src_in, guess_in, cond_in, sto_in, agg_in, pm_in, result,
           u, se, left, mo, gmat, rlhs, xt, ksend, krecv, kcorn, krsend, krrecv, hsend, hrecv, hcorn, rowbuf,
           rsend, xsend, xrecv, nsend, nrecv, tsend, trecv, csend, crecv, srecv, msend, mrecv, hsum, hrest, held, solve, coef, early, osend, orecv, vsend, vrecv, wmat, fmat, gfin, qts,
           cond, sto, agg, pm, ssem, rsem, lsem):
    members, rows, cols = guess_in.shape
    half_m = members // 2
    ext = rows + GROUP
    row = lax.axis_index("row")
    col = lax.axis_index("col")
    has = [row > 0, row < n_row - 1, col > 0, col < n_col - 1]
    dev = [(row - 1, col), (row + 1, col), (row, col - 1), (row, col + 1)]
    for v in (0, 1):
        for h in (2, 3):
            has.append(jnp.logical_and(has[v], has[h]))
            dev.append((dev[v][0], dev[h][1]))
    far_has = [row > 1, row < n_row - 2, col > 1, col < n_col - 2]
    far_dev = [(row - 2, col), (row + 2, col), (row, col - 2), (row, col + 2)]
    has += far_has
    dev += far_dev
    col_bit = col % 2
    row_bit = row % 2
    col_bit2 = col // 2 % 2
    row_bit2 = row // 2 % 2
    upper = (col_bit, row_bit, col_bit2, row_bit2)
    flip_col = (0, 1 - 2 * col_bit, 2 - 4 * col_bit2, 3 - 2 * col_bit - 4 * col_bit2)
    flip_row = (0, 1 - 2 * row_bit, 2 - 4 * row_bit2, 3 - 2 * row_bit - 4 * row_bit2)

    def mate(j):
        return (row + flip_row[j // 2 % 2 + 2 * (j // 8)], col + flip_col[j % 2 + 2 * (j // 4 % 2)])

    loads = [
        pltpu.make_async_copy(source, target, lsem.at[i])
        for i, (source, target) in enumerate((
            (guess_in, u.at[:, pl.ds(0, rows)]), (src_in, se.at[:, pl.ds(0, rows)]),
            (cond_in, cond), (agg_in, agg), (sto_in, sto), (pm_in, pm)))
    ]
    for load in loads:
        load.start()

    barrier = pltpu.get_barrier_semaphore()
    count = jnp.int32(0)
    for d in range(8):
        count = count + has[d].astype(jnp.int32)

        @pl.when(has[d])
        def _():
            pl.semaphore_signal(barrier, inc=1, device_id=dev[d], device_id_type=MESH)

    def copy(source, target, slot, device):
        return pltpu.make_async_remote_copy(
            src_ref=source, dst_ref=target, send_sem=ssem.at[slot], recv_sem=rsem.at[slot],
            device_id=device, device_id_type=MESH)

    sent = []

    def start(d, source, target, slot):
        @pl.when(has[d])
        def _():
            copy(source, target, slot, dev[d]).start()

        sent.append((d, source, target, slot))

    def arrive(d, source, target, slot):
        @pl.when(has[OPP[d]])
        def _():
            copy(source, target, slot, dev[d]).wait_recv()

    for d in range(12):
        @pl.when(jnp.logical_not(has[OPP[d]]))
        def _():
            if d < 2:
                krrecv[d] = jnp.ones((2 * GROUP, cols), F32)
                for p in range(3):
                    rowbuf[p, d] = jnp.zeros((WIDE * members, cols), F32)
            elif d < 4:
                krecv[d - 2] = jnp.ones((rows, cols), F32)
                for p in range(2):
                    hrecv[p, d - 2] = jnp.zeros((rows, cols), F32)
            elif d < 8:
                kcorn[d - 4] = jnp.ones((GROUP, cols), F32)
                for p in range(2):
                    hcorn[p, d - 4] = jnp.zeros((GROUP, cols), F32)
            for e in range(NX0):
                if d < 4:
                    xrecv[e, d] = jnp.zeros((half_m, cols), F32)
                    trecv[e, d] = jnp.zeros((2 * half_m, cols), F32)
                elif d < 8:
                    crecv[e, d - 4] = jnp.zeros((2 * half_m, cols), F32)
                else:
                    srecv[e, d - 8] = jnp.zeros((half_m, cols), F32)
            if d < 4:
                nrecv[d] = jnp.zeros((half_m, cols), F32)

    lane = lax.broadcasted_iota(jnp.int32, (ext, cols), 1)
    sub = lax.broadcasted_iota(jnp.int32, (ext, cols), 0)
    l8 = lane % GROUP
    owner = lane // GROUP
    lane8 = lane[0:GROUP]
    sub8 = sub[0:GROUP]

    def mirror(x):
        where = lax.broadcasted_iota(jnp.int32, x.shape, 1)
        bit = 1
        while bit < GROUP:
            x = jnp.where(where // bit % 2 == 0, pltpu.roll(x, cols - bit, 1), pltpu.roll(x, bit, 1))
            bit *= 2
        return x

    def repeat(x):
        width = GROUP
        while width < cols:
            x = x + pltpu.roll(x, width, 1)
            width *= 2
        return x

    def side_ref(source, target, corners, d, slot):
        if d < 4:
            return d, source, target.at[d - 2], slot + d
        return d, source.at[pl.ds(0 if d < 6 else rows - GROUP, GROUP)], corners.at[d - 4], slot + d

    def row_ref(p, d):
        return d, rsend.at[p, d], rowbuf.at[p, d], 16 + 2 * p + d

    def field_ref(d):
        return side_ref(hsend.at[0 if d % 2 == 0 else 1], hrecv.at[0], hcorn.at[0], d, 8)

    def again_ref(d):
        if d < 2:
            return row_ref(2, d)
        return side_ref(hsend.at[2], hrecv.at[1], hcorn.at[1], d, 20)

    def coef_ref(d):
        if d < 2:
            return d, krsend.at[d], krrecv.at[d], d
        return side_ref(ksend, krecv, kcorn, d, 0)

    def pack_sides(fields):
        packed = jnp.zeros((rows, cols), F32)
        for m, v in enumerate(fields):
            packed = jnp.where(owner[0:rows] == m, pltpu.roll(v, (GROUP * m + WIDE) % cols, 1), packed)
        return mirror(packed)

    def pack_rows(p, field):
        for m in range(members):
            rsend[p, 0, WIDE * m : WIDE * (m + 1), :] = field[m, 0:WIDE]
            rsend[p, 1, WIDE * m : WIDE * (m + 1), :] = field[m, rows - WIDE : rows]

    order = (2, 3, 1, 0, 4, 5, 6, 7)

    def under(south, north):
        return jnp.where(sub8 < WIDE, south, north)

    def fill_rows(p, field):
        for m in range(members):
            field[m, rows : rows + WIDE, :] = rowbuf[p, 0, WIDE * m : WIDE * (m + 1), :]
            field[m, rows + WIDE : ext, :] = rowbuf[p, 1, WIDE * m : WIDE * (m + 1), :]

    def sides(planes, corners):
        return (jnp.concatenate([planes[0], under(corners[0], corners[2])], axis=0),
                jnp.concatenate([planes[1], under(corners[1], corners[3])], axis=0))

    for load in loads:
        load.wait()
    agg_v = agg[...]
    sub64 = lax.broadcasted_iota(jnp.int32, (NA, cols), 0)
    for r in range(rows):
        hot = jnp.where(sub64 == agg_v[r : r + 1], 1.0, 0.0).astype(BF16)
        mo[0:NA, r * cols : (r + 1) * cols] = hot
        mo[NA : 2 * NA, r * cols : (r + 1) * cols] = hot
    xt[...] = jnp.zeros(xt.shape, F32)
    iota128 = lax.broadcasted_iota(jnp.int32, (cols, cols), 0)
    lane128 = lax.broadcasted_iota(jnp.int32, (cols, cols), 1)
    for k in range(LEVELS):
        pmk = pm[k : k + 1, :]
        pmk = jnp.where(upper[k] == 1, pltpu.roll(pmk, NA, 1), pmk)
        qts[k] = jnp.where(jnp.logical_and(iota128 == pmk, lane128 < NA), 1.0, 0.0).astype(BF16)

    def face(a, b):
        return 2.0 * (a * b) / (a + b)

    last = rows - 1
    c = cond[...]
    in_east = jnp.where(lane[0:rows] < cols - 1, face(c, pltpu.roll(c, cols - 1, 1)), 0.0)
    in_south = jnp.where(sub[0:rows] < last, face(c, pltpu.roll(c, last, 0)), 0.0)
    right = pltpu.roll(agg_v, cols - 1, 1)
    below = pltpu.roll(agg_v, last, 0)
    half = 0.5 * (sto[...] + in_east + pltpu.roll(in_east, 1, 1) + in_south + pltpu.roll(in_south, 1, 0))
    for r in range(rows):
        s = slice(r, r + 1)
        g = (jnp.where(sub64 == right[s], in_east[s], 0.0)
             + jnp.where(sub64 == below[s], in_south[s], 0.0)
             - jnp.where(sub64 == agg_v[s], half[s], 0.0))
        for i, part in enumerate(split3(g)):
            gmat[i * NA : (i + 1) * NA, r * cols : (r + 1) * cols] = part
    gx = dg(gmat[...], mo[0:NA], NT)
    xt[0:NA, 0:NA] = gx[0:NA] + (gx[NA : 2 * NA] + gx[2 * NA : 3 * NA])
    xfull = xt[...]
    inner = -(xfull + xfull.T)[0:NA]

    lane_c = lax.broadcasted_iota(jnp.int32, (NA, cols), 1)
    lane_1 = lax.broadcasted_iota(jnp.int32, (1, cols), 1)
    eye = jnp.where(lane_c == sub64, 1.0, 0.0)

    def squeeze(mat, pair):
        right = dot_hot(mat[:, 0:NA], pair, NT)
        full = hot_dot(pair, right, NN)
        both = jnp.where(lane_c < NA, full[0:NA], full[NA : 2 * NA])
        half = jnp.where(lane_c[0 : NA // 2] < NA, pltpu.roll(both[0 : NA // 2], NA, 1), both[NA // 2 : NA])
        return both, half

    def lower(both):
        return jnp.where(lane_c < NA, both, 0.0)

    def higher(both, halves):
        halves = jnp.concatenate([halves, pltpu.roll(halves, NA, 1)], axis=0)
        return jnp.where(lane_c < NA, pltpu.roll(both, NA, 1) + halves, 0.0)

    hots = [qts[k][0:NA, 0:NA] for k in range(LEVELS)]

    def onward(a, b):
        return dg(a, b, NN).astype(BF16)

    pair_12 = jnp.concatenate([hots[0], onward(hots[1], hots[0])], axis=0)
    pair_34 = jnp.concatenate([hots[2], onward(hots[3], hots[2])], axis=0)
    pair_all = jnp.concatenate([pair_12, onward(pair_34, pair_12[NA : 2 * NA])], axis=0)
    msend[0], hsum[0] = squeeze(inner, pair_12)

    aggf = agg[...].astype(F32)
    ksend[...] = pack_sides([cond[...], sto[...], aggf])
    for d, near, wide in ((0, 0, 0), (1, rows - WIDE, rows - GROUP)):
        krsend[d, 0:WIDE] = cond[near : near + WIDE]
        krsend[d, WIDE:GROUP] = sto[near : near + WIDE]
        krsend[d, GROUP : 2 * GROUP] = aggf[wide : wide + GROUP]
    side_g = pack_sides([u[m, 0:rows] for m in range(members)])
    side_f = pack_sides([se[m, 0:rows] for m in range(members)])
    inward = l8[0:rows] < WIDE
    hsend[0] = jnp.where(inward, side_g, pltpu.roll(side_f, WIDE, 1))
    hsend[1] = jnp.where(inward, pltpu.roll(side_g, cols - WIDE, 1), side_f)
    pack_rows(0, u)
    pack_rows(1, se)
    pl.semaphore_wait(barrier, count)
    def mat_copy(i):
        at = i // 3
        mates = mate((1, 2, 3, 4, 8, 12)[i])
        if i % 3 == 0:
            return copy(msend.at[at], mrecv.at[at], MATS + i, mates)
        return copy(hsum.at[at], hrest.at[2 * at + i % 3 - 1], MATS + i, mates)

    for d in order:
        start(*coef_ref(d))
    for d in (2, 3):
        start(*field_ref(d))
    for p in range(2):
        for d in (1, 0):
            start(*row_ref(p, d))
    for d in range(4, 8):
        start(*field_ref(d))
    for i in range(3):
        mat_copy(i).start()

    for d in range(8):
        arrive(*coef_ref(d))

    k_east, k_west = sides(krecv, kcorn)
    k_side = jnp.where(l8 < WIDE, k_east, k_west)

    def extend(value, at):
        main = jnp.concatenate([value[...]] + [krrecv[d, at * WIDE : (at + 1) * WIDE] for d in range(2)], axis=0)
        return main, repeat(jnp.where(lane < GROUP, pltpu.roll(k_side, (cols - at * GROUP) % cols, 1), 0.0))

    cm, cs = extend(cond, 0)
    sm, ss = extend(sto, 1)
    hasi = [h.astype(jnp.int32) for h in has[0:4]]

    def vertical(x):
        down = jnp.where(jnp.logical_and(sub == last, hasi[1] == 0), 0.0, face(x, pltpu.roll(x, ext - 1, 0)))
        up = jnp.where(jnp.logical_and(sub == 0, hasi[0] == 0), 0.0, face(x, pltpu.roll(x, 1, 0)))
        return down, up

    side_at = pltpu.roll(cs, cols - WIDE, 1)
    rim = jnp.logical_and(lane >= WIDE - 1, lane <= WIDE)
    main_at = repeat(jnp.where(rim, pltpu.roll(cm, WIDE, 1), 0.0))
    east = face(cm, jnp.where(lane == cols - 1, side_at, pltpu.roll(cm, cols - 1, 1)))
    west = face(cm, jnp.where(lane == 0, side_at, pltpu.roll(cm, 1, 1)))
    east = jnp.where(lane < cols - 1 + hasi[3], east, 0.0)
    west = jnp.where(lane >= 1 - hasi[2], west, 0.0)
    south, north = vertical(cm)
    diag = sm + east + west + south + north
    step = OMEGA_FINE / diag
    s_west = face(cs, jnp.where(l8 == WIDE - 1, main_at, pltpu.roll(cs, cols - 1, 1)))
    s_east = face(cs, jnp.where(l8 == WIDE, main_at, pltpu.roll(cs, 1, 1)))
    s_west = jnp.where(jnp.logical_and(l8 == WIDE - 1, hasi[3] == 0), 0.0, s_west)
    s_east = jnp.where(jnp.logical_and(l8 == WIDE, hasi[2] == 0), 0.0, s_east)
    s_south, s_north = vertical(cs)
    s_diag = ss + s_east + s_west + s_south + s_north
    s_step = OMEGA_FINE / s_diag
    for i, value in enumerate((east, west, south, north, diag, step)):
        coef[i] = value
    for i, value in enumerate((s_east, s_west, s_south, s_north, s_diag, s_step)):
        coef[6 + i] = value

    def apply_field(side, n, finish):
        lane_n = lane[0:n]
        edge = jnp.zeros((ext, cols), F32)
        for m in range(members):
            v = u[m]
            hm = pltpu.roll(side, (2 * cols - GROUP * m - WIDE) % cols, 1)[0:n]
            vn = v[0:n]
            from_w = jnp.where(lane_n == 0, hm, pltpu.roll(vn, 1, 1))
            from_e = jnp.where(lane_n == cols - 1, hm, pltpu.roll(vn, cols - 1, 1))
            from_s = pltpu.roll(v, ext - 1, 0)[0:n]
            from_n = pltpu.roll(v, 1, 0)[0:n]
            rest = se[m, 0:n] - (coef[4, 0:n] * vn - (
                coef[0, 0:n] * from_e + coef[1, 0:n] * from_w + coef[2, 0:n] * from_s + coef[3, 0:n] * from_n))
            if n == ext:
                edge = jnp.where(owner == m, pltpu.roll(v, (GROUP * m + WIDE) % cols, 1), edge)
            finish(m, vn, rest)
        return edge

    def sweep(side, s_src):
        def finish(m, v, rest):
            u[m] = v + coef[5] * rest

        edge = apply_field(side, ext, finish)
        from_w = jnp.where(l8 == WIDE - 1, edge, pltpu.roll(side, cols - 1, 1))
        from_e = jnp.where(l8 == WIDE, edge, pltpu.roll(side, 1, 1))
        rest = s_src - (coef[10] * side - (coef[6] * from_e + coef[7] * from_w
                        + coef[8] * pltpu.roll(side, ext - 1, 0) + coef[9] * pltpu.roll(side, 1, 0)))
        return side + coef[11] * rest


    agg_t = agg_v.astype(F32).T.astype(jnp.int32)

    def put(ref, slot, block):
        both = jnp.concatenate([block, pltpu.roll(block, NA, 1)], axis=0)
        hi, lo = split2(both)
        ref[slot * cols : (slot + 1) * cols, 0:cols] = hi
        ref[slot * cols : (slot + 1) * cols, cols : 2 * cols] = lo

    joined = []

    def couple(slot, own_ids, other_ids, faces, width):
        own = jnp.where(lax.broadcasted_iota(jnp.int32, (cols, width), 0) == own_ids, 1.0, 0.0).astype(BF16)
        other = jnp.where(lax.broadcasted_iota(jnp.int32, (NA, width), 0) == other_ids, faces, 0.0)
        links = dot_hot(other, own, NT)
        joined.append((slot, -links))
        return jnp.sum(links, axis=0, keepdims=True)

    row_ids = [krrecv[d].astype(jnp.int32) for d in range(2)]
    outer = couple(1, agg_v[last:rows], row_ids[0][GROUP : GROUP + 1], south[last:rows], cols)
    outer = outer + couple(2, agg_v[0:1], row_ids[1][2 * GROUP - 1 : 2 * GROUP], north[0:1], cols)
    k_ids = k_side[0:rows].T.astype(jnp.int32)
    near_e = 2 * GROUP + WIDE - 1
    outer = outer + couple(3, agg_t[cols - 1 : cols], k_ids[near_e : near_e + 1], east[0:rows].T[cols - 1 : cols], rows)
    outer = outer + couple(4, agg_t[0:1], k_ids[near_e + 1 : near_e + 2], west[0:rows].T[0:1], rows)

    def vec_copy(j):
        return copy(vsend.at[j.bit_length() - 1], vrecv.at[j - 1], VECS + j - 1, mate(j))

    def out_copy(i):
        return copy(osend.at[i // 3], orecv.at[i], OUTS + i, mate((1, 2, 3, 4, 8, 12)[i]))

    def weight(mat):
        d = jnp.sum(jnp.where(lane_c == sub64, mat, 0.0), axis=0, keepdims=True)
        ok = lane_1 < NA
        return jnp.where(ok, OMEGA_COARSE / jnp.where(ok, d, 1.0), 0.0)

    def parted(b):
        hi = b.astype(BF16).astype(F32)
        return jnp.where(lane_c < NA, hi, pltpu.roll(b - hi, NA, 1)).astype(BF16)

    def product(a, b):
        full = dg(stacked(a[:, 0:NA]), b, NN)
        part = full[0:NA] + jnp.where(lane_c < NA, full[NA : 2 * NA], 0.0)
        return jnp.where(lane_c < NA, part + pltpu.roll(part, NA, 1), 0.0)

    def smoother(mat):
        side_w = OMEGA_COARSE / jnp.sum(eye * mat, axis=1, keepdims=True)
        one = eye - mat * weight(mat)
        parts = parted(one)
        two = product(one, parts)
        return product(two, parts), side_w * (eye + one + two)

    block = inner + jnp.where(lane_c == sub64, outer, 0.0)
    outers = dot_hot(jnp.broadcast_to(outer[:, 0:NA], (GROUP, NA)), pair_all, NT)
    outers = [outers[:, 0:cols], outers[:, cols : 2 * cols]]
    level = jnp.zeros((GROUP, cols), F32)
    for k in range(LEVELS):
        level = jnp.where(sub8 == k, pltpu.roll(outers[k // 2], NA, 1) if k % 2 else outers[k // 2], level)
    osend[0] = jnp.where(lane8 < NA, level, 0.0)
    for i in range(3):
        out_copy(i).start()
    weights = weight(block)
    weights = jnp.broadcast_to(weights + pltpu.roll(weights, NA, 1), (half_m, cols))
    nsend[...] = weights

    def near_ref(d):
        return d, nsend, nrecv.at[d], NEAR + d

    for d in (2, 3, 1, 0):
        start(*near_ref(d))
    put(wmat, 0, block)
    for slot, links in joined:
        put(wmat, slot, links)

    for d in range(2, 8):
        arrive(*field_ref(d))
    for p in range(2):
        for d in range(2):
            arrive(*row_ref(p, d))
    fill_rows(0, u)
    fill_rows(1, se)
    h_east, h_west = sides(hrecv[0], hcorn[0])
    side = jnp.where(l8 < WIDE, h_east, pltpu.roll(h_west, WIDE, 1))
    s_src = jnp.where(l8 < WIDE, pltpu.roll(h_east, cols - WIDE, 1), h_west)
    for _ in range(SWEEPS):
        side = sweep(side, s_src)

    def keep_left(m, v, rest):
        left[m] = rest

    apply_field(side, rows, keep_left)
    for r in range(rows):
        for i, part in enumerate(split2(left[:, r, :])):
            rlhs[i * members : (i + 1) * members, r * cols : (r + 1) * cols] = part
    gr = dg(rlhs[...], mo[...], NT)
    gr = gr[0:members] + gr[members : 2 * members]
    lane_h = lax.broadcasted_iota(jnp.int32, (half_m, cols), 1)

    def fold(x):
        return jnp.where(lane_h < NA, x[0:half_m], x[half_m:members])

    y0 = fold(gr)

    def x_slot(e, d):
        return (d, xsend.at[e], xrecv.at[e, d], HOPS + 16 * e + d)

    def level_one(e, x, sweep_it, between=None):
        xsend[e] = x
        for d in (2, 3, 1, 0):
            start(*x_slot(e, d))
        early[...] = x + (y0 - times(x, wmat[0:cols])) * weights if sweep_it else y0 - times(x, wmat[0:cols])
        if between is not None:
            between()
        for d in range(4):
            arrive(*x_slot(e, d))
        every = jnp.concatenate([xrecv[e, d] for d in range(4)], axis=1)
        near = times(every, wmat[cols : 5 * cols])
        return early[...] - (near * weights if sweep_it else near)

    def t_slot(e, d):
        slot = HOPS + 16 * e + 4 + d
        if d < 4:
            return d, tsend.at[e, OPP[d]], trecv.at[e, d], slot
        if d < 8:
            return d, csend.at[e, d - 4], crecv.at[e, d - 4], slot
        return d, tsend.at[e, OPP[d - 8], pl.ds(half_m, half_m)], srecv.at[e, d - 8], slot

    def two_sweeps(e, x, between=None):
        full = times_t(x, wmat[...])
        first = x + (y0 - full[:, 0:cols]) * weights
        out = [full[:, (n + 1) * cols : (n + 2) * cols] * nrecv[n] for n in range(4)]
        for n in range(4):
            tsend[e, n, 0:half_m] = first
            tsend[e, n, half_m : 2 * half_m] = out[n]
        for i, (v, h) in enumerate(CORNERS):
            csend[e, i, 0:half_m] = out[v]
            csend[e, i, half_m : 2 * half_m] = out[h]
        for d in (7, 6, 5, 4, 2, 3, 1, 0, 8, 9, 10, 11):
            start(*t_slot(e, d))
        if between is not None:
            between()
        for d in range(12):
            arrive(*t_slot(e, d))
        got = [trecv[e, d, half_m : 2 * half_m] for d in range(4)]
        tiles = [first - ((got[0] + got[1]) + (got[2] + got[3]))]
        for n in range(4):
            tiles.append(trecv[e, n, 0:half_m] - (out[n] + srecv[e, n]))
        for i, (v, h) in enumerate(CORNERS):
            tiles[1 + OPP[h]] = tiles[1 + OPP[h]] - crecv[e, i, 0:half_m]
            tiles[1 + OPP[v]] = tiles[1 + OPP[v]] - crecv[e, i, half_m : 2 * half_m]
        return tiles[0] + (y0 - times(jnp.concatenate(tiles, axis=1), wmat[...])) * weights

    for i in range(3):
        mat_copy(i).wait_recv()
    mat_1 = msend[0] + mrecv[0]
    mat_2 = higher(mat_1, hrest[0] + hrest[1])
    mat_1 = lower(mat_1)
    msend[1], hsum[1] = squeeze(mat_2, pair_34)
    for i in range(3, 6):
        mat_copy(i).start()
    for i in range(3):
        out_copy(i).wait_recv()
    outer_1 = osend[0] + orecv[0]
    osend[1] = outer_1 + jnp.where(sub8 > 0, orecv[1] + orecv[2], 0.0)
    for i in range(3, 6):
        out_copy(i).start()
    for d in range(4):
        arrive(*near_ref(d))
    def lift(k):
        onto = hot_dot(hots[k + 1], held[k, 0], NN)
        held[k, 1] = product(held[k, 1], parted(held[k, 2]))
        held[k, 0] = jnp.concatenate([onto, jnp.zeros((cols - NA, cols), F32)], axis=0).T[0:NA]

    def link(k, mat, chain):
        cube, pre = smoother(mat)
        moved = product(cube, parted(chain))
        held[k, 0] = cube
        held[k, 1] = pre
        held[k, 2] = chain + moved
        chain = hot_dot(hots[k + 1], moved, NN)
        put(fmat, k + 1, chain)
        return chain

    def early_chains():
        chain = hots[0].astype(F32)
        chain = jnp.concatenate([chain, jnp.zeros((NA, cols - NA), F32)], axis=1)
        put(fmat, 0, chain)
        chain = link(0, mat_1 + eye * outer_1[0:1], chain)
        solve[...] = link(1, mat_2 + eye * osend[1, 1:2], chain)
        for k in range(LEVELS - 2):
            lift(k)

    def late_chains():
        for i in range(3, 6):
            mat_copy(i).wait_recv()
        for i in range(3, 6):
            out_copy(i).wait_recv()
        sums = osend[1] + orecv[3]
        both = msend[1] + mrecv[1]
        chain = link(2, lower(both) + eye * sums[2:3], solve[...])
        sums = sums + (orecv[4] + orecv[5])
        mat = higher(both, hrest[2] + hrest[3]) + eye * sums[3:4]
        solve[...] = jnp.where(lane_c < NA, mat, pltpu.roll(chain, NA, 1))

    sub_g = lax.broadcasted_iota(jnp.int32, (GROUP, cols), 0)

    def lanes_of(v, k):
        return jnp.broadcast_to(v[:, k : k + 1], (GROUP, cols))

    def row_of(v, r):
        return jnp.broadcast_to(v[r : r + 1], (GROUP, cols))

    def pair_product(a, b):
        return [[a[i][0] * b[0][j] + a[i][1] * b[1][j] for j in range(2)] for i in range(2)]

    def pair_inverse(a):
        scale = 1.0 / (a[0][0] * a[1][1] - a[0][1] * a[1][0])
        return [[a[1][1] * scale, -a[0][1] * scale], [-a[1][0] * scale, a[0][0] * scale]]

    def quad_inverse(a):
        first = pair_inverse([a[i][0:2] for i in range(2)])
        right = pair_product(first, [a[i][2:4] for i in range(2)])
        below = [a[i][0:2] for i in range(2, 4)]
        moved = pair_product(below, right)
        second = pair_inverse([[a[2 + i][2 + j] - moved[i][j] for j in range(2)] for i in range(2)])
        down = pair_product(second, pair_product(below, first))
        back = pair_product(right, down)
        over = pair_product(right, second)
        return ([[first[i][j] + back[i][j] for j in range(2)] + [-over[i][j] for j in range(2)] for i in range(2)]
                + [[-down[i][j] for j in range(2)] + second[i] for i in range(2)])

    def eliminate(first, end):
        blocks = [solve[k : k + GROUP] for k in range(0, NA, GROUP)]
        for k in range(first, end, 4):
            q, r = k // GROUP, k % GROUP
            across = [[lanes_of(v, k + j) for v in blocks] for j in range(4)]
            inv = quad_inverse([[row_of(across[j][q], r + i) for j in range(4)] for i in range(4)])
            lines = [row_of(blocks[q], r + i) for i in range(4)]
            pivots = [(inv[i][0] * lines[0] + inv[i][1] * lines[1]) + (inv[i][2] * lines[2] + inv[i][3] * lines[3])
                      for i in range(4)]
            blocks = [v - ((across[0][i] * pivots[0] + across[1][i] * pivots[1])
                           + (across[2][i] * pivots[2] + across[3][i] * pivots[3])) for i, v in enumerate(blocks)]
            for i in range(4):
                blocks[q] = jnp.where(sub_g == r + i, pivots[i], blocks[q])
        for i, v in enumerate(blocks):
            solve[GROUP * i : GROUP * (i + 1)] = v

    x = two_sweeps(0, y0 * weights, early_chains)
    rem = level_one(0, x, False, lambda: (late_chains(), eliminate(0, SPLIT)))
    up = times_t(rem, fmat[...])
    for k in range(LEVELS):
        vsend[k] = up[:, k * cols : (k + 1) * cols]
    for j in reversed(range(1, 2 ** LEVELS)):
        vec_copy(j).start()
    lift(LEVELS - 2)
    eliminate(SPLIT, NA)
    final = jnp.where(lane_c < NA, pltpu.roll(solve[...], NA, 1), 0.0)
    put(gfin, LEVELS - 1, final)
    for k in reversed(range(LEVELS - 1)):
        final = held[k, 1] + product(held[k, 0], parted(final))
        put(gfin, k, final)
    for j in range(1, 2 ** LEVELS):
        vec_copy(j).wait_recv()
    ys = []
    for k in range(LEVELS):
        y = [vrecv[j - 1] for j in range(2 ** k, 2 ** (k + 1))]
        y = y + [vsend[0]] if k == 0 else y
        while len(y) > 1:
            y = [a + b for a, b in zip(y[::2], y[1::2])]
        ys.append(y[0])
    x = two_sweeps(1, x + times(jnp.concatenate(ys, axis=1), gfin[...]))
    x = level_one(1, x, True)

    whole = jnp.concatenate([x, pltpu.roll(x, NA, 1)], axis=0)
    whole_hi = whole.astype(BF16).astype(F32)
    lane_m = lax.broadcasted_iota(jnp.int32, (members, cols), 1)
    spread = jnp.where(lane_m < NA, whole_hi, pltpu.roll(whole - whole_hi, NA, 1)).astype(BF16)
    for q in range(0, rows, 4):
        part = dg(spread, mo[:, q * cols : (q + 4) * cols], NN)
        for r in range(q, q + 4):
            u[:, r, :] = u[:, r, :] + part[:, (r - q) * cols : (r - q + 1) * cols]
    hsend[2] = pack_sides([u[m, 0:rows] for m in range(members)])
    pack_rows(2, u)
    for d in order:
        start(*again_ref(d))
    for d in range(8):
        arrive(*again_ref(d))
    fill_rows(2, u)
    h_east, h_west = sides(hrecv[1], hcorn[1])
    side = jnp.where(l8 < WIDE, h_east, h_west)
    for _ in range(SWEEPS):
        side = sweep(side, s_src)

    def out(m, v, rest):
        result[0, m] = v
        result[1, m] = rest

    apply_field(side, rows, out)
    for d, source, target, slot in sent:
        @pl.when(has[d])
        def _():
            copy(source, target, slot, dev[d]).wait_send()

    for i in range(6):
        mat_copy(i).wait_send()
        out_copy(i).wait_send()
    for j in range(1, 2 ** LEVELS):
        vec_copy(j).wait_send()


def shards(n_row, n_col, source, guess, conductivity, storage, aggregates, pair_maps):
    members, rows, cols = source.shape
    cells = rows * cols
    ext = rows + GROUP
    vm = pl.BlockSpec(memory_space=pltpu.VMEM)
    half_m = members // 2
    mates = 2 ** LEVELS - 1
    slots = OUTS + 6
    hbm = pl.BlockSpec(memory_space=pltpu.HBM)
    result = pl.pallas_call(
        functools.partial(kernel, n_row, n_col),
        out_shape=jax.ShapeDtypeStruct((2,) + source.shape, F32),
        in_specs=[hbm] * 6,
        out_specs=vm,
        scratch_shapes=[
            pltpu.VMEM((members, ext, cols), F32),
            pltpu.VMEM((members, ext, cols), F32),
            pltpu.VMEM((members, rows, cols), F32),
            pltpu.VMEM((2 * NA, cells), BF16),
            pltpu.VMEM((3 * NA, cells), BF16),
            pltpu.VMEM((2 * members, cells), BF16),
            pltpu.VMEM((cols, cols), F32),
            pltpu.VMEM((rows, cols), F32),
            pltpu.VMEM((2, rows, cols), F32),
            pltpu.VMEM((4, GROUP, cols), F32),
            pltpu.VMEM((2, 2 * GROUP, cols), F32),
            pltpu.VMEM((2, 2 * GROUP, cols), F32),
            pltpu.VMEM((3, rows, cols), F32),
            pltpu.VMEM((2, 2, rows, cols), F32),
            pltpu.VMEM((2, 4, GROUP, cols), F32),
            pltpu.VMEM((3, 2, WIDE * members, cols), F32),
            pltpu.VMEM((3, 2, WIDE * members, cols), F32),
            pltpu.VMEM((NX0, half_m, cols), F32),
            pltpu.VMEM((NX0, 4, half_m, cols), F32),
            pltpu.VMEM((half_m, cols), F32),
            pltpu.VMEM((4, half_m, cols), F32),
            pltpu.VMEM((NX0, 4, 2 * half_m, cols), F32),
            pltpu.VMEM((NX0, 4, 2 * half_m, cols), F32),
            pltpu.VMEM((NX0, 4, 2 * half_m, cols), F32),
            pltpu.VMEM((NX0, 4, 2 * half_m, cols), F32),
            pltpu.VMEM((NX0, 4, half_m, cols), F32),
            pltpu.VMEM((2, NA, cols), F32),
            pltpu.VMEM((2, NA, cols), F32),
            pltpu.VMEM((2, NA // 2, cols), F32),
            pltpu.VMEM((4, NA // 2, cols), F32),
            pltpu.VMEM((LEVELS - 1, 3, NA, cols), F32),
            pltpu.VMEM((NA, cols), F32),
            pltpu.VMEM((12, ext, cols), F32),
            pltpu.VMEM((half_m, cols), F32),
            pltpu.VMEM((2, GROUP, cols), F32),
            pltpu.VMEM((6, GROUP, cols), F32),
            pltpu.VMEM((LEVELS, half_m, cols), F32),
            pltpu.VMEM((mates, half_m, cols), F32),
            pltpu.VMEM((5 * cols, 2 * cols), BF16),
            pltpu.VMEM((LEVELS * cols, 2 * cols), BF16),
            pltpu.VMEM((LEVELS * cols, 2 * cols), BF16),
            pltpu.VMEM((LEVELS, cols, cols), BF16),
            pltpu.VMEM((rows, cols), F32),
            pltpu.VMEM((rows, cols), F32),
            pltpu.VMEM((rows, cols), jnp.int32),
            pltpu.VMEM((LEVELS, cols), jnp.int32),
            pltpu.SemaphoreType.DMA((slots,)),
            pltpu.SemaphoreType.DMA((slots,)),
            pltpu.SemaphoreType.DMA((6,)),
        ],
        compiler_params=pltpu.CompilerParams(collective_id=0, has_side_effects=True, vmem_limit_bytes=VMEM_LIMIT),
    )(*(pltpu.with_memory_space_constraint(a, pltpu.HBM) for a in (
        source, guess, conductivity, storage, aggregates, pair_maps.reshape(LEVELS, -1))))
    return result[0], result[1]


def solution(mesh):
    placed = (
        P(None, "row", "col"),
        P(None, "row", "col"),
        P("row", "col"),
        P("row", "col"),
        P("row", "col"),
        P(None, "row", "col", None),
    )
    return jax.shard_map(
        functools.partial(shards, mesh.shape["row"], mesh.shape["col"]),
        mesh=mesh,
        in_specs=placed,
        out_specs=(P(None, "row", "col"), P(None, "row", "col")),
        check_vma=False,
    )
```
